32 devices in a mesh: groups: 2 (over y), ctx: 4 (over z), head: 4 (over x, core).
Axes of the slice: x: 2, y: 2, z: 4, core: 2. Of those that a mesh axis runs over, the one named last changes fastest.
Arguments:
- activations: bfloat16 [16384, 1024], P(('groups', 'ctx')), parts along dimension 0, may hold values from -40 to 40
- out_grad: bfloat16 [16384, 1024], P(('groups', 'ctx')), parts along dimension 0, may hold values from -5 to 5
- segment_ids: int32 [16384], P(('groups', 'ctx')), parts along dimension 0, may hold values from 0 to 7, never falling along the last dimension, each value on 1 to 2048 neighbouring positions
- qkv_weight: bfloat16 [1024, 3072], P(None, 'head'), may hold values from -0.25 to 0.25
- out_weight: bfloat16 [1024, 1024], P(None, 'head'), may hold values from -0.1875 to 0.1875
Outputs:
- input_grad: bfloat16 [16384, 1024], P(('groups', 'ctx'), 'head'), parts along dimension 0
- qkv_weight_grad: float32 [2048, 3072], P(('groups', 'ctx'), 'head'), parts along dimension 0
- out_weight_grad: float32 [2048, 1024], P(('groups', 'ctx'), 'head'), parts along dimension 0
The draws below stay inside these ranges and needn't reach their ends.
There are 2 independent parts, one for each index of `groups`. The reference program is written for one: setup_inputs(seed, part) draws one part's arguments, and reference() takes and returns one part's arrays. A program takes and returns all parts, laid end to end along the dimension named above; an argument that names none is the same for every part. Nothing has to cross between parts.
Inputs may be any that keep to these rules, and one draw needn't show every extreme that they name: `segment_ids`: segment numbers never fall along the sequence; each document holds 1 to 2048 tokens, one exactly 2048.
All inputs are finite; a program needn't handle non-finite values.
Results may differ from the reference program's by a relative error of at most 0.025.
The reference program's roundings to bfloat16 on the way (of `projected`, `queries`, `keys`, `head_grads`, `weights_low`, `attended`, `score_grad` and `qkv_grad`) count: a program that leaves them out, or rounds other values in their place, can miss the bound.
Values may be sent and summed in bfloat16 or wider, within the bound.
A program may use at most 128 MiB of HBM per device.

```python
import math
import jax
import jax.numpy as jnp
import numpy as np
from jax import lax

D = 1024
H = 16
HD = 64
WIN = 512
QBLK = 512
TOKENS = 8192
DOCS = 8
DOC_MOST = 2048
N_HEAD = 4


def draw_activations(key, part):
    base_key = jax.random.fold_in(key, 0)
    base = jax.random.truncated_normal(base_key, -6.0, 6.0, (TOKENS, D), jnp.float32)
    return base.astype(jnp.bfloat16)


def draw_qkv_weight(key, part):
    base_key = jax.random.fold_in(key, 0)
    limit = min(6.0, 0.25 * math.sqrt(D))
    base = jax.random.truncated_normal(base_key, -limit, limit, (D, H, 3, HD), jnp.float32) / math.sqrt(D)
    return base.reshape(D, H * 3 * HD).astype(jnp.bfloat16)


def with_spikes(array, rng, source, target, blocks, factor):
    owner, partner = [(jnp.arange(array.shape[dim]) // (array.shape[dim] // blocks)).reshape([-1 if axis == dim else 1 for axis in range(array.ndim)]) for dim in (source, target)]
    chosen = jax.random.permutation(rng, blocks)[partner]
    strong = (owner == chosen) | (owner == (partner + blocks // 2) % blocks)
    return jnp.where(strong, factor * array, array)


def block_levels(key, shape, shards, low, top_value):
    level, own = 1.0, jax.random.fold_in(key, 6)
    for axis_at, shards_of in shards:
        heights = jnp.exp(jax.random.uniform(jax.random.fold_in(own, axis_at), (shards_of,), jnp.float32, low / len(shards), top_value / len(shards)))
        level = level * jnp.repeat(heights, shape[axis_at] // shards_of).reshape([-1 if axis == axis_at else 1 for axis in range(len(shape))])
    return level


def length_profile(count, total, most, slope):
    portions = [(1 << 20) // math.isqrt(grade ** slope) + 1 for grade in range(2, count + 1)]
    rest, given = total - most - (count - 1), [1] * (count - 1)
    while rest > 0:
        movable = [i for i in range(count - 1) if given[i] < most]
        pool, left = sum([portions[i] for i in movable]), rest
        for i in movable:
            more = min(most - given[i], max(1, left * portions[i] // pool), rest)
            given[i] = given[i] + more
            rest = rest - more
    return np.array([most] + given)


def uneven_parts(own_key, count, total, bound, skew):
    if count == 2:
        one = jax.random.randint(own_key, (), max(1, total - bound), min(bound, total - 1) + 1)
        return jnp.stack([one, total - one])
    sizes = jnp.asarray(length_profile(count, total, bound, skew), jnp.int32)
    couples = (count - 1) // 2
    source_of, taker = sizes[1:1 + 2 * couples:2], sizes[2:2 + 2 * couples:2]
    room = jnp.minimum(source_of - 1, bound - taker)
    moved = jax.random.randint(jax.random.fold_in(own_key, 1), (couples,), 0, 1 << 20) % (room + 1)
    sizes = sizes.at[1:1 + 2 * couples:2].set(source_of - moved).at[2:2 + 2 * couples:2].set(taker + moved)
    return sizes[jax.random.permutation(jax.random.fold_in(own_key, 2), count)]


def noise(key, shape, scale, most, cuts=(), kind=jnp.bfloat16):
    entries = jax.random.normal(key, shape, jnp.float32) * scale
    if len(cuts) > 0:
        entries = block_levels(key, shape, cuts, -0.22, 0.18) * entries
    return jnp.clip(entries, min=-most, max=most).astype(kind)


def bell_draw_with(stream_key, dims, scale, reach, pieces, heavy, kind=jnp.bfloat16):
    drawn = scale * jax.random.normal(stream_key, dims, jnp.float32)
    if pieces:
        drawn = drawn * block_levels(stream_key, dims, pieces, -0.22, 0.18)
    return jnp.clip(with_spikes(drawn, jax.random.fold_in(stream_key, 3), *heavy), -reach, reach).astype(kind)


def setup_inputs(seed: int = 0, part: int = 0) -> dict:
    keys = jax.random.split(jax.random.key(seed), 6)
    own_keys = jax.random.split(jax.random.fold_in(keys[5], part), 6)
    activations = draw_activations(jax.random.fold_in(jax.random.fold_in(keys[5], part), 71), part)
    out_grad = bell_draw_with(own_keys[1], (TOKENS, D), 0.25, 5.0, ((0, 4),), (0, 1, 4, 2.0))
    segment_ids = jnp.searchsorted(jnp.cumsum(uneven_parts(own_keys[2], DOCS, TOKENS, DOC_MOST, 2)), jnp.arange(TOKENS), side="right").astype(jnp.int32)
    qkv_weight = draw_qkv_weight(jax.random.fold_in(keys[5], 71), part)
    out_weight = noise(keys[4], (D, H * HD), (H * HD) ** -0.5, 0.1875, ((1, 4),))
    return {"activations": activations, "out_grad": out_grad, "segment_ids": segment_ids, "qkv_weight": qkv_weight, "out_weight": out_weight}


def rope_tables(first, count, width):
    middle = width // 2
    position = (first + jnp.arange(count, dtype=jnp.int32)).astype(jnp.float32)
    exponent = jnp.arange(middle, dtype=jnp.int32).astype(jnp.float32) * (2.0 / width)
    inverse = jnp.power(jnp.float32(10000.0), -exponent)
    angles = position[:, None] * inverse[None, :]
    angles = jnp.concatenate([angles, angles], axis=1)
    return jnp.cos(angles), jnp.sin(angles)


def rotate(values, cosine_table, sine_table):
    middle = values.shape[-1] // 2
    turned = jnp.concatenate([-values[..., middle:], values[..., :middle]], axis=-1)
    return values * cosine_table[:, None, :] + turned * sine_table[:, None, :]


def unrotate(gradient, cosine_table, sine_table):
    middle = gradient.shape[-1] // 2
    scaled = gradient * sine_table[:, None, :]
    turned = jnp.concatenate([scaled[..., middle:], -scaled[..., :middle]], axis=-1)
    return gradient * cosine_table[:, None, :] + turned


def window_mask(row_position, column_position, row_segment, column_segment, seq_total):
    inside_rows = (row_position >= 0) & (row_position < seq_total)
    inside_columns = (column_position >= 0) & (column_position < seq_total)
    within = jnp.abs(row_position[:, None] - column_position[None, :]) <= WIN
    same_doc = row_segment[:, None] == column_segment[None, :]
    return within & inside_rows[:, None] & inside_columns[None, :] & same_doc


def band_tile(query_block, key_block, value_block, grad_block, allowed):
    factor = query_block.shape[-1] ** -0.5
    visible = allowed[None, :, :]
    scores = jnp.einsum("qhd,khd->hqk", query_block.astype(jnp.float32), key_block.astype(jnp.float32)) * factor
    scores = jnp.where(visible, scores, -1e30)
    highest = jnp.max(scores, axis=-1)
    summed = jnp.sum(jnp.where(visible, jnp.exp(scores - highest[..., None]), 0.0), axis=-1)
    log_total = highest + jnp.log(summed)
    weights = jnp.where(visible, jnp.exp(scores - log_total[..., None]), 0.0)
    weights_low = weights.astype(jnp.bfloat16)
    attended = jnp.einsum("hqk,khd->qhd", weights_low.astype(jnp.float32), value_block.astype(jnp.float32)).astype(jnp.bfloat16)
    row_delta = jnp.sum(grad_block.astype(jnp.float32) * attended.astype(jnp.float32), axis=-1)
    weight_grad = jnp.einsum("qhd,khd->hqk", grad_block.astype(jnp.float32), value_block.astype(jnp.float32))
    score_grad = (weights * (weight_grad - row_delta.T[:, :, None]) * factor).astype(jnp.bfloat16)
    query_grad = jnp.einsum("hqk,khd->qhd", score_grad.astype(jnp.float32), key_block.astype(jnp.float32))
    key_grad = jnp.einsum("hqk,qhd->khd", score_grad.astype(jnp.float32), query_block.astype(jnp.float32))
    value_grad = jnp.einsum("hqk,qhd->khd", weights_low.astype(jnp.float32), grad_block.astype(jnp.float32))
    return attended, query_grad, key_grad, value_grad


def reference(activations, out_grad, segment_ids, qkv_weight, out_weight):
    tokens = TOKENS
    projected = jnp.dot(activations, qkv_weight, preferred_element_type=jnp.float32).astype(jnp.bfloat16)
    projected = projected.reshape(tokens, H, 3, HD)
    cosine_table, sine_table = rope_tables(0, tokens, HD)
    queries = rotate(projected[:, :, 0].astype(jnp.float32), cosine_table, sine_table).astype(jnp.bfloat16)
    rotated_keys = rotate(projected[:, :, 1].astype(jnp.float32), cosine_table, sine_table).astype(jnp.bfloat16)
    values = projected[:, :, 2]
    head_grads = jnp.dot(out_grad, out_weight, preferred_element_type=jnp.float32).astype(jnp.bfloat16)
    head_grads = head_grads.reshape(tokens, H, HD)
    padding = ((WIN, WIN), (0, 0), (0, 0))
    wide_keys = jnp.pad(rotated_keys, padding)
    wide_values = jnp.pad(values, padding)
    wide_segments = jnp.pad(segment_ids, (WIN, WIN))
    wide_position = jnp.arange(tokens + 2 * WIN, dtype=jnp.int32) - WIN
    own_position = jnp.arange(tokens, dtype=jnp.int32)
    span = QBLK + 2 * WIN
    blocks = tokens // QBLK

    def step(carry, block_index):
        key_acc, value_acc = carry
        start = (block_index * QBLK).astype(jnp.int32)
        allowed = window_mask(lax.dynamic_slice_in_dim(own_position, start, QBLK, 0),
                              lax.dynamic_slice_in_dim(wide_position, start, span, 0),
                              lax.dynamic_slice_in_dim(segment_ids, start, QBLK, 0),
                              lax.dynamic_slice_in_dim(wide_segments, start, span, 0), tokens)
        attended, query_grad, key_grad, value_grad = band_tile(
            lax.dynamic_slice_in_dim(queries, start, QBLK, 0),
            lax.dynamic_slice_in_dim(wide_keys, start, span, 0),
            lax.dynamic_slice_in_dim(wide_values, start, span, 0),
            lax.dynamic_slice_in_dim(head_grads, start, QBLK, 0), allowed)
        key_acc = lax.dynamic_update_slice_in_dim(key_acc, lax.dynamic_slice_in_dim(key_acc, start, span, 0) + key_grad, start, 0)
        value_acc = lax.dynamic_update_slice_in_dim(value_acc, lax.dynamic_slice_in_dim(value_acc, start, span, 0) + value_grad, start, 0)
        return (key_acc, value_acc), (attended, query_grad)

    empty = jnp.zeros((tokens + 2 * WIN, H, HD), jnp.float32)
    (key_acc, value_acc), (attended_all, query_all) = lax.scan(step, (empty, empty), jnp.arange(blocks, dtype=jnp.int32))
    attended_all = attended_all.reshape(tokens, H * HD)
    query_all = query_all.reshape(tokens, H, HD)
    key_grads = key_acc[WIN:WIN + tokens]
    value_grads = value_acc[WIN:WIN + tokens]
    query_pre = unrotate(query_all, cosine_table, sine_table)
    key_pre = unrotate(key_grads, cosine_table, sine_table)
    qkv_grad = jnp.stack([query_pre, key_pre, value_grads], axis=2).reshape(tokens, H * 3 * HD).astype(jnp.bfloat16)
    qkv_weight_grad = jnp.dot(activations.T, qkv_grad, preferred_element_type=jnp.float32)
    out_weight_grad = jnp.dot(out_grad.T, attended_all, preferred_element_type=jnp.float32)
    group_width = (H // N_HEAD) * 3 * HD
    summed = jnp.zeros((tokens, D), jnp.float32)
    for group in range(N_HEAD):
        term = jnp.dot(qkv_grad[:, group * group_width:(group + 1) * group_width],
                       qkv_weight[:, group * group_width:(group + 1) * group_width].T,
                       preferred_element_type=jnp.float32)
        term = lax.optimization_barrier(term.astype(jnp.bfloat16)).astype(jnp.float32)
        summed = summed + term
    return summed.astype(jnp.bfloat16), qkv_weight_grad, out_weight_grad
```

```python
import functools

import jax
import jax.numpy as jnp
from jax import lax
from jax.experimental import pallas as pl
from jax.experimental.pallas import tpu as pltpu
from jax.sharding import PartitionSpec as P

HD = 64
HALF = HD // 2
WIN = 512
T = 256
RIM = WIN // T
SPAN = 2 * RIM + 1
CHUNK = 512
LOW = -1e30
OUTSIDE = 127
NT = (((1,), (1,)), ((), ()))
F32 = jnp.float32
BF16 = jnp.bfloat16
MESH = pl.DeviceIdType.MESH


def dot(a, b):
    return jnp.dot(a, b, preferred_element_type=F32)


def layer_kernel(nx, nz, acts, og, seg, w, ow, cos_ref, sin_ref,
                 in_out, qkv_out, ow_out,
                 wt, owt, kt, vt, kx, vx, qt, gt, pen, seg_low, seg_high, tri,
                 s_ref, p_ref, ds_ref, dk, dv, grad, att,
                 rim_send, rim_recv, part, recv, send1, recv1, recv2,
                 halo_ss, halo_rs, seg_ss, seg_rs, rim_ss, rim_rs,
                 right_ss, right_rs, left_ss, left_rs, swap_ss, swap_rs, cross_ss, cross_rs):
    tokens, model = acts.shape
    width = ow.shape[1]
    heads = width // HD
    pairs = heads // 2
    nb = tokens // T
    cols = model // (2 * nx)
    share = model // nz
    chunks = tokens // CHUNK
    head = lax.axis_index("head")
    z = lax.axis_index("ctx")
    x, core = head // 2, head % 2
    sibling = x * 2 + (1 - core)
    has_low, has_high = z > 0, z < nz - 1
    above = {"ctx": jnp.minimum(z + 1, nz - 1)}
    below = {"ctx": jnp.maximum(z - 1, 0)}

    barrier = pltpu.get_barrier_semaphore()
    pl.semaphore_signal(barrier, inc=1, device_id={"head": sibling}, device_id_type=MESH)
    for k in range(1, nx):
        peer = ((x + k) % nx) * 2 + core
        pl.semaphore_signal(barrier, inc=1, device_id={"head": peer}, device_id_type=MESH)
    for k in range(1, nz):
        pl.semaphore_signal(barrier, inc=1, device_id={"ctx": (z + k) % nz}, device_id_type=MESH)

    def remote(src, dst, ss, rs, device):
        return pltpu.make_async_remote_copy(src_ref=src, dst_ref=dst, send_sem=ss, recv_sem=rs,
                                            device_id=device, device_id_type=MESH)

    def halo_up(a, n):
        return remote(a.at[pl.ds(nb, RIM)], a.at[pl.ds(0, RIM)], halo_ss.at[0, n], halo_rs.at[0, n], above)

    def halo_down(a, n):
        return remote(a.at[pl.ds(RIM, RIM)], a.at[pl.ds(nb + RIM, RIM)], halo_ss.at[1, n], halo_rs.at[1, n], below)

    def seg_up():
        return remote(seg, seg_low, seg_ss.at[0], seg_rs.at[0], above)

    def seg_down():
        return remote(seg, seg_high, seg_ss.at[1], seg_rs.at[1], below)

    def rim_up(p):
        return remote(rim_send.at[p, 0], rim_recv.at[p, 0], rim_ss.at[p, 0], rim_rs.at[p, 0], above)

    def rim_down(p):
        return remote(rim_send.at[p, 1], rim_recv.at[p, 1], rim_ss.at[p, 1], rim_rs.at[p, 1], below)

    def right(p, d):
        return remote(part.at[p, d], recv.at[p, d + 1], right_ss.at[p, d], right_rs.at[p, d], above)

    def left(p, d):
        return remote(part.at[p, d], recv.at[p, d], left_ss.at[p, d], left_rs.at[p, d], below)

    def swap(k, r):
        return remote(send1.at[k, r], recv1.at[k, r], swap_ss.at[k, r], swap_rs.at[k, r], {"head": sibling})

    def cross(k, r):
        return remote(recv1.at[k, r], recv2.at[k, r], cross_ss.at[k, r], cross_rs.at[k, r],
                      {"head": ((x + k) % nx) * 2 + core})

    def rows(start, size, unit):
        return pl.ds(pl.multiple_of(start, unit), size)

    @pl.loop(0, model // T)
    def _(c):
        at = rows(c * T, T, T)
        wt[:, at] = w[at, :].T
        owt[:, at] = ow[at, :].T

    lane_doc = lax.broadcasted_iota(jnp.int32, (128, T), 0)

    def token_major(t, row):
        one = jnp.where(lane_doc == row, 1.0, 0.0).astype(BF16).T
        for p in range(pairs):
            kx[p, t, :, :2 * HD] = kt[t, p * 2 * HD:(p + 1) * 2 * HD, :].T
            kx[p, t, :, 2 * HD:] = one
            vx[p, t] = vt[t, p * 2 * HD:(p + 1) * 2 * HD, :].T

    def project(i):
        at = rows(i * T, T, T)
        projected = lax.dot_general(wt[...], acts[at, :], NT, preferred_element_type=F32).astype(BF16)
        gt[i] = lax.dot_general(owt[...], og[at, :], NT, preferred_element_type=F32).astype(BF16)
        cos, sin = cos_ref[i], sin_ref[i]

        def rope(u):
            u = u.astype(F32)
            low, high = u[:HALF], u[HALF:]
            return jnp.concatenate([low * cos - high * sin, high * cos + low * sin], axis=0).astype(BF16)

        for h in range(heads):
            to = slice(h * HD, (h + 1) * HD)
            base = h * 3 * HD
            qt[i, to, :] = rope(projected[base:base + HD]) * BF16(HD ** -0.5)
            kt[i + RIM, to, :] = rope(projected[base + HD:base + 2 * HD])
            vt[i + RIM, to, :] = projected[base + 2 * HD:base + 3 * HD]
        row = seg[pl.ds(i, 1), :]
        pen[i] = jnp.where(lane_doc == row, 0.0, LOW).astype(BF16)
        token_major(i + RIM, row)

    @pl.loop(0, nb)
    def _(j):
        project(jnp.where(j < RIM, j, jnp.where(j < 2 * RIM, nb - 2 * RIM + j, j - RIM)))

        @pl.when(j == 2 * RIM - 1)
        def _():
            pl.semaphore_wait(barrier, nx + nz - 1)

            @pl.when(has_high)
            def _():
                seg_up().start()
                halo_up(kt, 0).start()
                halo_up(vt, 1).start()

            @pl.when(has_low)
            def _():
                seg_down().start()
                halo_down(kt, 0).start()
                halo_down(vt, 1).start()

    r = lax.broadcasted_iota(jnp.int32, (T, T), 0)
    c = lax.broadcasted_iota(jnp.int32, (T, T), 1)
    tri[0] = jnp.where(r >= c, 0.0, LOW).astype(F32)
    tri[1] = jnp.where(r <= c, 0.0, LOW).astype(F32)

    @pl.loop(0, nb + 2 * RIM)
    def _(t):
        dk[t] = jnp.zeros_like(dk[t])
        dv[t] = jnp.zeros_like(dv[t])

    def fill(a, first):
        a[first:first + RIM] = jnp.zeros((RIM, width, T), BF16)

    @pl.when(z == 0)
    def _():
        fill(kt, 0)
        fill(vt, 0)
        seg_low[...] = jnp.full_like(seg_low, OUTSIDE)

    @pl.when(z == nz - 1)
    def _():
        fill(kt, nb + RIM)
        fill(vt, nb + RIM)
        seg_high[...] = jnp.full_like(seg_high, OUTSIDE)

    def halo_arrive():
        @pl.when(has_low)
        def _():
            seg_up().wait_recv()
            halo_up(kt, 0).wait_recv()
            halo_up(vt, 1).wait_recv()

        @pl.when(has_high)
        def _():
            seg_down().wait_recv()
            halo_down(kt, 0).wait_recv()
            halo_down(vt, 1).wait_recv()

        for t in range(RIM):
            token_major(t, seg_low[nb - RIM + t:nb - RIM + t + 1, :])
            token_major(nb + RIM + t, seg_high[t:t + 1, :])

    zero = jnp.zeros((HD, T), BF16)

    def place(h, block, rest):
        return jnp.concatenate(([block, zero] if h == 0 else [zero, block]) + rest, axis=0)

    def feature(p, h):
        return rows(p * 2 * HD + h * HD, HD, HD)

    def score(p, i, h):
        rhs = place(h, qt[i, feature(p, h), :], [pen[i]])
        top = None
        for t in range(SPAN):
            s = dot(kx[p, i + t], rhs)
            if t == 0:
                s = s + tri[0]
            if t == SPAN - 1:
                s = s + tri[1]
            s_ref[h, t] = s
            best = jnp.max(s.reshape(T // 8, 8, T), axis=0)
            top = best if top is None else jnp.maximum(top, best)
        return jnp.max(top, axis=0, keepdims=True)

    def soft(h, top):
        total = jnp.zeros((8, T), F32)
        for t in range(SPAN):
            e = jnp.exp(s_ref[h, t] - top)
            total = total + jnp.sum(e.reshape(T // 8, 8, T), axis=0)
            p_ref[h, t] = e.astype(BF16)
        return 1.0 / jnp.sum(total, axis=0, keepdims=True)

    def attend(p, i, h, scale):
        at = feature(p, h)
        out = jnp.zeros((HD, T), F32)
        for t in range(SPAN):
            out = out + dot(vt[i + t, at, :], p_ref[h, t])
        out = (out * scale).astype(BF16)
        att[at, rows(i * T, T, T)] = out
        return jnp.sum(out.astype(F32) * gt[i, at, :].astype(F32), axis=0, keepdims=True)

    def query_grad(p, i, h, delta, scale):
        at = feature(p, h)
        rhs = place(h, gt[i, at, :], [])
        out = jnp.zeros((HD, T), F32)
        for t in range(SPAN):
            ds = (p_ref[h, t].astype(F32) * (dot(vx[p, i + t], rhs) - delta)).astype(BF16)
            ds_ref[h, t] = ds
            out = out + dot(kt[i + t, at, :], ds)
        out = out * (scale * HD ** -0.5)
        grad[rows((2 * p + h) * 3 * HD, HD, HD), rows(i * T, T, T)] = unrope(out, i)

    def key_grad(p, i, h, scale):
        at = feature(p, h)
        g = (gt[i, at, :].astype(F32) * scale).astype(BF16)
        q = (qt[i, at, :].astype(F32) * scale).astype(BF16)
        for t in range(SPAN):
            dv[i + t, at, :] += lax.dot_general(g, p_ref[h, t], NT, preferred_element_type=F32)
            dk[i + t, at, :] += lax.dot_general(q, ds_ref[h, t], NT, preferred_element_type=F32)

    def unrope(u, i):
        cos, sin = cos_ref[i], sin_ref[i]
        low, high = u[:HALF], u[HALF:]
        return jnp.concatenate([low * cos + high * sin, high * cos - low * sin], axis=0).astype(BF16)

    def rim_out(p, side, first):
        at = rows(p * 2 * HD, 2 * HD, 2 * HD)
        for t in range(RIM):
            rim_send[p, side, 0, t] = dk[first + t, at, :].astype(BF16)
            rim_send[p, side, 1, t] = dv[first + t, at, :].astype(BF16)

    def rim_in(p, side, first):
        at = rows(p * 2 * HD, 2 * HD, 2 * HD)
        for t in range(RIM):
            dk[first + t, at, :] += rim_recv[p, side, 0, t].astype(F32)
            dv[first + t, at, :] += rim_recv[p, side, 1, t].astype(F32)

    def finish(p):
        @pl.when(has_low)
        def _():
            rim_up(p).wait_recv()
            rim_in(p, 0, RIM)

        @pl.when(has_high)
        def _():
            rim_down(p).wait_recv()
            rim_in(p, 1, nb)

        @pl.loop(0, nb)
        def _(i):
            to = rows(i * T, T, T)
            for h in range(2):
                base = (2 * p + h) * 3 * HD
                grad[rows(base + HD, HD, HD), to] = unrope(dk[i + RIM, feature(p, h), :], i)
                grad[rows(base + 2 * HD, HD, HD), to] = dv[i + RIM, feature(p, h), :].astype(BF16)

    def weight_grads(p):
        order = []
        for n in range(nz):
            order.append(nz - 1 - n // 2 if n % 2 == 0 else n // 2)
        for d in order:
            to = slice(d * share, (d + 1) * share)
            part[p, d, :6 * HD, :] = dot(grad[rows(p * 6 * HD, 6 * HD, 2 * HD), :], acts[:, to]).astype(BF16)
            part[p, d, 6 * HD:, :] = dot(att[rows(p * 2 * HD, 2 * HD, 2 * HD), :], og[:, to]).astype(BF16)
            if d > 0:
                @pl.when(z == 0)
                def _():
                    right(p, d).start()
            if d < nz - 1:
                @pl.when(z == nz - 1)
                def _():
                    left(p, d).start()

    def hop(p, n):
        up = z + nz - 1 - n
        down = n - (nz - 1 - z)

        @pl.when(has_low & (up < nz))
        def _():
            right(p, up).wait_recv()
            part[p, up] = (part[p, up].astype(F32) + recv[p, up + 1].astype(F32)).astype(BF16)
            right(p, up).start()

        @pl.when(has_high & (down >= 0))
        def _():
            left(p, down).wait_recv()
            part[p, down] = (part[p, down].astype(F32) + recv[p, down].astype(F32)).astype(BF16)
            left(p, down).start()

    def land(p):
        def put(value):
            qkv_out[:, rows(p * 6 * HD, 6 * HD, 2 * HD)] = value[:6 * HD].T
            ow_out[:, rows(p * 2 * HD, 2 * HD, 2 * HD)] = value[6 * HD:].T

        @pl.when(z == 0)
        def _():
            left(p, z).wait_recv()
            put(part[p, z].astype(F32) + recv[p, z].astype(F32))

        @pl.when(z == nz - 1)
        def _():
            right(p, z).wait_recv()
            put(part[p, z].astype(F32) + recv[p, z + 1].astype(F32))

        @pl.when(has_low & has_high)
        def _():
            right(p, z).wait_recv()
            left(p, z).wait_recv()
            put(part[p, z].astype(F32) + recv[p, z].astype(F32) + recv[p, z + 1].astype(F32))

    @pl.loop(0, pairs * nb)
    def _(n):
        p, j = n // nb, n % nb
        i = jnp.where(j < 2, j + 2, jnp.where(j < 4, j - 2, jnp.where(j < 6, nb - 6 + j, j - 2)))

        @pl.when(n == 2)
        def _():
            halo_arrive()

        top0 = score(p, i, 0)
        top1 = score(p, i, 1)
        scale0 = soft(0, top0)
        delta0 = attend(p, i, 0, scale0)
        scale1 = soft(1, top1)
        query_grad(p, i, 0, delta0, scale0)
        delta1 = attend(p, i, 1, scale1)
        key_grad(p, i, 0, scale0)
        query_grad(p, i, 1, delta1, scale1)
        key_grad(p, i, 1, scale1)

        @pl.when((j == 3) & has_low)
        def _():
            rim_out(p, 1, 0)
            rim_down(p).start()

        @pl.when((j == 5) & has_high)
        def _():
            rim_out(p, 0, nb + RIM)
            rim_up(p).start()

        if pairs > 1:
            for m in range(1, nz):
                @pl.when((p > 0) & (j == 2 * m))
                def _():
                    if m < nz - 1:
                        hop(p - 1, m)
                    else:
                        land(p - 1)

        @pl.when(j == nb - 1)
        def _():
            finish(p)
            weight_grads(p)

    def term(block, r):
        at = rows(block * cols, cols, cols)
        return dot(w[at, :], grad[:, r * CHUNK:(r + 1) * CHUNK]).astype(BF16)

    last = pairs - 1
    for k in list(range(1, nx)) + [0]:
        for r in range(chunks):
            send1[k, r] = term(((x + k) % nx) * 2 + (1 - core), r)
            swap(k, r).start()
    for k in range(1, nx):
        for r in range(chunks):
            own = term(((x + k) % nx) * 2 + core, r).astype(F32)
            swap(k, r).wait_recv()
            recv1[k, r] = (own + recv1[k, r].astype(F32)).astype(BF16)
            cross(k, r).start()
    for m in range(1, nz - 1):
        hop(last, m)
    for r in range(chunks):
        value = term(x * 2 + core, r).astype(F32)
        swap(0, r).wait_recv()
        value = value + recv1[0, r].astype(F32)
        for k in range(1, nx):
            cross(k, r).wait_recv()
            value = value + recv2[k, r].astype(F32)
        in_out[r * CHUNK:(r + 1) * CHUNK, :] = value.astype(BF16).T
    land(last)

    @pl.when(has_high)
    def _():
        seg_up().wait_send()
        halo_up(kt, 0).wait_send()
        halo_up(vt, 1).wait_send()
        for p in range(pairs):
            rim_up(p).wait_send()

    @pl.when(has_low)
    def _():
        seg_down().wait_send()
        halo_down(kt, 0).wait_send()
        halo_down(vt, 1).wait_send()
        for p in range(pairs):
            rim_down(p).wait_send()

    for p in range(pairs):
        for d in range(nz):
            if d > 0:
                @pl.when(z < d)
                def _():
                    right(p, d).wait_send()
            if d < nz - 1:
                @pl.when(z > d)
                def _():
                    left(p, d).wait_send()
    for k in range(nx):
        for r in range(chunks):
            swap(k, r).wait_send()
            if k > 0:
                cross(k, r).wait_send()


def local(activations, out_grad, segment_ids, qkv_weight, out_weight):
    tokens, model = activations.shape
    columns = qkv_weight.shape[1]
    width = columns // 3
    pairs = width // (2 * HD)
    nb = tokens // T
    nt = nb + 2 * RIM
    nz = lax.axis_size("ctx")
    nx = lax.axis_size("head") // 2
    cols = model // (2 * nx)
    share = model // nz
    chunks = tokens // CHUNK
    me = lax.axis_index("ctx")
    position = (me * tokens + jnp.arange(tokens, dtype=jnp.int32)).astype(F32)
    exponent = jnp.arange(HALF, dtype=jnp.int32).astype(F32) * (2.0 / HD)
    inverse = jnp.power(F32(10000.0), -exponent)
    angles = inverse[None, :, None] * position.reshape(nb, 1, T)
    cos, sin = jnp.cos(angles), jnp.sin(angles)
    vmem = pl.BlockSpec(memory_space=pltpu.VMEM)
    dma = pltpu.SemaphoreType.DMA
    v = pltpu.VMEM
    return pl.pallas_call(
        functools.partial(layer_kernel, nx, nz),
        in_specs=[vmem] * 7,
        out_specs=[vmem] * 3,
        out_shape=[
            jax.ShapeDtypeStruct((tokens, cols), BF16),
            jax.ShapeDtypeStruct((share, columns), F32),
            jax.ShapeDtypeStruct((share, width), F32),
        ],
        scratch_shapes=[
            v((columns, model), BF16), v((width, model), BF16),
            v((nt, width, T), BF16), v((nt, width, T), BF16),
            v((pairs, nt, T, 2 * HD + 128), BF16), v((pairs, nt, T, 2 * HD), BF16),
            v((nb, width, T), BF16), v((nb, width, T), BF16),
            v((nb, 128, T), BF16), v((nb, T), jnp.int32), v((nb, T), jnp.int32), v((2, T, T), F32),
            v((2, SPAN, T, T), F32), v((2, SPAN, T, T), BF16), v((2, SPAN, T, T), BF16),
            v((nt, width, T), F32), v((nt, width, T), F32),
            v((columns, tokens), BF16), v((width, tokens), BF16),
            v((pairs, 2, 2, RIM, 2 * HD, T), BF16), v((pairs, 2, 2, RIM, 2 * HD, T), BF16),
            v((pairs, nz, 8 * HD, share), BF16), v((pairs, nz + 1, 8 * HD, share), BF16),
            v((nx, chunks, cols, CHUNK), BF16), v((nx, chunks, cols, CHUNK), BF16),
            v((nx, chunks, cols, CHUNK), BF16),
            dma((2, 2)), dma((2, 2)), dma((2,)), dma((2,)), dma((pairs, 2)), dma((pairs, 2)),
            dma((pairs, nz)), dma((pairs, nz)), dma((pairs, nz)), dma((pairs, nz)),
            dma((nx, chunks)), dma((nx, chunks)), dma((nx, chunks)), dma((nx, chunks)),
        ],
        compiler_params=pltpu.CompilerParams(
            collective_id=0, has_side_effects=True, vmem_limit_bytes=60 * 1024 * 1024
        ),
        cost_estimate=pl.CostEstimate(
            flops=12 * tokens * SPAN * T * width + 16 * tokens * model * width,
            bytes_accessed=8 * tokens * model, transcendentals=tokens * SPAN * T * width // HD
        ),
    )(activations, out_grad, segment_ids.reshape(nb, T), qkv_weight, out_weight, cos, sin)


def solution(mesh):
    in_specs = (
        P(("groups", "ctx"), None),
        P(("groups", "ctx"), None),
        P(("groups", "ctx")),
        P(None, "head"),
        P(None, "head"),
    )
    out_specs = (
        P(("groups", "ctx"), "head"),
        P(("groups", "ctx"), "head"),
        P(("groups", "ctx"), "head"),
    )
    return jax.shard_map(local, mesh=mesh, in_specs=in_specs, out_specs=out_specs, check_vma=False)
```

```python
import functools
import itertools

import jax
import jax.numpy as jnp
from jax import lax
from jax.experimental import pallas as pl
from jax.experimental.pallas import tpu as pltpu
from jax.sharding import PartitionSpec as P

HD = 64
HALF = HD // 2
WIN = 512
T = 256
RIM = WIN // T
SPAN = 2 * RIM + 1
LOW = -1e30
OUTSIDE = 127
NT = (((1,), (1,)), ((), ()))
F32 = jnp.float32
BF16 = jnp.bfloat16
MESH = pl.DeviceIdType.MESH


def dot(a, b):
    return jnp.dot(a, b, preferred_element_type=F32)


def layer_kernel(nx, nz, acts, og, seg, w, ow, cos_ref, sin_ref,
                 in_out, qkv_out, ow_out,
                 wt, owt, kt, vt, kx, vx, qt, gt, pen, seg_low, seg_high, tri,
                 s_ref, p_ref, ds_ref, dk, dv, grad, att,
                 rim_send, rim_recv, part, recv, sums, send1, own, recv1, recv2,
                 halo_ss, halo_rs, seg_ss, seg_rs, rim_ss, rim_rs,
                 right_ss, right_rs, left_ss, left_rs, swap_ss, swap_rs, cross_ss, cross_rs):
    tokens, model = acts.shape
    width = ow.shape[1]
    heads = width // HD
    pairs = heads // 2
    nb = tokens // T
    cols = model // (2 * nx)
    share = model // nz
    head = lax.axis_index("head")
    z = lax.axis_index("ctx")
    x, core = head // 2, head % 2
    sibling = x * 2 + (1 - core)
    has_low, has_high = z > 0, z < nz - 1
    above = {"ctx": jnp.minimum(z + 1, nz - 1)}
    below = {"ctx": jnp.maximum(z - 1, 0)}

    barrier = pltpu.get_barrier_semaphore()
    pl.semaphore_signal(barrier, inc=1, device_id={"head": sibling}, device_id_type=MESH)
    for k in range(1, nx):
        peer = ((x + k) % nx) * 2 + core
        pl.semaphore_signal(barrier, inc=1, device_id={"head": peer}, device_id_type=MESH)
    for k in range(1, nz):
        pl.semaphore_signal(barrier, inc=1, device_id={"ctx": (z + k) % nz}, device_id_type=MESH)

    def remote(src, dst, ss, rs, device):
        return pltpu.make_async_remote_copy(src_ref=src, dst_ref=dst, send_sem=ss, recv_sem=rs,
                                            device_id=device, device_id_type=MESH)

    def halo_up(a, n):
        return remote(a.at[pl.ds(nb, RIM)], a.at[pl.ds(0, RIM)], halo_ss.at[0, n], halo_rs.at[0, n], above)

    def halo_down(a, n):
        return remote(a.at[pl.ds(RIM, RIM)], a.at[pl.ds(nb + RIM, RIM)], halo_ss.at[1, n], halo_rs.at[1, n], below)

    def seg_up():
        return remote(seg, seg_low, seg_ss.at[0], seg_rs.at[0], above)

    def seg_down():
        return remote(seg, seg_high, seg_ss.at[1], seg_rs.at[1], below)

    def rim_up(p):
        return remote(rim_send.at[p, 0], rim_recv.at[p, 0], rim_ss.at[p, 0], rim_rs.at[p, 0], above)

    def rim_down(p):
        return remote(rim_send.at[p, 1], rim_recv.at[p, 1], rim_ss.at[p, 1], rim_rs.at[p, 1], below)

    def right(c, d):
        return remote(part.at[c, d], recv.at[c, d + 1], right_ss.at[c, d], right_rs.at[c, d], above)

    def left(c, d):
        return remote(part.at[c, d], recv.at[c, d], left_ss.at[c, d], left_rs.at[c, d], below)

    def swap(k, r):
        return remote(send1.at[k, r], recv1.at[k, r], swap_ss.at[k, r], swap_rs.at[k, r], {"head": sibling})

    def cross(k, r):
        return remote(recv1.at[k, r], recv2.at[k, r], cross_ss.at[k, r], cross_rs.at[k, r],
                      {"head": ((x + k) % nx) * 2 + core})

    def rows(start, size, unit):
        return pl.ds(pl.multiple_of(start, unit), size)

    @pl.loop(0, model // T)
    def _(c):
        at = rows(c * T, T, T)
        wt[:, at] = w[at, :].T
        owt[:, at] = ow[at, :].T

    lane_doc = lax.broadcasted_iota(jnp.int32, (128, T), 0)

    def token_major(t, row):
        one = jnp.where(lane_doc == row, 1.0, 0.0).astype(BF16).T
        for p in range(pairs):
            kx[p, t, :, :2 * HD] = kt[t, p * 2 * HD:(p + 1) * 2 * HD, :].T
            kx[p, t, :, 2 * HD:] = one
            vx[p, t] = vt[t, p * 2 * HD:(p + 1) * 2 * HD, :].T

    def project(i):
        at = rows(i * T, T, T)
        projected = lax.dot_general(wt[...], acts[at, :], NT, preferred_element_type=F32).astype(BF16)
        gt[i] = lax.dot_general(owt[...], og[at, :], NT, preferred_element_type=F32).astype(BF16)
        cos, sin = cos_ref[i], sin_ref[i]

        def rope(u):
            u = u.astype(F32)
            low, high = u[:HALF], u[HALF:]
            return jnp.concatenate([low * cos - high * sin, high * cos + low * sin], axis=0).astype(BF16)

        for h in range(heads):
            to = slice(h * HD, (h + 1) * HD)
            base = h * 3 * HD
            qt[i, to, :] = rope(projected[base:base + HD]) * BF16(HD ** -0.5)
            kt[i + RIM, to, :] = rope(projected[base + HD:base + 2 * HD])
            vt[i + RIM, to, :] = projected[base + 2 * HD:base + 3 * HD]
        row = seg[pl.ds(i, 1), :]
        pen[i] = jnp.where(lane_doc == row, 0.0, LOW).astype(BF16)
        token_major(i + RIM, row)

    @pl.loop(0, nb)
    def _(j):
        project(jnp.where(j < RIM, j, jnp.where(j < 2 * RIM, nb - 2 * RIM + j, j - RIM)))

        @pl.when(j == 2 * RIM - 1)
        def _():
            pl.semaphore_wait(barrier, nx + nz - 1)

            @pl.when(has_high)
            def _():
                seg_up().start()
                halo_up(kt, 0).start()
                halo_up(vt, 1).start()

            @pl.when(has_low)
            def _():
                seg_down().start()
                halo_down(kt, 0).start()
                halo_down(vt, 1).start()

    r = lax.broadcasted_iota(jnp.int32, (T, T), 0)
    c = lax.broadcasted_iota(jnp.int32, (T, T), 1)
    tri[0] = jnp.where(r >= c, 0.0, LOW).astype(F32)
    tri[1] = jnp.where(r <= c, 0.0, LOW).astype(F32)

    @pl.loop(0, nb + 2 * RIM)
    def _(t):
        dk[t] = jnp.zeros_like(dk[t])
        dv[t] = jnp.zeros_like(dv[t])

    def fill(a, first):
        a[first:first + RIM] = jnp.zeros((RIM, width, T), BF16)

    @pl.when(z == 0)
    def _():
        fill(kt, 0)
        fill(vt, 0)
        seg_low[...] = jnp.full_like(seg_low, OUTSIDE)

    @pl.when(z == nz - 1)
    def _():
        fill(kt, nb + RIM)
        fill(vt, nb + RIM)
        seg_high[...] = jnp.full_like(seg_high, OUTSIDE)

    def halo_arrive():
        @pl.when(has_low)
        def _():
            seg_up().wait_recv()
            halo_up(kt, 0).wait_recv()
            halo_up(vt, 1).wait_recv()

        @pl.when(has_high)
        def _():
            seg_down().wait_recv()
            halo_down(kt, 0).wait_recv()
            halo_down(vt, 1).wait_recv()

        for t in range(RIM):
            token_major(t, seg_low[nb - RIM + t:nb - RIM + t + 1, :])
            token_major(nb + RIM + t, seg_high[t:t + 1, :])

    zero = jnp.zeros((HD, T), BF16)

    def place(h, block, rest):
        return jnp.concatenate(([block, zero] if h == 0 else [zero, block]) + rest, axis=0)

    def feature(p, h):
        return rows(p * 2 * HD + h * HD, HD, HD)

    def block(p, i):
        top, scale, delta = [None] * 2, [None] * 2, [None] * 2
        ats = [feature(p, h) for h in range(2)]

        def score(h):
            rhs = place(h, qt[i, ats[h], :], [pen[i]])
            high = None
            for t in range(SPAN):
                s = dot(kx[p, i + t], rhs)
                if t == 0:
                    s = s + tri[0]
                if t == SPAN - 1:
                    s = s + tri[1]
                s_ref[h, t] = s
                best = jnp.max(s.reshape(T // 8, 8, T), axis=0)
                high = best if high is None else jnp.maximum(high, best)
                yield
            top[h] = jnp.max(high, axis=0, keepdims=True)

        def soft(h):
            total = jnp.zeros((8, T), F32)
            for t in range(SPAN):
                e = jnp.exp(s_ref[h, t] - top[h])
                total = total + jnp.sum(e.reshape(T // 8, 8, T), axis=0)
                p_ref[h, t] = e.astype(BF16)
                yield
            scale[h] = 1.0 / jnp.sum(total, axis=0, keepdims=True)

        def attend(h):
            out = jnp.zeros((HD, T), F32)
            for t in range(SPAN):
                out = out + dot(vt[i + t, ats[h], :], p_ref[h, t])
                yield
            out = (out * scale[h]).astype(BF16)
            att[ats[h], rows(i * T, T, T)] = out
            delta[h] = jnp.sum(out.astype(F32) * gt[i, ats[h], :].astype(F32), axis=0, keepdims=True)

        def score_grad(h):
            rhs = place(h, gt[i, ats[h], :], [])
            for t in range(SPAN):
                back = dot(vx[p, i + t], rhs)
                ds_ref[h, t] = (p_ref[h, t].astype(F32) * (back - delta[h])).astype(BF16)
                yield

        def query_grad(h):
            out = jnp.zeros((HD, T), F32)
            for t in range(SPAN):
                out = out + dot(kt[i + t, ats[h], :], ds_ref[h, t])
                yield
            out = out * (scale[h] * HD ** -0.5)
            grad[rows((2 * p + h) * 3 * HD, HD, HD), rows(i * T, T, T)] = unrope(out, i)

        def value_grad(h):
            g = (gt[i, ats[h], :].astype(F32) * scale[h]).astype(BF16)
            for t in range(SPAN):
                dv[i + t, ats[h], :] += lax.dot_general(g, p_ref[h, t], NT, preferred_element_type=F32)
                yield

        def key_grad(h):
            q = (qt[i, ats[h], :].astype(F32) * scale[h]).astype(BF16)
            for t in range(SPAN):
                dk[i + t, ats[h], :] += lax.dot_general(q, ds_ref[h, t], NT, preferred_element_type=F32)
                yield

        def run(*stages):
            for _ in itertools.zip_longest(*stages):
                pass

        run(score(0))
        run(score(1))
        run(soft(0))
        run(attend(0))
        run(soft(1), value_grad(0))
        run(attend(1))
        run(score_grad(0), value_grad(1))
        run(score_grad(1))
        run(query_grad(0))
        run(key_grad(0))
        run(query_grad(1))
        run(key_grad(1))

    def unrope(u, i):
        cos, sin = cos_ref[i], sin_ref[i]
        low, high = u[:HALF], u[HALF:]
        return jnp.concatenate([low * cos + high * sin, high * cos - low * sin], axis=0).astype(BF16)

    def rim_out(p, side, first):
        at = rows(p * 2 * HD, 2 * HD, 2 * HD)
        for t in range(RIM):
            rim_send[p, side, 0, t] = dk[first + t, at, :].astype(BF16)
            rim_send[p, side, 1, t] = dv[first + t, at, :].astype(BF16)

    def rim_in(p, side, first):
        at = rows(p * 2 * HD, 2 * HD, 2 * HD)
        for t in range(RIM):
            dk[first + t, at, :] += rim_recv[p, side, 0, t].astype(F32)
            dv[first + t, at, :] += rim_recv[p, side, 1, t].astype(F32)

    def low_in(p):
        rim_up(p).wait_recv()
        rim_in(p, 0, RIM)

    def high_in(p):
        rim_down(p).wait_recv()
        rim_in(p, 1, nb)

    def finish(p, i):
        to = rows(i * T, T, T)
        for h in range(2):
            base = (2 * p + h) * 3 * HD
            grad[rows(base + HD, HD, HD), to] = unrope(dk[i + RIM, feature(p, h), :], i)
            grad[rows(base + 2 * HD, HD, HD), to] = dv[i + RIM, feature(p, h), :].astype(BF16)

    def weight_grads(p, sub):
        c = 2 * p + sub
        order = []
        for n in range(nz):
            order.append(nz - 1 - n // 2 if n % 2 == 0 else n // 2)
        for d in order:
            to = slice(d * share, (d + 1) * share)
            for h in range(2):
                base = (2 * p + h) * 3 * HD
                if sub == 0:
                    part[c, d, h * HD:(h + 1) * HD, :] = dot(grad[rows(base, HD, HD), :], acts[:, to]).astype(BF16)
                else:
                    part[c, d, 2 * h * HD:2 * (h + 1) * HD, :] = dot(
                        grad[rows(base + HD, 2 * HD, HD), :], acts[:, to]).astype(BF16)
            if sub == 0:
                part[c, d, 2 * HD:, :] = dot(att[rows(p * 2 * HD, 2 * HD, 2 * HD), :], og[:, to]).astype(BF16)
            if d > 0:
                @pl.when(z == 0)
                def _():
                    right(c, d).start()
            if d < nz - 1:
                @pl.when(z == nz - 1)
                def _():
                    left(c, d).start()

    def hop(c, n):
        up = z + nz - 1 - n
        down = n - (nz - 1 - z)

        @pl.when(has_low & (up < nz))
        def _():
            right(c, up).wait_recv()
            part[c, up] = (part[c, up].astype(F32) + recv[c, up + 1].astype(F32)).astype(BF16)
            right(c, up).start()

        @pl.when(has_high & (down >= 0))
        def _():
            left(c, down).wait_recv()
            part[c, down] = (part[c, down].astype(F32) + recv[c, down].astype(F32)).astype(BF16)
            left(c, down).start()

    def land(p, sub):
        c = 2 * p + sub

        def put(value):
            for h in range(2):
                base = (2 * p + h) * 3 * HD
                if sub == 0:
                    sums[rows(base, HD, HD), :] = value[h * HD:(h + 1) * HD]
                else:
                    sums[rows(base + HD, 2 * HD, HD), :] = value[2 * h * HD:2 * (h + 1) * HD]
            if sub == 0:
                sums[rows(3 * width + p * 2 * HD, 2 * HD, 2 * HD), :] = value[2 * HD:]

        @pl.when(z == 0)
        def _():
            left(c, z).wait_recv()
            put(part[c, z].astype(F32) + recv[c, z].astype(F32))

        @pl.when(z == nz - 1)
        def _():
            right(c, z).wait_recv()
            put(part[c, z].astype(F32) + recv[c, z + 1].astype(F32))

        @pl.when(has_low & has_high)
        def _():
            right(c, z).wait_recv()
            left(c, z).wait_recv()
            put(part[c, z].astype(F32) + recv[c, z].astype(F32) + recv[c, z + 1].astype(F32))

    odd = z % 2 == 1
    last = pairs - 1

    def tile(m):
        return jnp.where(odd, m, nb - 1 - m)

    def produce(m):
        to = rows(tile(m) * T, T, T)
        for k in list(range(1, nx)) + [0]:
            there = ((x + k) % nx) * 2
            at = rows((there + 1 - core) * cols, cols, cols)
            send1[k, m] = dot(w[at, :], grad[:, to]).astype(BF16)
            swap(k, m).start()
        for k in list(range(1, nx)) + [0]:
            there = ((x + k) % nx) * 2
            at = rows((there + core) * cols, cols, cols)
            own[k, m] = dot(w[at, :], grad[:, to]).astype(BF16)

    def forward(m):
        for k in range(1, nx):
            swap(k, m).wait_recv()
            recv1[k, m] = (own[k, m].astype(F32) + recv1[k, m].astype(F32)).astype(BF16)
            cross(k, m).start()

    def deliver(m):
        swap(0, m).wait_recv()
        value = own[0, m].astype(F32) + recv1[0, m].astype(F32)
        for k in range(1, nx):
            cross(k, m).wait_recv()
            value = value + recv2[k, m].astype(F32)
        in_out[rows(tile(m) * T, T, T), :] = value.astype(BF16).T

    @pl.loop(0, pairs * nb)
    def _(n):
        p, j = n // nb, n % nb
        i = jnp.where(j < 2, j + 2, jnp.where(j < 4, j - 2, jnp.where(j < 6, nb - 6 + j, j - 2)))
        i = jnp.where(p == last, tile(j), i)
        low_at = jnp.where(p == last, jnp.where(odd, 1, nb - 1), 3)
        high_at = jnp.where(p == last, jnp.where(odd, nb - 1, 1), 5)

        @pl.when(n == (2 if pairs > 1 else 0))
        def _():
            halo_arrive()

        block(p, i)

        @pl.when((j == low_at) & has_low)
        def _():
            rim_out(p, 1, 0)
            rim_down(p).start()

        @pl.when((j == high_at) & has_high)
        def _():
            rim_out(p, 0, nb + RIM)
            rim_up(p).start()

        if pairs > 1:
            for m in range(1, nz):
                @pl.when((p > 0) & (j == min(m, nb - 1)))
                def _():
                    if m < nz - 1:
                        hop(2 * p - 2, m)
                    else:
                        land(p - 1, 0)

            @pl.when((p > 0) & (j == 2))
            def _():
                weight_grads(p - 1, 1)

            for m in range(1, nz):
                @pl.when((p > 0) & (j == min(m + 4, nb - 1)))
                def _():
                    if m < nz - 1:
                        hop(2 * p - 1, m)
                    else:
                        land(p - 1, 1)

            @pl.when((p < last) & (j == nb - 1))
            def _():
                @pl.when(has_low)
                def _():
                    low_in(p)

                @pl.when(has_high)
                def _():
                    high_in(p)

                @pl.loop(0, nb)
                def _(t):
                    finish(p, t)

                weight_grads(p, 0)

        @pl.when((p == last) & (j == 4))
        def _():
            @pl.when(odd)
            def _():
                low_in(p)

            @pl.when(jnp.logical_not(odd) & has_high)
            def _():
                high_in(p)

        for at_step, tiles in ((4, (0, 1)), (5, (2, 3)), (6, (4,)), (7, tuple(range(5, nb - 2)))):
            @pl.when((p == last) & (j == at_step))
            def _():
                for m in tiles:
                    finish(p, tile(m))
                    produce(m)
                for m in tiles:
                    forward(m)

    weight_grads(last, 0)
    if nz > 2:
        hop(2 * last, 1)

    @pl.when(odd & has_high)
    def _():
        high_in(last)

    @pl.when(jnp.logical_not(odd) & has_low)
    def _():
        low_in(last)

    for m in (nb - 2, nb - 1):
        finish(last, tile(m))
    weight_grads(last, 1)
    for m in range(2, nz - 1):
        hop(2 * last, m)
    for m in (nb - 2, nb - 1):
        produce(m)
    if nz > 2:
        hop(2 * last + 1, 1)
    for m in (nb - 2, nb - 1):
        forward(m)
    for m in range(2, nz - 1):
        hop(2 * last + 1, m)
    for m in range(nb - 2):
        deliver(m)
    land(last, 0)
    for m in (nb - 2, nb - 1):
        deliver(m)
    land(last, 1)
    qkv_out[...] = sums[:3 * width, :].T
    ow_out[...] = sums[3 * width:, :].T

    @pl.when(has_high)
    def _():
        seg_up().wait_send()
        halo_up(kt, 0).wait_send()
        halo_up(vt, 1).wait_send()
        for p in range(pairs):
            rim_up(p).wait_send()

    @pl.when(has_low)
    def _():
        seg_down().wait_send()
        halo_down(kt, 0).wait_send()
        halo_down(vt, 1).wait_send()
        for p in range(pairs):
            rim_down(p).wait_send()

    for c in range(2 * pairs):
        for d in range(nz):
            if d > 0:
                @pl.when(z < d)
                def _():
                    right(c, d).wait_send()
            if d < nz - 1:
                @pl.when(z > d)
                def _():
                    left(c, d).wait_send()
    for k in range(nx):
        for m in range(nb):
            swap(k, m).wait_send()
            if k > 0:
                cross(k, m).wait_send()


def local(activations, out_grad, segment_ids, qkv_weight, out_weight):
    tokens, model = activations.shape
    columns = qkv_weight.shape[1]
    width = columns // 3
    pairs = width // (2 * HD)
    nb = tokens // T
    nt = nb + 2 * RIM
    nz = lax.axis_size("ctx")
    nx = lax.axis_size("head") // 2
    cols = model // (2 * nx)
    share = model // nz
    me = lax.axis_index("ctx")
    position = (me * tokens + jnp.arange(tokens, dtype=jnp.int32)).astype(F32)
    exponent = jnp.arange(HALF, dtype=jnp.int32).astype(F32) * (2.0 / HD)
    inverse = jnp.power(F32(10000.0), -exponent)
    angles = inverse[None, :, None] * position.reshape(nb, 1, T)
    cos, sin = jnp.cos(angles), jnp.sin(angles)
    vmem = pl.BlockSpec(memory_space=pltpu.VMEM)
    dma = pltpu.SemaphoreType.DMA
    v = pltpu.VMEM
    return pl.pallas_call(
        functools.partial(layer_kernel, nx, nz),
        in_specs=[vmem] * 7,
        out_specs=[vmem] * 3,
        out_shape=[
            jax.ShapeDtypeStruct((tokens, cols), BF16),
            jax.ShapeDtypeStruct((share, columns), F32),
            jax.ShapeDtypeStruct((share, width), F32),
        ],
        scratch_shapes=[
            v((columns, model), BF16), v((width, model), BF16),
            v((nt, width, T), BF16), v((nt, width, T), BF16),
            v((pairs, nt, T, 2 * HD + 128), BF16), v((pairs, nt, T, 2 * HD), BF16),
            v((nb, width, T), BF16), v((nb, width, T), BF16),
            v((nb, 128, T), BF16), v((nb, T), jnp.int32), v((nb, T), jnp.int32), v((2, T, T), F32),
            v((2, SPAN, T, T), F32), v((2, SPAN, T, T), BF16), v((2, SPAN, T, T), BF16),
            v((nt, width, T), F32), v((nt, width, T), F32),
            v((columns, tokens), BF16), v((width, tokens), BF16),
            v((pairs, 2, 2, RIM, 2 * HD, T), BF16), v((pairs, 2, 2, RIM, 2 * HD, T), BF16),
            v((2 * pairs, nz, 4 * HD, share), BF16), v((2 * pairs, nz + 1, 4 * HD, share), BF16),
            v((4 * width, share), F32),
            v((nx, nb, cols, T), BF16), v((nx, nb, cols, T), BF16),
            v((nx, nb, cols, T), BF16), v((nx, nb, cols, T), BF16),
            dma((2, 2)), dma((2, 2)), dma((2,)), dma((2,)), dma((pairs, 2)), dma((pairs, 2)),
            dma((2 * pairs, nz)), dma((2 * pairs, nz)), dma((2 * pairs, nz)), dma((2 * pairs, nz)),
            dma((nx, nb)), dma((nx, nb)), dma((nx, nb)), dma((nx, nb)),
        ],
        compiler_params=pltpu.CompilerParams(
            collective_id=0, has_side_effects=True, vmem_limit_bytes=60 * 1024 * 1024
        ),
        cost_estimate=pl.CostEstimate(
            flops=12 * tokens * SPAN * T * width + 16 * tokens * model * width,
            bytes_accessed=8 * tokens * model, transcendentals=tokens * SPAN * T * width // HD
        ),
    )(activations, out_grad, segment_ids.reshape(nb, T), qkv_weight, out_weight, cos, sin)


def solution(mesh):
    in_specs = (
        P(("groups", "ctx"), None),
        P(("groups", "ctx"), None),
        P(("groups", "ctx")),
        P(None, "head"),
        P(None, "head"),
    )
    out_specs = (
        P(("groups", "ctx"), "head"),
        P(("groups", "ctx"), "head"),
        P(("groups", "ctx"), "head"),
    )
    return jax.shard_map(local, mesh=mesh, in_specs=in_specs, out_specs=out_specs, check_vma=False)
```

```python
import functools
import itertools

import jax
import jax.numpy as jnp
import numpy as np
from jax import lax
from jax.experimental import pallas as pl
from jax.experimental.pallas import tpu as pltpu
from jax.sharding import PartitionSpec as P

HD = 64
HALF = HD // 2
WIN = 512
T = 256
RIM = WIN // T
SPAN = 2 * RIM + 1
LOW = -1e30
OUTSIDE = 127
PIECES = 4
NT = (((1,), (1,)), ((), ()))
F32 = jnp.float32
BF16 = jnp.bfloat16
MESH = pl.DeviceIdType.MESH


def dot(a, b):
    return jnp.dot(a, b, preferred_element_type=F32)


def layer_kernel(nx, nz, acts_in, og_in, seg_in, w_in, ow_in, cos_in, sin_in,
                 in_out, qkv_out, ow_out,
                 acts, og, seg, w, ow, cos_ref, sin_ref, acts_ls, og_ls, load_ls, wt, owt, kt, vt, kx, vx, qt, gt, pen, seg_low, seg_high, tri,
                 s_ref, p_ref, ds_ref, dk, dv, grad, att,
                 rim_send, rim_recv, part, recv, sums, send1, own, recv1, recv2,
                 halo_ss, halo_rs, seg_ss, seg_rs, rim_ss, rim_rs,
                 right_ss, right_rs, left_ss, left_rs, swap_ss, swap_rs, cross_ss, cross_rs):
    tokens, model = acts.shape
    width = ow.shape[1]
    heads = width // HD
    pairs = heads // 2
    nb = tokens // T
    cols = model // (2 * nx)
    share = model // nz
    head = lax.axis_index("head")
    z = lax.axis_index("ctx")
    x, core = head // 2, head % 2
    sibling = x * 2 + (1 - core)
    has_low, has_high = z > 0, z < nz - 1
    above = {"ctx": jnp.minimum(z + 1, nz - 1)}
    below = {"ctx": jnp.maximum(z - 1, 0)}

    def loads():
        here = pl.ds(z * nb, nb)
        pairs_of = ((w_in, w), (ow_in, ow), (cos_in.at[here], cos_ref), (sin_in.at[here], sin_ref), (seg_in, seg))
        return [pltpu.make_async_copy(src, dst, load_ls.at[n]) for n, (src, dst) in enumerate(pairs_of)]

    def load_tile(i):
        at = pl.ds(pl.multiple_of(i * T, T), T)
        return (pltpu.make_async_copy(acts_in.at[at], acts.at[at], acts_ls.at[i]),
                pltpu.make_async_copy(og_in.at[at], og.at[at], og_ls.at[i]))

    def early(j):
        return jnp.where(j < RIM, j, jnp.where(j < 2 * RIM, nb - 2 * RIM + j, j - RIM))

    for copy in loads():
        copy.start()
    for j in range(nb):
        for copy in load_tile(early(j)):
            copy.start()

    barrier = pltpu.get_barrier_semaphore()
    pl.semaphore_signal(barrier, inc=1, device_id={"head": sibling}, device_id_type=MESH)
    for k in range(1, nx):
        peer = ((x + k) % nx) * 2 + core
        pl.semaphore_signal(barrier, inc=1, device_id={"head": peer}, device_id_type=MESH)
    for k in range(1, nz):
        pl.semaphore_signal(barrier, inc=1, device_id={"ctx": (z + k) % nz}, device_id_type=MESH)

    def remote(src, dst, ss, rs, device):
        return pltpu.make_async_remote_copy(src_ref=src, dst_ref=dst, send_sem=ss, recv_sem=rs,
                                            device_id=device, device_id_type=MESH)

    def halo_up(a, n, p):
        at = pl.ds(p * 2 * HD, 2 * HD)
        return remote(a.at[pl.ds(nb, RIM), at], a.at[pl.ds(0, RIM), at], halo_ss.at[0, n, p], halo_rs.at[0, n, p], above)

    def halo_down(a, n, p):
        at = pl.ds(p * 2 * HD, 2 * HD)
        return remote(a.at[pl.ds(RIM, RIM), at], a.at[pl.ds(nb + RIM, RIM), at],
                      halo_ss.at[1, n, p], halo_rs.at[1, n, p], below)

    def seg_up():
        return remote(seg, seg_low, seg_ss.at[0], seg_rs.at[0], above)

    def seg_down():
        return remote(seg, seg_high, seg_ss.at[1], seg_rs.at[1], below)

    def rim_up(p):
        return remote(rim_send.at[p, 0], rim_recv.at[p, 0], rim_ss.at[p, 0], rim_rs.at[p, 0], above)

    def rim_down(p):
        return remote(rim_send.at[p, 1], rim_recv.at[p, 1], rim_ss.at[p, 1], rim_rs.at[p, 1], below)

    def right(c, d):
        return remote(part.at[c, d], recv.at[c, d + 1], right_ss.at[c, d], right_rs.at[c, d], above)

    def left(c, d):
        return remote(part.at[c, d], recv.at[c, d], left_ss.at[c, d], left_rs.at[c, d], below)

    def swap(k, r):
        return remote(send1.at[k, r], recv1.at[k, r], swap_ss.at[k, r], swap_rs.at[k, r], {"head": sibling})

    def cross(k, r):
        return remote(recv1.at[k, r], recv2.at[k, r], cross_ss.at[k, r], cross_rs.at[k, r],
                      {"head": ((x + k) % nx) * 2 + core})

    def rows(start, size, unit):
        return pl.ds(pl.multiple_of(start, unit), size)

    for copy in loads():
        copy.wait()

    @pl.loop(0, model // T)
    def _(c):
        at = rows(c * T, T, T)
        wt[:, at] = w[at, :].T
        owt[:, at] = ow[at, :].T

    lane_doc = lax.broadcasted_iota(jnp.int32, (128, T), 0)

    def doc_row(ids, i):
        return jnp.concatenate([ids[pl.ds(i * (T // 128) + n, 1), :] for n in range(T // 128)], axis=1)

    def token_major(t, row, which):
        one = jnp.where(lane_doc == row, 1.0, 0.0).astype(BF16).T
        for p in which:
            kx[p, t, :, :2 * HD] = kt[t, p * 2 * HD:(p + 1) * 2 * HD, :].T
            kx[p, t, :, 2 * HD:] = one
            vx[p, t] = vt[t, p * 2 * HD:(p + 1) * 2 * HD, :].T

    def project(i):
        at = rows(i * T, T, T)
        projected = lax.dot_general(wt[...], acts[at, :], NT, preferred_element_type=F32).astype(BF16)
        gt[i] = lax.dot_general(owt[...], og[at, :], NT, preferred_element_type=F32).astype(BF16)
        cos, sin = cos_ref[i], sin_ref[i]

        def rope(u):
            u = u.astype(F32)
            low, high = u[:HALF], u[HALF:]
            return jnp.concatenate([low * cos - high * sin, high * cos + low * sin], axis=0).astype(BF16)

        for h in range(heads):
            to = slice(h * HD, (h + 1) * HD)
            base = h * 3 * HD
            qt[i, to, :] = rope(projected[base:base + HD]) * BF16(HD ** -0.5)
            kt[i + RIM, to, :] = rope(projected[base + HD:base + 2 * HD])
            vt[i + RIM, to, :] = projected[base + 2 * HD:base + 3 * HD]
        row = doc_row(seg, i)
        pen[i] = jnp.where(lane_doc == row, 0.0, LOW).astype(BF16)
        token_major(i + RIM, row, range(pairs))

    @pl.loop(0, nb)
    def _(j):
        for copy in load_tile(early(j)):
            copy.wait()
        project(early(j))

        @pl.when(j == 2 * RIM - 1)
        def _():
            pl.semaphore_wait(barrier, nx + nz - 1)

            @pl.when(has_high)
            def _():
                seg_up().start()
                for p in range(pairs):
                    halo_up(kt, 0, p).start()
                    halo_up(vt, 1, p).start()

            @pl.when(has_low)
            def _():
                seg_down().start()
                for p in range(pairs):
                    halo_down(kt, 0, p).start()
                    halo_down(vt, 1, p).start()

    r = lax.broadcasted_iota(jnp.int32, (T, T), 0)
    c = lax.broadcasted_iota(jnp.int32, (T, T), 1)
    tri[0] = jnp.where(r >= c, 0.0, LOW).astype(F32)
    tri[1] = jnp.where(r <= c, 0.0, LOW).astype(F32)

    @pl.loop(0, nb + 2 * RIM)
    def _(t):
        dk[t] = jnp.zeros_like(dk[t])
        dv[t] = jnp.zeros_like(dv[t])

    def fill(a, first):
        a[first:first + RIM] = jnp.zeros((RIM, width, T), BF16)

    @pl.when(z == 0)
    def _():
        fill(kt, 0)
        fill(vt, 0)
        seg_low[...] = jnp.full_like(seg_low, OUTSIDE)

    @pl.when(z == nz - 1)
    def _():
        fill(kt, nb + RIM)
        fill(vt, nb + RIM)
        seg_high[...] = jnp.full_like(seg_high, OUTSIDE)

    def halo_arrive(p):
        @pl.when(has_low)
        def _():
            if p == 0:
                seg_up().wait_recv()
            halo_up(kt, 0, p).wait_recv()
            halo_up(vt, 1, p).wait_recv()

        @pl.when(has_high)
        def _():
            if p == 0:
                seg_down().wait_recv()
            halo_down(kt, 0, p).wait_recv()
            halo_down(vt, 1, p).wait_recv()

        for t in range(RIM):
            token_major(t, doc_row(seg_low, nb - RIM + t), [p])
            token_major(nb + RIM + t, doc_row(seg_high, t), [p])

    zero = jnp.zeros((HD, T), BF16)

    def place(h, block, rest):
        return jnp.concatenate(([block, zero] if h == 0 else [zero, block]) + rest, axis=0)

    def feature(p, h):
        return rows(p * 2 * HD + h * HD, HD, HD)

    def block(p, i):
        top, scale, delta = [None] * 2, [None] * 2, [None] * 2
        ats = [feature(p, h) for h in range(2)]

        def score(h):
            rhs = place(h, qt[i, ats[h], :], [pen[i]])
            high = None
            for t in range(SPAN):
                s = dot(kx[p, i + t], rhs)
                if t == 0:
                    s = s + tri[0]
                if t == SPAN - 1:
                    s = s + tri[1]
                s_ref[h, t] = s
                best = jnp.max(s.reshape(T // 8, 8, T), axis=0)
                high = best if high is None else jnp.maximum(high, best)
                yield
            top[h] = jnp.max(high, axis=0, keepdims=True)

        def soft(h):
            total = jnp.zeros((8, T), F32)
            for t in range(SPAN):
                e = jnp.exp(s_ref[h, t] - top[h])
                total = total + jnp.sum(e.reshape(T // 8, 8, T), axis=0)
                p_ref[h, t] = e.astype(BF16)
                yield
            scale[h] = 1.0 / jnp.sum(total, axis=0, keepdims=True)

        def attend(h):
            out = jnp.zeros((HD, T), F32)
            for t in range(SPAN):
                out = out + dot(vt[i + t, ats[h], :], p_ref[h, t])
                yield
            out = (out * scale[h]).astype(BF16)
            att[ats[h], rows(i * T, T, T)] = out
            delta[h] = jnp.sum(out.astype(F32) * gt[i, ats[h], :].astype(F32), axis=0, keepdims=True)

        def score_grad(h):
            rhs = place(h, gt[i, ats[h], :], [])
            for t in range(SPAN):
                back = dot(vx[p, i + t], rhs)
                ds_ref[h, t] = (p_ref[h, t].astype(F32) * (back - delta[h])).astype(BF16)
                yield

        def query_grad(h):
            out = jnp.zeros((HD, T), F32)
            for t in range(SPAN):
                out = out + dot(kt[i + t, ats[h], :], ds_ref[h, t])
                yield
            out = out * (scale[h] * HD ** -0.5)
            grad[rows((2 * p + h) * 3 * HD, HD, HD), rows(i * T, T, T)] = unrope(out, i)

        def value_grad(h):
            g = (gt[i, ats[h], :].astype(F32) * scale[h]).astype(BF16)
            for t in range(SPAN):
                dv[i + t, ats[h], :] += lax.dot_general(g, p_ref[h, t], NT, preferred_element_type=F32)
                yield

        def key_grad(h):
            q = (qt[i, ats[h], :].astype(F32) * scale[h]).astype(BF16)
            for t in range(SPAN):
                dk[i + t, ats[h], :] += lax.dot_general(q, ds_ref[h, t], NT, preferred_element_type=F32)
                yield

        def run(*stages):
            for _ in itertools.zip_longest(*stages):
                pass

        run(score(0))
        run(score(1))
        run(soft(0))
        run(attend(0))
        run(soft(1), value_grad(0))
        run(attend(1))
        run(score_grad(0), value_grad(1))
        run(score_grad(1))
        run(query_grad(0))
        run(key_grad(0))
        run(query_grad(1))
        run(key_grad(1))

    def unrope(u, i):
        cos, sin = cos_ref[i], sin_ref[i]
        low, high = u[:HALF], u[HALF:]
        return jnp.concatenate([low * cos + high * sin, high * cos - low * sin], axis=0).astype(BF16)

    def rim_out(p, side, first):
        at = rows(p * 2 * HD, 2 * HD, 2 * HD)
        for t in range(RIM):
            rim_send[p, side, 0, t] = dk[first + t, at, :].astype(BF16)
            rim_send[p, side, 1, t] = dv[first + t, at, :].astype(BF16)

    def rim_in(p, side, first):
        at = rows(p * 2 * HD, 2 * HD, 2 * HD)
        for t in range(RIM):
            dk[first + t, at, :] += rim_recv[p, side, 0, t].astype(F32)
            dv[first + t, at, :] += rim_recv[p, side, 1, t].astype(F32)

    def low_in(p):
        rim_up(p).wait_recv()
        rim_in(p, 0, RIM)

    def high_in(p):
        rim_down(p).wait_recv()
        rim_in(p, 1, nb)

    def finish(p, i):
        to = rows(i * T, T, T)
        for h in range(2):
            base = (2 * p + h) * 3 * HD
            grad[rows(base + HD, HD, HD), to] = unrope(dk[i + RIM, feature(p, h), :], i)
            grad[rows(base + 2 * HD, HD, HD), to] = dv[i + RIM, feature(p, h), :].astype(BF16)

    def weight_grads(p, sub):
        c = 2 * p + sub
        order = []
        for n in range(nz):
            order.append(nz - 1 - n // 2 if n % 2 == 0 else n // 2)
        for d in order:
            to = slice(d * share, (d + 1) * share)
            for h in range(2):
                base = (2 * p + h) * 3 * HD
                if sub == 0:
                    part[c, d, h * HD:(h + 1) * HD, :] = dot(grad[rows(base, HD, HD), :], acts[:, to]).astype(BF16)
                else:
                    part[c, d, 2 * h * HD:2 * (h + 1) * HD, :] = dot(
                        grad[rows(base + HD, 2 * HD, HD), :], acts[:, to]).astype(BF16)
            if sub == 0:
                part[c, d, 2 * HD:, :] = dot(att[rows(p * 2 * HD, 2 * HD, 2 * HD), :], og[:, to]).astype(BF16)
            if d > 0:
                @pl.when(z == 0)
                def _():
                    right(c, d).start()
            if d < nz - 1:
                @pl.when(z == nz - 1)
                def _():
                    left(c, d).start()

    def hop(c, n):
        up = z + nz - 1 - n
        down = n - (nz - 1 - z)

        @pl.when(has_low & (up < nz))
        def _():
            right(c, up).wait_recv()
            part[c, up] = (part[c, up].astype(F32) + recv[c, up + 1].astype(F32)).astype(BF16)
            right(c, up).start()

        @pl.when(has_high & (down >= 0))
        def _():
            left(c, down).wait_recv()
            part[c, down] = (part[c, down].astype(F32) + recv[c, down].astype(F32)).astype(BF16)
            left(c, down).start()

    def land(p, sub):
        c = 2 * p + sub

        def put(value):
            for h in range(2):
                base = (2 * p + h) * 3 * HD
                if sub == 0:
                    sums[rows(base, HD, HD), :] = value[h * HD:(h + 1) * HD]
                else:
                    sums[rows(base + HD, 2 * HD, HD), :] = value[2 * h * HD:2 * (h + 1) * HD]
            if sub == 0:
                sums[rows(3 * width + p * 2 * HD, 2 * HD, 2 * HD), :] = value[2 * HD:]

        @pl.when(z == 0)
        def _():
            left(c, z).wait_recv()
            put(part[c, z].astype(F32) + recv[c, z].astype(F32))

        @pl.when(z == nz - 1)
        def _():
            right(c, z).wait_recv()
            put(part[c, z].astype(F32) + recv[c, z + 1].astype(F32))

        @pl.when(has_low & has_high)
        def _():
            right(c, z).wait_recv()
            left(c, z).wait_recv()
            put(part[c, z].astype(F32) + recv[c, z].astype(F32) + recv[c, z + 1].astype(F32))

    odd = z % 2 == 1
    last = pairs - 1

    def tile(m):
        return jnp.where(odd, m, nb - 1 - m)

    def produce(m):
        to = rows(tile(m) * T, T, T)
        for k in list(range(1, nx)) + [0]:
            there = ((x + k) % nx) * 2
            at = rows((there + 1 - core) * cols, cols, cols)
            send1[k, m] = dot(w[at, :], grad[:, to]).astype(BF16)
            swap(k, m).start()
        for k in list(range(1, nx)) + [0]:
            there = ((x + k) % nx) * 2
            at = rows((there + core) * cols, cols, cols)
            own[k, m] = dot(w[at, :], grad[:, to]).astype(BF16)

    def forward(m):
        for k in range(1, nx):
            swap(k, m).wait_recv()
            recv1[k, m] = (own[k, m].astype(F32) + recv1[k, m].astype(F32)).astype(BF16)
            cross(k, m).start()

    def deliver(m):
        swap(0, m).wait_recv()
        value = own[0, m].astype(F32) + recv1[0, m].astype(F32)
        for k in range(1, nx):
            cross(k, m).wait_recv()
            value = value + recv2[k, m].astype(F32)
        in_out[rows(tile(m) * T, T, T), :] = value.astype(BF16).T

    @pl.loop(0, pairs * nb)
    def _(n):
        p, j = n // nb, n % nb
        i = jnp.where(j < 2, j + 2, jnp.where(j < 4, j - 2, jnp.where(j < 6, nb - 6 + j, j - 2)))
        i = jnp.where(p == last, tile(j), i)
        low_at = jnp.where(p == last, jnp.where(odd, 1, nb - 1), 3)
        high_at = jnp.where(p == last, jnp.where(odd, nb - 1, 1), 5)

        for q in range(pairs):
            @pl.when(n == (2 if q == 0 and pairs > 1 else q * nb))
            def _():
                halo_arrive(q)

        block(p, i)

        @pl.when((j == low_at) & has_low)
        def _():
            rim_out(p, 1, 0)
            rim_down(p).start()

        @pl.when((j == high_at) & has_high)
        def _():
            rim_out(p, 0, nb + RIM)
            rim_up(p).start()

        if pairs > 1:
            for m in range(1, nz):
                @pl.when((p > 0) & (j == min(m, nb - 1)))
                def _():
                    if m < nz - 1:
                        hop(2 * p - 2, m)
                    else:
                        land(p - 1, 0)

            @pl.when((p > 0) & (j == 2))
            def _():
                weight_grads(p - 1, 1)

            for m in range(1, nz):
                @pl.when((p > 0) & (j == min(m + 4, nb - 1)))
                def _():
                    if m < nz - 1:
                        hop(2 * p - 1, m)
                    else:
                        land(p - 1, 1)

            @pl.when((p < last) & (j == nb - 1))
            def _():
                @pl.when(has_low)
                def _():
                    low_in(p)

                @pl.when(has_high)
                def _():
                    high_in(p)

                @pl.loop(0, nb)
                def _(t):
                    finish(p, t)

                weight_grads(p, 0)

        @pl.when((p == last) & (j == 4))
        def _():
            @pl.when(odd)
            def _():
                low_in(p)

            @pl.when(jnp.logical_not(odd) & has_high)
            def _():
                high_in(p)

        for at_step, tiles in ((4, (0, 1)), (5, (2, 3)), (6, (4,)), (7, tuple(range(5, nb - 2)))):
            @pl.when((p == last) & (j == at_step))
            def _():
                for m in tiles:
                    finish(p, tile(m))
                    produce(m)
                for m in tiles:
                    forward(m)

    weight_grads(last, 0)
    if nz > 2:
        hop(2 * last, 1)

    @pl.when(odd & has_high)
    def _():
        high_in(last)

    @pl.when(jnp.logical_not(odd) & has_low)
    def _():
        low_in(last)

    for m in (nb - 2, nb - 1):
        finish(last, tile(m))
    weight_grads(last, 1)
    for m in range(2, nz - 1):
        hop(2 * last, m)
    for m in (nb - 2, nb - 1):
        produce(m)
    if nz > 2:
        hop(2 * last + 1, 1)
    for m in (nb - 2, nb - 1):
        forward(m)
    for m in range(2, nz - 1):
        hop(2 * last + 1, m)
    for m in range(nb - 2):
        deliver(m)
    land(last, 0)
    for m in (nb - 2, nb - 1):
        deliver(m)
    land(last, 1)
    qkv_out[...] = sums[:3 * width, :].T
    ow_out[...] = sums[3 * width:, :].T

    @pl.when(has_high)
    def _():
        seg_up().wait_send()
        for p in range(pairs):
            halo_up(kt, 0, p).wait_send()
            halo_up(vt, 1, p).wait_send()
            rim_up(p).wait_send()

    @pl.when(has_low)
    def _():
        seg_down().wait_send()
        for p in range(pairs):
            halo_down(kt, 0, p).wait_send()
            halo_down(vt, 1, p).wait_send()
            rim_down(p).wait_send()

    for c in range(2 * pairs):
        for d in range(nz):
            if d > 0:
                @pl.when(z < d)
                def _():
                    right(c, d).wait_send()
            if d < nz - 1:
                @pl.when(z > d)
                def _():
                    left(c, d).wait_send()
    for k in range(nx):
        for m in range(nb):
            swap(k, m).wait_send()
            if k > 0:
                cross(k, m).wait_send()


def hand_over_kernel(count, *refs):
    sources, targets, sems = refs[:count], refs[count:2 * count], refs[2 * count]
    copies = []
    for source, target in zip(sources, targets):
        size = source.shape[0] // PIECES
        for n in range(PIECES):
            at = pl.ds(n * size, size)
            copies.append(pltpu.make_async_copy(source.at[at], target.at[at], sems.at[len(copies)]))
    for copy in copies:
        copy.start()
    for copy in copies:
        copy.wait()


def hand_over(arrays):
    anywhere = pl.BlockSpec(memory_space=pl.ANY)
    return pl.pallas_call(
        functools.partial(hand_over_kernel, len(arrays)),
        in_specs=[anywhere] * len(arrays),
        out_specs=[anywhere] * len(arrays),
        out_shape=[jax.ShapeDtypeStruct(a.shape, a.dtype) for a in arrays],
        scratch_shapes=[pltpu.SemaphoreType.DMA((len(arrays) * PIECES,))],
    )(*arrays)


def local(activations, out_grad, segment_ids, qkv_weight, out_weight):
    tokens, model = activations.shape
    columns = qkv_weight.shape[1]
    width = columns // 3
    pairs = width // (2 * HD)
    nb = tokens // T
    nt = nb + 2 * RIM
    nz = lax.axis_size("ctx")
    nx = lax.axis_size("head") // 2
    cols = model // (2 * nx)
    share = model // nz
    position = np.arange(nz * tokens, dtype=np.float32)
    exponent = np.arange(HALF, dtype=np.float32) * np.float32(2.0 / HD)
    inverse = np.power(np.float32(10000.0), -exponent).astype(np.float32)
    angles = (inverse[None, :, None] * position.reshape(nz * nb, 1, T)).astype(np.float64)
    cos, sin = jnp.asarray(np.cos(angles), F32), jnp.asarray(np.sin(angles), F32)
    vmem = pl.BlockSpec(memory_space=pltpu.VMEM)
    dma = pltpu.SemaphoreType.DMA
    v = pltpu.VMEM
    out = pl.pallas_call(
        functools.partial(layer_kernel, nx, nz),
        in_specs=[pl.BlockSpec(memory_space=pl.ANY)] * 7,
        out_specs=[vmem] * 3,
        out_shape=[
            jax.ShapeDtypeStruct((tokens, cols), BF16),
            jax.ShapeDtypeStruct((share, columns), F32),
            jax.ShapeDtypeStruct((share, width), F32),
        ],
        scratch_shapes=[
            v((tokens, model), BF16), v((tokens, model), BF16), v((tokens // 128, 128), jnp.int32),
            v((model, columns), BF16), v((model, width), BF16), v((nb, HALF, T), F32), v((nb, HALF, T), F32),
            dma((nb,)), dma((nb,)), dma((5,)),
            v((columns, model), BF16), v((width, model), BF16),
            v((nt, width, T), BF16), v((nt, width, T), BF16),
            v((pairs, nt, T, 2 * HD + 128), BF16), v((pairs, nt, T, 2 * HD), BF16),
            v((nb, width, T), BF16), v((nb, width, T), BF16),
            v((nb, 128, T), BF16), v((tokens // 128, 128), jnp.int32), v((tokens // 128, 128), jnp.int32), v((2, T, T), F32),
            v((2, SPAN, T, T), F32), v((2, SPAN, T, T), BF16), v((2, SPAN, T, T), BF16),
            v((nt, width, T), F32), v((nt, width, T), F32),
            v((columns, tokens), BF16), v((width, tokens), BF16),
            v((pairs, 2, 2, RIM, 2 * HD, T), BF16), v((pairs, 2, 2, RIM, 2 * HD, T), BF16),
            v((2 * pairs, nz, 4 * HD, share), BF16), v((2 * pairs, nz + 1, 4 * HD, share), BF16),
            v((4 * width, share), F32),
            v((nx, nb, cols, T), BF16), v((nx, nb, cols, T), BF16),
            v((nx, nb, cols, T), BF16), v((nx, nb, cols, T), BF16),
            dma((2, 2, pairs)), dma((2, 2, pairs)), dma((2,)), dma((2,)), dma((pairs, 2)), dma((pairs, 2)),
            dma((2 * pairs, nz)), dma((2 * pairs, nz)), dma((2 * pairs, nz)), dma((2 * pairs, nz)),
            dma((nx, nb)), dma((nx, nb)), dma((nx, nb)), dma((nx, nb)),
        ],
        compiler_params=pltpu.CompilerParams(
            collective_id=0, has_side_effects=True, vmem_limit_bytes=60 * 1024 * 1024
        ),
        cost_estimate=pl.CostEstimate(
            flops=12 * tokens * SPAN * T * width + 16 * tokens * model * width,
            bytes_accessed=8 * tokens * model, transcendentals=tokens * SPAN * T * width // HD
        ),
    )(activations, out_grad, segment_ids.reshape(tokens // 128, 128), qkv_weight, out_weight, cos, sin)
    return hand_over(out)


def solution(mesh):
    in_specs = (
        P(("groups", "ctx"), None),
        P(("groups", "ctx"), None),
        P(("groups", "ctx")),
        P(None, "head"),
        P(None, "head"),
    )
    out_specs = (
        P(("groups", "ctx"), "head"),
        P(("groups", "ctx"), "head"),
        P(("groups", "ctx"), "head"),
    )
    return jax.shard_map(local, mesh=mesh, in_specs=in_specs, out_specs=out_specs, check_vma=False)
```

```python
import functools
import itertools

import jax
import jax.numpy as jnp
import numpy as np
from jax import lax
from jax.experimental import pallas as pl
from jax.experimental.pallas import tpu as pltpu
from jax.sharding import PartitionSpec as P

HD = 64
HALF = HD // 2
WIN = 512
T = 256
RIM = WIN // T
SPAN = 2 * RIM + 1
LOW = -1e30
OUTSIDE = 127
PIECES = 2
NT = (((1,), (1,)), ((), ()))
F32 = jnp.float32
BF16 = jnp.bfloat16
MESH = pl.DeviceIdType.MESH


def dot(a, b):
    return jnp.dot(a, b, preferred_element_type=F32)


def layer_kernel(nx, nz, acts_in, og_in, seg_in, w_in, ow_in, cos_in, sin_in,
                 in_out, qkv_out, ow_out,
                 acts, og, seg, w, ow, cos_ref, sin_ref, acts_ls, og_ls, load_ls, wt, owt, kt, vt, kx, vx, qt, gt, pen, seg_low, seg_high, tri,
                 s_ref, p_ref, ds_ref, dk, dv, grad, att,
                 rim_send, rim_recv, part, recv, sums, send1, own, recv1, recv2,
                 halo_ss, halo_rs, seg_ss, seg_rs, rim_ss, rim_rs,
                 right_ss, right_rs, left_ss, left_rs, swap_ss, swap_rs, cross_ss, cross_rs):
    tokens, model = acts.shape
    width = ow.shape[1]
    heads = width // HD
    pairs = heads // 2
    nb = tokens // T
    cols = model // (2 * nx)
    share = model // nz
    head = lax.axis_index("head")
    z = lax.axis_index("ctx")
    x, core = head // 2, head % 2
    sibling = x * 2 + (1 - core)
    has_low, has_high = z > 0, z < nz - 1
    above = {"ctx": jnp.minimum(z + 1, nz - 1)}
    below = {"ctx": jnp.maximum(z - 1, 0)}

    def loads():
        here = pl.ds(z * nb, nb)
        pairs_of = ((w_in, w), (ow_in, ow), (cos_in.at[here], cos_ref), (sin_in.at[here], sin_ref), (seg_in, seg))
        return [pltpu.make_async_copy(src, dst, load_ls.at[n]) for n, (src, dst) in enumerate(pairs_of)]

    def load_tile(i):
        at = pl.ds(pl.multiple_of(i * T, T), T)
        return (pltpu.make_async_copy(acts_in.at[at], acts.at[at], acts_ls.at[i]),
                pltpu.make_async_copy(og_in.at[at], og.at[at], og_ls.at[i]))

    def early(j):
        return jnp.where(j < RIM, j, jnp.where(j < 2 * RIM, nb - 2 * RIM + j, j - RIM))

    for copy in loads():
        copy.start()
    for j in range(nb):
        for copy in load_tile(early(j)):
            copy.start()

    barrier = pltpu.get_barrier_semaphore()
    pl.semaphore_signal(barrier, inc=1, device_id={"head": sibling}, device_id_type=MESH)
    for k in range(1, nx):
        peer = ((x + k) % nx) * 2 + core
        pl.semaphore_signal(barrier, inc=1, device_id={"head": peer}, device_id_type=MESH)
    for k in range(1, nz):
        pl.semaphore_signal(barrier, inc=1, device_id={"ctx": (z + k) % nz}, device_id_type=MESH)

    def remote(src, dst, ss, rs, device):
        return pltpu.make_async_remote_copy(src_ref=src, dst_ref=dst, send_sem=ss, recv_sem=rs,
                                            device_id=device, device_id_type=MESH)

    def halo_up(a, n, p):
        at = pl.ds(p * 2 * HD, 2 * HD)
        return remote(a.at[pl.ds(nb, RIM), at], a.at[pl.ds(0, RIM), at], halo_ss.at[0, n, p], halo_rs.at[0, n, p], above)

    def halo_down(a, n, p):
        at = pl.ds(p * 2 * HD, 2 * HD)
        return remote(a.at[pl.ds(RIM, RIM), at], a.at[pl.ds(nb + RIM, RIM), at],
                      halo_ss.at[1, n, p], halo_rs.at[1, n, p], below)

    def seg_up():
        return remote(seg, seg_low, seg_ss.at[0], seg_rs.at[0], above)

    def seg_down():
        return remote(seg, seg_high, seg_ss.at[1], seg_rs.at[1], below)

    def rim_up(p):
        return remote(rim_send.at[p, 0], rim_recv.at[p, 0], rim_ss.at[p, 0], rim_rs.at[p, 0], above)

    def rim_down(p):
        return remote(rim_send.at[p, 1], rim_recv.at[p, 1], rim_ss.at[p, 1], rim_rs.at[p, 1], below)

    def right(c, d):
        return remote(part.at[c, d], recv.at[c, d + 1], right_ss.at[c, d], right_rs.at[c, d], above)

    def left(c, d):
        return remote(part.at[c, d], recv.at[c, d], left_ss.at[c, d], left_rs.at[c, d], below)

    def swap(k, r):
        return remote(send1.at[k, r], recv1.at[k, r], swap_ss.at[k, r], swap_rs.at[k, r], {"head": sibling})

    def cross(k, r):
        return remote(recv1.at[k, r], recv2.at[k, r], cross_ss.at[k, r], cross_rs.at[k, r],
                      {"head": ((x + k) % nx) * 2 + core})

    def rows(start, size, unit):
        return pl.ds(pl.multiple_of(start, unit), size)

    for copy in loads():
        copy.wait()

    @pl.loop(0, model // T)
    def _(c):
        at = rows(c * T, T, T)
        wt[:, at] = w[at, :].T
        owt[:, at] = ow[at, :].T

    lane_doc = lax.broadcasted_iota(jnp.int32, (128, T), 0)

    def doc_row(ids, i):
        return jnp.concatenate([ids[pl.ds(i * (T // 128) + n, 1), :] for n in range(T // 128)], axis=1)

    def token_major(t, row, which):
        one = jnp.where(lane_doc == row, 1.0, 0.0).astype(BF16).T
        for p in which:
            kx[p, t, :, :2 * HD] = kt[t, p * 2 * HD:(p + 1) * 2 * HD, :].T
            kx[p, t, :, 2 * HD:] = one
            vx[p, t] = vt[t, p * 2 * HD:(p + 1) * 2 * HD, :].T

    def project(i):
        at = rows(i * T, T, T)
        projected = lax.dot_general(wt[...], acts[at, :], NT, preferred_element_type=F32).astype(BF16)
        gt[i] = lax.dot_general(owt[...], og[at, :], NT, preferred_element_type=F32).astype(BF16)
        cos, sin = cos_ref[i], sin_ref[i]

        def rope(u):
            u = u.astype(F32)
            low, high = u[:HALF], u[HALF:]
            return jnp.concatenate([low * cos - high * sin, high * cos + low * sin], axis=0).astype(BF16)

        for h in range(heads):
            to = slice(h * HD, (h + 1) * HD)
            base = h * 3 * HD
            qt[i, to, :] = rope(projected[base:base + HD]) * BF16(HD ** -0.5)
            kt[i + RIM, to, :] = rope(projected[base + HD:base + 2 * HD])
            vt[i + RIM, to, :] = projected[base + 2 * HD:base + 3 * HD]
        row = doc_row(seg, i)
        pen[i] = jnp.where(lane_doc == row, 0.0, LOW).astype(BF16)
        token_major(i + RIM, row, range(pairs))

    @pl.loop(0, nb)
    def _(j):
        for copy in load_tile(early(j)):
            copy.wait()
        project(early(j))

        @pl.when(j == 2 * RIM - 1)
        def _():
            pl.semaphore_wait(barrier, nx + nz - 1)

            @pl.when(has_high)
            def _():
                seg_up().start()
                for p in range(pairs):
                    halo_up(kt, 0, p).start()
                    halo_up(vt, 1, p).start()

            @pl.when(has_low)
            def _():
                seg_down().start()
                for p in range(pairs):
                    halo_down(kt, 0, p).start()
                    halo_down(vt, 1, p).start()

    r = lax.broadcasted_iota(jnp.int32, (T, T), 0)
    c = lax.broadcasted_iota(jnp.int32, (T, T), 1)
    tri[0] = jnp.where(r >= c, 0.0, LOW).astype(F32)
    tri[1] = jnp.where(r <= c, 0.0, LOW).astype(F32)

    @pl.loop(0, nb + 2 * RIM)
    def _(t):
        dk[t] = jnp.zeros_like(dk[t])
        dv[t] = jnp.zeros_like(dv[t])

    def fill(a, first):
        a[first:first + RIM] = jnp.zeros((RIM, width, T), BF16)

    @pl.when(z == 0)
    def _():
        fill(kt, 0)
        fill(vt, 0)
        seg_low[...] = jnp.full_like(seg_low, OUTSIDE)

    @pl.when(z == nz - 1)
    def _():
        fill(kt, nb + RIM)
        fill(vt, nb + RIM)
        seg_high[...] = jnp.full_like(seg_high, OUTSIDE)

    def halo_arrive(p):
        @pl.when(has_low)
        def _():
            if p == 0:
                seg_up().wait_recv()
            halo_up(kt, 0, p).wait_recv()
            halo_up(vt, 1, p).wait_recv()

        @pl.when(has_high)
        def _():
            if p == 0:
                seg_down().wait_recv()
            halo_down(kt, 0, p).wait_recv()
            halo_down(vt, 1, p).wait_recv()

        for t in range(RIM):
            token_major(t, doc_row(seg_low, nb - RIM + t), [p])
            token_major(nb + RIM + t, doc_row(seg_high, t), [p])

    zero = jnp.zeros((HD, T), BF16)

    def place(h, block, rest):
        return jnp.concatenate(([block, zero] if h == 0 else [zero, block]) + rest, axis=0)

    def feature(p, h):
        return rows(p * 2 * HD + h * HD, HD, HD)

    def block(p, i):
        top, scale, delta = [None] * 2, [None] * 2, [None] * 2
        ats = [feature(p, h) for h in range(2)]

        def score(h):
            rhs = place(h, qt[i, ats[h], :], [pen[i]])
            high = None
            for t in range(SPAN):
                s = dot(kx[p, i + t], rhs)
                if t == 0:
                    s = s + tri[0]
                if t == SPAN - 1:
                    s = s + tri[1]
                s_ref[h, t] = s
                best = jnp.max(s.reshape(T // 8, 8, T), axis=0)
                high = best if high is None else jnp.maximum(high, best)
                yield
            top[h] = jnp.max(high, axis=0, keepdims=True)

        def soft(h):
            total = jnp.zeros((8, T), F32)
            for t in range(SPAN):
                e = jnp.exp(s_ref[h, t] - top[h])
                total = total + jnp.sum(e.reshape(T // 8, 8, T), axis=0)
                p_ref[h, t] = e.astype(BF16)
                yield
            scale[h] = 1.0 / jnp.sum(total, axis=0, keepdims=True)

        def attend(h):
            out = jnp.zeros((HD, T), F32)
            for t in range(SPAN):
                out = out + dot(vt[i + t, ats[h], :], p_ref[h, t])
                yield
            out = (out * scale[h]).astype(BF16)
            att[ats[h], rows(i * T, T, T)] = out
            delta[h] = jnp.sum(out.astype(F32) * gt[i, ats[h], :].astype(F32), axis=0, keepdims=True)

        def score_grad(h):
            rhs = place(h, gt[i, ats[h], :], [])
            for t in range(SPAN):
                back = dot(vx[p, i + t], rhs)
                ds_ref[h, t] = (p_ref[h, t].astype(F32) * (back - delta[h])).astype(BF16)
                yield

        def query_grad(h):
            out = jnp.zeros((HD, T), F32)
            for t in range(SPAN):
                out = out + dot(kt[i + t, ats[h], :], ds_ref[h, t])
                yield
            out = out * (scale[h] * HD ** -0.5)
            grad[rows((2 * p + h) * 3 * HD, HD, HD), rows(i * T, T, T)] = unrope(out, i)

        def value_grad(h):
            g = (gt[i, ats[h], :].astype(F32) * scale[h]).astype(BF16)
            for t in range(SPAN):
                dv[i + t, ats[h], :] += lax.dot_general(g, p_ref[h, t], NT, preferred_element_type=F32)
                yield

        def key_grad(h):
            q = (qt[i, ats[h], :].astype(F32) * scale[h]).astype(BF16)
            for t in range(SPAN):
                dk[i + t, ats[h], :] += lax.dot_general(q, ds_ref[h, t], NT, preferred_element_type=F32)
                yield

        def run(*stages):
            for _ in itertools.zip_longest(*stages):
                pass

        run(score(0))
        run(score(1))
        run(soft(0))
        run(attend(0))
        run(soft(1), value_grad(0))
        run(attend(1))
        run(score_grad(0), value_grad(1))
        run(score_grad(1))
        run(query_grad(0))
        run(key_grad(0))
        run(query_grad(1))
        run(key_grad(1))

    def unrope(u, i):
        cos, sin = cos_ref[i], sin_ref[i]
        low, high = u[:HALF], u[HALF:]
        return jnp.concatenate([low * cos + high * sin, high * cos - low * sin], axis=0).astype(BF16)

    def rim_out(p, side, first):
        at = rows(p * 2 * HD, 2 * HD, 2 * HD)
        for t in range(RIM):
            rim_send[p, side, 0, t] = dk[first + t, at, :].astype(BF16)
            rim_send[p, side, 1, t] = dv[first + t, at, :].astype(BF16)

    def rim_in(p, side, first):
        at = rows(p * 2 * HD, 2 * HD, 2 * HD)
        for t in range(RIM):
            dk[first + t, at, :] += rim_recv[p, side, 0, t].astype(F32)
            dv[first + t, at, :] += rim_recv[p, side, 1, t].astype(F32)

    def low_in(p):
        rim_up(p).wait_recv()
        rim_in(p, 0, RIM)

    def high_in(p):
        rim_down(p).wait_recv()
        rim_in(p, 1, nb)

    def finish(p, i):
        to = rows(i * T, T, T)
        for h in range(2):
            base = (2 * p + h) * 3 * HD
            grad[rows(base + HD, HD, HD), to] = unrope(dk[i + RIM, feature(p, h), :], i)
            grad[rows(base + 2 * HD, HD, HD), to] = dv[i + RIM, feature(p, h), :].astype(BF16)

    def weight_grads(p, sub):
        c = 2 * p + sub
        order = []
        for n in range(nz):
            order.append(nz - 1 - n // 2 if n % 2 == 0 else n // 2)
        for d in order:
            to = slice(d * share, (d + 1) * share)
            for h in range(2):
                base = (2 * p + h) * 3 * HD
                if sub == 0:
                    part[c, d, h * HD:(h + 1) * HD, :] = dot(grad[rows(base, HD, HD), :], acts[:, to]).astype(BF16)
                else:
                    part[c, d, 2 * h * HD:2 * (h + 1) * HD, :] = dot(
                        grad[rows(base + HD, 2 * HD, HD), :], acts[:, to]).astype(BF16)
            if sub == 0:
                part[c, d, 2 * HD:, :] = dot(att[rows(p * 2 * HD, 2 * HD, 2 * HD), :], og[:, to]).astype(BF16)
            if d > 0:
                @pl.when(z == 0)
                def _():
                    right(c, d).start()
            if d < nz - 1:
                @pl.when(z == nz - 1)
                def _():
                    left(c, d).start()

    def hop(c, n):
        up = z + nz - 1 - n
        down = n - (nz - 1 - z)

        @pl.when(has_low & (up < nz))
        def _():
            right(c, up).wait_recv()
            part[c, up] = (part[c, up].astype(F32) + recv[c, up + 1].astype(F32)).astype(BF16)
            right(c, up).start()

        @pl.when(has_high & (down >= 0))
        def _():
            left(c, down).wait_recv()
            part[c, down] = (part[c, down].astype(F32) + recv[c, down].astype(F32)).astype(BF16)
            left(c, down).start()

    def land(p, sub):
        c = 2 * p + sub

        def put(value):
            for h in range(2):
                base = (2 * p + h) * 3 * HD
                if sub == 0:
                    sums[rows(base, HD, HD), :] = value[h * HD:(h + 1) * HD]
                else:
                    sums[rows(base + HD, 2 * HD, HD), :] = value[2 * h * HD:2 * (h + 1) * HD]
            if sub == 0:
                sums[rows(3 * width + p * 2 * HD, 2 * HD, 2 * HD), :] = value[2 * HD:]

        @pl.when(z == 0)
        def _():
            left(c, z).wait_recv()
            put(part[c, z].astype(F32) + recv[c, z].astype(F32))

        @pl.when(z == nz - 1)
        def _():
            right(c, z).wait_recv()
            put(part[c, z].astype(F32) + recv[c, z + 1].astype(F32))

        @pl.when(has_low & has_high)
        def _():
            right(c, z).wait_recv()
            left(c, z).wait_recv()
            put(part[c, z].astype(F32) + recv[c, z].astype(F32) + recv[c, z + 1].astype(F32))

    odd = z % 2 == 1
    last = pairs - 1

    def tile(m):
        return jnp.where(odd, m, nb - 1 - m)

    def produce(m):
        to = rows(tile(m) * T, T, T)
        for k in list(range(1, nx)) + [0]:
            there = ((x + k) % nx) * 2
            at = rows((there + 1 - core) * cols, cols, cols)
            send1[k, m] = dot(w[at, :], grad[:, to]).astype(BF16)
            swap(k, m).start()
        for k in list(range(1, nx)) + [0]:
            there = ((x + k) % nx) * 2
            at = rows((there + core) * cols, cols, cols)
            own[k, m] = dot(w[at, :], grad[:, to]).astype(BF16)

    def forward(m):
        for k in range(1, nx):
            swap(k, m).wait_recv()
            recv1[k, m] = (own[k, m].astype(F32) + recv1[k, m].astype(F32)).astype(BF16)
            cross(k, m).start()

    def deliver(m):
        swap(0, m).wait_recv()
        value = own[0, m].astype(F32) + recv1[0, m].astype(F32)
        for k in range(1, nx):
            cross(k, m).wait_recv()
            value = value + recv2[k, m].astype(F32)
        in_out[rows(tile(m) * T, T, T), :] = value.astype(BF16).T

    @pl.loop(0, pairs * nb)
    def _(n):
        p, j = n // nb, n % nb
        i = jnp.where(j < 2, j + 2, jnp.where(j < 4, j - 2, jnp.where(j < 6, nb - 6 + j, j - 2)))
        i = jnp.where(p == last, tile(j), i)
        low_at = jnp.where(p == last, jnp.where(odd, 1, nb - 1), 3)
        high_at = jnp.where(p == last, jnp.where(odd, nb - 1, 1), 5)

        for q in range(pairs):
            @pl.when(n == (2 if q == 0 and pairs > 1 else q * nb))
            def _():
                halo_arrive(q)

        block(p, i)

        @pl.when((j == low_at) & has_low)
        def _():
            rim_out(p, 1, 0)
            rim_down(p).start()

        @pl.when((j == high_at) & has_high)
        def _():
            rim_out(p, 0, nb + RIM)
            rim_up(p).start()

        if pairs > 1:
            for m in range(1, nz):
                @pl.when((p > 0) & (j == min(m, nb - 1)))
                def _():
                    if m < nz - 1:
                        hop(2 * p - 2, m)
                    else:
                        land(p - 1, 0)

            @pl.when((p > 0) & (j == 2))
            def _():
                weight_grads(p - 1, 1)

            for m in range(1, nz):
                @pl.when((p > 0) & (j == min(m + 4, nb - 1)))
                def _():
                    if m < nz - 1:
                        hop(2 * p - 1, m)
                    else:
                        land(p - 1, 1)

            @pl.when((p < last) & (j == nb - 1))
            def _():
                @pl.when(has_low)
                def _():
                    low_in(p)

                @pl.when(has_high)
                def _():
                    high_in(p)

                @pl.loop(0, nb)
                def _(t):
                    finish(p, t)

                weight_grads(p, 0)

        @pl.when((p == last) & (j == 4))
        def _():
            @pl.when(odd)
            def _():
                low_in(p)

            @pl.when(jnp.logical_not(odd) & has_high)
            def _():
                high_in(p)

        for at_step, tiles in ((4, (0, 1)), (5, (2, 3)), (6, (4,)), (7, tuple(range(5, nb - 2)))):
            @pl.when((p == last) & (j == at_step))
            def _():
                for m in tiles:
                    finish(p, tile(m))
                    produce(m)
                for m in tiles:
                    forward(m)

    weight_grads(last, 0)
    if nz > 2:
        hop(2 * last, 1)

    @pl.when(odd & has_high)
    def _():
        high_in(last)

    @pl.when(jnp.logical_not(odd) & has_low)
    def _():
        low_in(last)

    for m in (nb - 2, nb - 1):
        finish(last, tile(m))
    weight_grads(last, 1)
    for m in range(2, nz - 1):
        hop(2 * last, m)
    for m in (nb - 2, nb - 1):
        produce(m)
    if nz > 2:
        hop(2 * last + 1, 1)
    for m in (nb - 2, nb - 1):
        forward(m)
    for m in range(2, nz - 1):
        hop(2 * last + 1, m)
    for m in range(nb - 2):
        deliver(m)
    land(last, 0)
    for m in (nb - 2, nb - 1):
        deliver(m)
    land(last, 1)
    qkv_out[...] = sums[:3 * width, :].T
    ow_out[...] = sums[3 * width:, :].T

    @pl.when(has_high)
    def _():
        seg_up().wait_send()
        for p in range(pairs):
            halo_up(kt, 0, p).wait_send()
            halo_up(vt, 1, p).wait_send()
            rim_up(p).wait_send()

    @pl.when(has_low)
    def _():
        seg_down().wait_send()
        for p in range(pairs):
            halo_down(kt, 0, p).wait_send()
            halo_down(vt, 1, p).wait_send()
            rim_down(p).wait_send()

    for c in range(2 * pairs):
        for d in range(nz):
            if d > 0:
                @pl.when(z < d)
                def _():
                    right(c, d).wait_send()
            if d < nz - 1:
                @pl.when(z > d)
                def _():
                    left(c, d).wait_send()
    for k in range(nx):
        for m in range(nb):
            swap(k, m).wait_send()
            if k > 0:
                cross(k, m).wait_send()


def hand_over_kernel(count, *refs):
    sources, targets, held = refs[:count], refs[count:2 * count], refs[2 * count:3 * count]
    sems = refs[3 * count]
    into, out = [], []
    for source, target, hold in zip(sources, targets, held):
        size = source.shape[0] // PIECES
        for n in range(PIECES):
            at = pl.ds(n * size, size)
            into.append(pltpu.make_async_copy(source.at[at], hold.at[at], sems.at[0, len(into)]))
            out.append(pltpu.make_async_copy(hold.at[at], target.at[at], sems.at[1, len(out)]))
    for copy in into:
        copy.start()
    for first, second in zip(into, out):
        first.wait()
        second.start()
    for copy in out:
        copy.wait()


def hand_over(arrays):
    anywhere = pl.BlockSpec(memory_space=pl.ANY)
    return pl.pallas_call(
        functools.partial(hand_over_kernel, len(arrays)),
        in_specs=[anywhere] * len(arrays),
        out_specs=[anywhere] * len(arrays),
        out_shape=[jax.ShapeDtypeStruct(a.shape, a.dtype) for a in arrays],
        scratch_shapes=[pltpu.VMEM(a.shape, a.dtype) for a in arrays]
        + [pltpu.SemaphoreType.DMA((2, len(arrays) * PIECES))],
        compiler_params=pltpu.CompilerParams(vmem_limit_bytes=60 * 1024 * 1024),
    )(*arrays)


def local(activations, out_grad, segment_ids, qkv_weight, out_weight):
    tokens, model = activations.shape
    columns = qkv_weight.shape[1]
    width = columns // 3
    pairs = width // (2 * HD)
    nb = tokens // T
    nt = nb + 2 * RIM
    nz = lax.axis_size("ctx")
    nx = lax.axis_size("head") // 2
    cols = model // (2 * nx)
    share = model // nz
    position = np.arange(nz * tokens, dtype=np.float32)
    exponent = np.arange(HALF, dtype=np.float32) * np.float32(2.0 / HD)
    inverse = np.power(np.float32(10000.0), -exponent).astype(np.float32)
    angles = (inverse[None, :, None] * position.reshape(nz * nb, 1, T)).astype(np.float64)
    cos, sin = jnp.asarray(np.cos(angles), F32), jnp.asarray(np.sin(angles), F32)
    vmem = pl.BlockSpec(memory_space=pltpu.VMEM)
    dma = pltpu.SemaphoreType.DMA
    v = pltpu.VMEM
    out = pl.pallas_call(
        functools.partial(layer_kernel, nx, nz),
        in_specs=[pl.BlockSpec(memory_space=pl.ANY)] * 7,
        out_specs=[vmem] * 3,
        out_shape=[
            jax.ShapeDtypeStruct((tokens, cols), BF16),
            jax.ShapeDtypeStruct((share, columns), F32),
            jax.ShapeDtypeStruct((share, width), F32),
        ],
        scratch_shapes=[
            v((tokens, model), BF16), v((tokens, model), BF16), v((tokens // 128, 128), jnp.int32),
            v((model, columns), BF16), v((model, width), BF16), v((nb, HALF, T), F32), v((nb, HALF, T), F32),
            dma((nb,)), dma((nb,)), dma((5,)),
            v((columns, model), BF16), v((width, model), BF16),
            v((nt, width, T), BF16), v((nt, width, T), BF16),
            v((pairs, nt, T, 2 * HD + 128), BF16), v((pairs, nt, T, 2 * HD), BF16),
            v((nb, width, T), BF16), v((nb, width, T), BF16),
            v((nb, 128, T), BF16), v((tokens // 128, 128), jnp.int32), v((tokens // 128, 128), jnp.int32), v((2, T, T), F32),
            v((2, SPAN, T, T), F32), v((2, SPAN, T, T), BF16), v((2, SPAN, T, T), BF16),
            v((nt, width, T), F32), v((nt, width, T), F32),
            v((columns, tokens), BF16), v((width, tokens), BF16),
            v((pairs, 2, 2, RIM, 2 * HD, T), BF16), v((pairs, 2, 2, RIM, 2 * HD, T), BF16),
            v((2 * pairs, nz, 4 * HD, share), BF16), v((2 * pairs, nz + 1, 4 * HD, share), BF16),
            v((4 * width, share), F32),
            v((nx, nb, cols, T), BF16), v((nx, nb, cols, T), BF16),
            v((nx, nb, cols, T), BF16), v((nx, nb, cols, T), BF16),
            dma((2, 2, pairs)), dma((2, 2, pairs)), dma((2,)), dma((2,)), dma((pairs, 2)), dma((pairs, 2)),
            dma((2 * pairs, nz)), dma((2 * pairs, nz)), dma((2 * pairs, nz)), dma((2 * pairs, nz)),
            dma((nx, nb)), dma((nx, nb)), dma((nx, nb)), dma((nx, nb)),
        ],
        compiler_params=pltpu.CompilerParams(
            collective_id=0, has_side_effects=True, vmem_limit_bytes=60 * 1024 * 1024
        ),
        cost_estimate=pl.CostEstimate(
            flops=12 * tokens * SPAN * T * width + 16 * tokens * model * width,
            bytes_accessed=8 * tokens * model, transcendentals=tokens * SPAN * T * width // HD
        ),
    )(activations, out_grad, segment_ids.reshape(tokens // 128, 128), qkv_weight, out_weight, cos, sin)
    return hand_over(out)


def solution(mesh):
    in_specs = (
        P(("groups", "ctx"), None),
        P(("groups", "ctx"), None),
        P(("groups", "ctx")),
        P(None, "head"),
        P(None, "head"),
    )
    out_specs = (
        P(("groups", "ctx"), "head"),
        P(("groups", "ctx"), "head"),
        P(("groups", "ctx"), "head"),
    )
    return jax.shard_map(local, mesh=mesh, in_specs=in_specs, out_specs=out_specs, check_vma=False)
```

```python
import functools
import itertools

import jax
import jax.numpy as jnp
import numpy as np
from jax import lax
from jax.experimental import pallas as pl
from jax.experimental.pallas import tpu as pltpu
from jax.sharding import PartitionSpec as P

HD = 64
HALF = HD // 2
WIN = 512
T = 256
RIM = WIN // T
SPAN = 2 * RIM + 1
LOW = -1e30
OUTSIDE = 127
PIECES = 2
NT = (((1,), (1,)), ((), ()))
F32 = jnp.float32
BF16 = jnp.bfloat16
MESH = pl.DeviceIdType.MESH


def dot(a, b):
    return jnp.dot(a, b, preferred_element_type=F32)


def layer_kernel(nx, nz, acts_in, og_in, seg_in, w_in, ow_in, cos_in, sin_in,
                 in_out, qkv_out, ow_out,
                 acts, og, seg, w, ow, cos_ref, sin_ref, acts_ls, og_ls, load_ls, wt, owt, kt, vt, kx, vx, qt, gt, pen, seg_low, seg_high, tri,
                 s_ref, p_ref, ds_ref, dk, dv, grad, att,
                 rim_send, rim_recv, part, recv, sums, send1, own, recv1, recv2,
                 halo_ss, halo_rs, seg_ss, seg_rs, rim_ss, rim_rs,
                 right_ss, right_rs, left_ss, left_rs, swap_ss, swap_rs, cross_ss, cross_rs):
    tokens, model = acts.shape
    width = ow.shape[1]
    heads = width // HD
    pairs = heads // 2
    nb = tokens // T
    cols = model // (2 * nx)
    share = model // nz
    head = lax.axis_index("head")
    z = lax.axis_index("ctx")
    x, core = head // 2, head % 2
    sibling = x * 2 + (1 - core)
    has_low, has_high = z > 0, z < nz - 1
    above = {"ctx": jnp.minimum(z + 1, nz - 1)}
    below = {"ctx": jnp.maximum(z - 1, 0)}

    def loads():
        here = pl.ds(z * nb, nb)
        pairs_of = ((w_in, w), (ow_in, ow), (cos_in.at[here], cos_ref), (sin_in.at[here], sin_ref), (seg_in, seg))
        return [pltpu.make_async_copy(src, dst, load_ls.at[n]) for n, (src, dst) in enumerate(pairs_of)]

    def load_tile(i):
        at = pl.ds(pl.multiple_of(i * T, T), T)
        return (pltpu.make_async_copy(acts_in.at[at], acts.at[at], acts_ls.at[i]),
                pltpu.make_async_copy(og_in.at[at], og.at[at], og_ls.at[i]))

    def early(j):
        return jnp.where(j < RIM, j, jnp.where(j < 2 * RIM, nb - 2 * RIM + j, j - RIM))

    for copy in loads():
        copy.start()
    for j in range(nb):
        for copy in load_tile(early(j)):
            copy.start()

    barrier = pltpu.get_barrier_semaphore()
    pl.semaphore_signal(barrier, inc=1, device_id={"head": sibling}, device_id_type=MESH)
    for k in range(1, nx):
        peer = ((x + k) % nx) * 2 + core
        pl.semaphore_signal(barrier, inc=1, device_id={"head": peer}, device_id_type=MESH)
    for k in range(1, nz):
        pl.semaphore_signal(barrier, inc=1, device_id={"ctx": (z + k) % nz}, device_id_type=MESH)

    def remote(src, dst, ss, rs, device):
        return pltpu.make_async_remote_copy(src_ref=src, dst_ref=dst, send_sem=ss, recv_sem=rs,
                                            device_id=device, device_id_type=MESH)

    def halo_up(a, n, p):
        at = pl.ds(p * 2 * HD, 2 * HD)
        return remote(a.at[pl.ds(nb, RIM), at], a.at[pl.ds(0, RIM), at], halo_ss.at[0, n, p], halo_rs.at[0, n, p], above)

    def halo_down(a, n, p):
        at = pl.ds(p * 2 * HD, 2 * HD)
        return remote(a.at[pl.ds(RIM, RIM), at], a.at[pl.ds(nb + RIM, RIM), at],
                      halo_ss.at[1, n, p], halo_rs.at[1, n, p], below)

    def seg_up():
        return remote(seg, seg_low, seg_ss.at[0], seg_rs.at[0], above)

    def seg_down():
        return remote(seg, seg_high, seg_ss.at[1], seg_rs.at[1], below)

    def rim_up(p):
        return remote(rim_send.at[p, 0], rim_recv.at[p, 0], rim_ss.at[p, 0], rim_rs.at[p, 0], above)

    def rim_down(p):
        return remote(rim_send.at[p, 1], rim_recv.at[p, 1], rim_ss.at[p, 1], rim_rs.at[p, 1], below)

    def right(c, d):
        return remote(part.at[c, d], recv.at[c, d + 1], right_ss.at[c, d], right_rs.at[c, d], above)

    def left(c, d):
        return remote(part.at[c, d], recv.at[c, d], left_ss.at[c, d], left_rs.at[c, d], below)

    def swap(k, r):
        return remote(send1.at[k, r], recv1.at[k, r], swap_ss.at[k, r], swap_rs.at[k, r], {"head": sibling})

    def cross(k, r):
        return remote(recv1.at[k, r], recv2.at[k, r], cross_ss.at[k, r], cross_rs.at[k, r],
                      {"head": ((x + k) % nx) * 2 + core})

    def rows(start, size, unit):
        return pl.ds(pl.multiple_of(start, unit), size)

    for copy in loads():
        copy.wait()

    @pl.loop(0, model // T)
    def _(c):
        at = rows(c * T, T, T)
        wt[:, at] = w[at, :].T
        owt[:, at] = ow[at, :].T

    lane_doc = lax.broadcasted_iota(jnp.int32, (128, T), 0)

    def doc_row(ids, i):
        return jnp.concatenate([ids[pl.ds(i * (T // 128) + n, 1), :] for n in range(T // 128)], axis=1)

    def token_major(t, row, which):
        one = jnp.where(lane_doc == row, 1.0, 0.0).astype(BF16).T
        for p in which:
            kx[p, t, :, :2 * HD] = kt[t, p * 2 * HD:(p + 1) * 2 * HD, :].T
            kx[p, t, :, 2 * HD:] = one
            vx[p, t] = vt[t, p * 2 * HD:(p + 1) * 2 * HD, :].T

    def project(i):
        at = rows(i * T, T, T)
        projected = lax.dot_general(wt[...], acts[at, :], NT, preferred_element_type=F32).astype(BF16)
        gt[i] = lax.dot_general(owt[...], og[at, :], NT, preferred_element_type=F32).astype(BF16)
        cos, sin = cos_ref[i], sin_ref[i]

        def rope(u):
            u = u.astype(F32)
            low, high = u[:HALF], u[HALF:]
            return jnp.concatenate([low * cos - high * sin, high * cos + low * sin], axis=0).astype(BF16)

        for h in range(heads):
            to = slice(h * HD, (h + 1) * HD)
            base = h * 3 * HD
            qt[i, to, :] = rope(projected[base:base + HD]) * BF16(HD ** -0.5)
            kt[i + RIM, to, :] = rope(projected[base + HD:base + 2 * HD])
            vt[i + RIM, to, :] = projected[base + 2 * HD:base + 3 * HD]
        row = doc_row(seg, i)
        pen[i] = jnp.where(lane_doc == row, 0.0, LOW).astype(BF16)
        token_major(i + RIM, row, range(pairs))

    @pl.loop(0, nb)
    def _(j):
        for copy in load_tile(early(j)):
            copy.wait()
        project(early(j))

        @pl.when(j == 2 * RIM - 1)
        def _():
            pl.semaphore_wait(barrier, nx + nz - 1)

            @pl.when(has_high)
            def _():
                seg_up().start()
                for p in range(pairs):
                    halo_up(kt, 0, p).start()
                    halo_up(vt, 1, p).start()

            @pl.when(has_low)
            def _():
                seg_down().start()
                for p in range(pairs):
                    halo_down(kt, 0, p).start()
                    halo_down(vt, 1, p).start()

    r = lax.broadcasted_iota(jnp.int32, (T, T), 0)
    c = lax.broadcasted_iota(jnp.int32, (T, T), 1)
    tri[0] = jnp.where(r >= c, 0.0, LOW).astype(F32)
    tri[1] = jnp.where(r <= c, 0.0, LOW).astype(F32)

    @pl.loop(0, nb + 2 * RIM)
    def _(t):
        dk[t] = jnp.zeros_like(dk[t])
        dv[t] = jnp.zeros_like(dv[t])

    def fill(a, first):
        a[first:first + RIM] = jnp.zeros((RIM, width, T), BF16)

    @pl.when(z == 0)
    def _():
        fill(kt, 0)
        fill(vt, 0)
        seg_low[...] = jnp.full_like(seg_low, OUTSIDE)

    @pl.when(z == nz - 1)
    def _():
        fill(kt, nb + RIM)
        fill(vt, nb + RIM)
        seg_high[...] = jnp.full_like(seg_high, OUTSIDE)

    def halo_arrive(p):
        @pl.when(has_low)
        def _():
            if p == 0:
                seg_up().wait_recv()
            halo_up(kt, 0, p).wait_recv()
            halo_up(vt, 1, p).wait_recv()

        @pl.when(has_high)
        def _():
            if p == 0:
                seg_down().wait_recv()
            halo_down(kt, 0, p).wait_recv()
            halo_down(vt, 1, p).wait_recv()

        for t in range(RIM):
            token_major(t, doc_row(seg_low, nb - RIM + t), [p])
            token_major(nb + RIM + t, doc_row(seg_high, t), [p])

    zero = jnp.zeros((HD, T), BF16)

    def place(h, block, rest):
        return jnp.concatenate(([block, zero] if h == 0 else [zero, block]) + rest, axis=0)

    def feature(p, h):
        return rows(p * 2 * HD + h * HD, HD, HD)

    def block(p, i):
        top, scale, delta = [None] * 2, [None] * 2, [None] * 2
        ats = [feature(p, h) for h in range(2)]

        def score(h):
            rhs = place(h, qt[i, ats[h], :], [pen[i]])
            high = None
            for t in range(SPAN):
                s = dot(kx[p, i + t], rhs)
                if t == 0:
                    s = s + tri[0]
                if t == SPAN - 1:
                    s = s + tri[1]
                s_ref[h, t] = s
                best = jnp.max(s.reshape(T // 8, 8, T), axis=0)
                high = best if high is None else jnp.maximum(high, best)
                yield
            top[h] = jnp.max(high, axis=0, keepdims=True)

        def soft(h):
            total = jnp.zeros((8, T), F32)
            for t in range(SPAN):
                e = jnp.exp(s_ref[h, t] - top[h])
                total = total + jnp.sum(e.reshape(T // 8, 8, T), axis=0)
                p_ref[h, t] = e.astype(BF16)
                yield
            scale[h] = 1.0 / jnp.sum(total, axis=0, keepdims=True)

        def attend(h):
            out = jnp.zeros((HD, T), F32)
            for t in range(SPAN):
                out = out + dot(vt[i + t, ats[h], :], p_ref[h, t])
                yield
            out = (out * scale[h]).astype(BF16)
            att[ats[h], rows(i * T, T, T)] = out
            delta[h] = jnp.sum(out.astype(F32) * gt[i, ats[h], :].astype(F32), axis=0, keepdims=True)

        def score_grad(h):
            rhs = place(h, gt[i, ats[h], :], [])
            for t in range(SPAN):
                back = dot(vx[p, i + t], rhs)
                ds_ref[h, t] = (p_ref[h, t].astype(F32) * (back - delta[h])).astype(BF16)
                yield

        def query_grad(h):
            out = jnp.zeros((HD, T), F32)
            for t in range(SPAN):
                out = out + dot(kt[i + t, ats[h], :], ds_ref[h, t])
                yield
            out = out * (scale[h] * HD ** -0.5)
            grad[rows((2 * p + h) * 3 * HD, HD, HD), rows(i * T, T, T)] = unrope(out, i)

        def value_grad(h):
            g = (gt[i, ats[h], :].astype(F32) * scale[h]).astype(BF16)
            for t in range(SPAN):
                dv[i + t, ats[h], :] += lax.dot_general(g, p_ref[h, t], NT, preferred_element_type=F32)
                yield

        def key_grad(h):
            q = (qt[i, ats[h], :].astype(F32) * scale[h]).astype(BF16)
            for t in range(SPAN):
                dk[i + t, ats[h], :] += lax.dot_general(q, ds_ref[h, t], NT, preferred_element_type=F32)
                yield

        def run(*stages):
            for _ in itertools.zip_longest(*stages):
                pass

        run(score(0))
        run(score(1))
        run(soft(0))
        run(attend(0))
        run(soft(1), value_grad(0))
        run(attend(1))
        run(score_grad(0), value_grad(1))
        run(score_grad(1))
        run(query_grad(0))
        run(key_grad(0))
        run(query_grad(1))
        run(key_grad(1))

    def unrope(u, i):
        cos, sin = cos_ref[i], sin_ref[i]
        low, high = u[:HALF], u[HALF:]
        return jnp.concatenate([low * cos + high * sin, high * cos - low * sin], axis=0).astype(BF16)

    def rim_out(p, side, first):
        at = rows(p * 2 * HD, 2 * HD, 2 * HD)
        for t in range(RIM):
            rim_send[p, side, 0, t] = dk[first + t, at, :].astype(BF16)
            rim_send[p, side, 1, t] = dv[first + t, at, :].astype(BF16)

    def rim_in(p, side, first):
        at = rows(p * 2 * HD, 2 * HD, 2 * HD)
        for t in range(RIM):
            dk[first + t, at, :] += rim_recv[p, side, 0, t].astype(F32)
            dv[first + t, at, :] += rim_recv[p, side, 1, t].astype(F32)

    def low_in(p):
        rim_up(p).wait_recv()
        rim_in(p, 0, RIM)

    def high_in(p):
        rim_down(p).wait_recv()
        rim_in(p, 1, nb)

    def finish(p, i):
        to = rows(i * T, T, T)
        for h in range(2):
            base = (2 * p + h) * 3 * HD
            grad[rows(base + HD, HD, HD), to] = unrope(dk[i + RIM, feature(p, h), :], i)
            grad[rows(base + 2 * HD, HD, HD), to] = dv[i + RIM, feature(p, h), :].astype(BF16)

    def weight_grads(p, sub):
        c = 2 * p + sub
        order = []
        for n in range(nz):
            order.append(nz - 1 - n // 2 if n % 2 == 0 else n // 2)
        for d in order:
            to = slice(d * share, (d + 1) * share)
            for h in range(2):
                base = (2 * p + h) * 3 * HD
                if sub == 0:
                    part[c, d, h * HD:(h + 1) * HD, :] = dot(grad[rows(base, HD, HD), :], acts[:, to]).astype(BF16)
                else:
                    part[c, d, 2 * h * HD:2 * (h + 1) * HD, :] = dot(
                        grad[rows(base + HD, 2 * HD, HD), :], acts[:, to]).astype(BF16)
            if sub == 0:
                part[c, d, 2 * HD:, :] = dot(att[rows(p * 2 * HD, 2 * HD, 2 * HD), :], og[:, to]).astype(BF16)
            if d > 0:
                @pl.when(z == 0)
                def _():
                    right(c, d).start()
            if d < nz - 1:
                @pl.when(z == nz - 1)
                def _():
                    left(c, d).start()

    def hop(c, n):
        up = z + nz - 1 - n
        down = n - (nz - 1 - z)

        @pl.when(has_low & (up < nz))
        def _():
            right(c, up).wait_recv()
            part[c, up] = (part[c, up].astype(F32) + recv[c, up + 1].astype(F32)).astype(BF16)
            right(c, up).start()

        @pl.when(has_high & (down >= 0))
        def _():
            left(c, down).wait_recv()
            part[c, down] = (part[c, down].astype(F32) + recv[c, down].astype(F32)).astype(BF16)
            left(c, down).start()

    def land(p, sub):
        c = 2 * p + sub

        def put(value):
            for h in range(2):
                base = (2 * p + h) * 3 * HD
                if sub == 0:
                    sums[rows(base, HD, HD), :] = value[h * HD:(h + 1) * HD]
                else:
                    sums[rows(base + HD, 2 * HD, HD), :] = value[2 * h * HD:2 * (h + 1) * HD]
            if sub == 0:
                sums[rows(3 * width + p * 2 * HD, 2 * HD, 2 * HD), :] = value[2 * HD:]

        @pl.when(z == 0)
        def _():
            left(c, z).wait_recv()
            put(part[c, z].astype(F32) + recv[c, z].astype(F32))

        @pl.when(z == nz - 1)
        def _():
            right(c, z).wait_recv()
            put(part[c, z].astype(F32) + recv[c, z + 1].astype(F32))

        @pl.when(has_low & has_high)
        def _():
            right(c, z).wait_recv()
            left(c, z).wait_recv()
            put(part[c, z].astype(F32) + recv[c, z].astype(F32) + recv[c, z + 1].astype(F32))

    odd = z % 2 == 1
    last = pairs - 1

    def tile(m):
        return jnp.where(odd, m, nb - 1 - m)

    def produce(m):
        to = rows(tile(m) * T, T, T)
        for k in list(range(1, nx)) + [0]:
            there = ((x + k) % nx) * 2
            at = rows((there + 1 - core) * cols, cols, cols)
            send1[k, m] = dot(w[at, :], grad[:, to]).astype(BF16)
            swap(k, m).start()
        for k in list(range(1, nx)) + [0]:
            there = ((x + k) % nx) * 2
            at = rows((there + core) * cols, cols, cols)
            own[k, m] = dot(w[at, :], grad[:, to]).astype(BF16)

    def forward(m):
        for k in range(1, nx):
            swap(k, m).wait_recv()
            recv1[k, m] = (own[k, m].astype(F32) + recv1[k, m].astype(F32)).astype(BF16)
            cross(k, m).start()

    def deliver(m):
        swap(0, m).wait_recv()
        value = own[0, m].astype(F32) + recv1[0, m].astype(F32)
        for k in range(1, nx):
            cross(k, m).wait_recv()
            value = value + recv2[k, m].astype(F32)
        in_out[rows(tile(m) * T, T, T), :] = value.astype(BF16).T

    if pairs > 1:
        plan = [(0, 2), (0, 3), (0, 4), (0, 0), (0, 1), (0, nb - 2), (0, nb - 1), (1, 0), (1, 1)]
        plan = plan + [(0, i) for i in range(5, nb - 2)] + [(1, m) for m in range(2, nb)]
    else:
        plan = [(0, m) for m in range(nb)]

    def after(p, i):
        return plan.index((p, i))

    first_end = after(0, nb - 3) if pairs > 1 else None

    @pl.loop(0, len(plan))
    def _(n):
        p, i = jnp.int32(plan[0][0]), jnp.int32(plan[0][1])
        for k, (pair, at_block) in enumerate(plan[1:], 1):
            p = jnp.where(n == k, pair, p)
            i = jnp.where(n == k, at_block, i)
        i = jnp.where(p == last, tile(i), i)

        for q in range(pairs):
            @pl.when(n == (after(q, 0) if q == last else 3))
            def _():
                halo_arrive(q)

        block(p, i)

        if pairs > 1:
            @pl.when((n == after(0, 1)) & has_low)
            def _():
                rim_out(0, 1, 0)
                rim_down(0).start()

            @pl.when((n == after(0, nb - 1)) & has_high)
            def _():
                rim_out(0, 0, nb + RIM)
                rim_up(0).start()

            @pl.when(n == first_end)
            def _():
                @pl.when(has_low)
                def _():
                    low_in(0)

                @pl.when(has_high)
                def _():
                    high_in(0)

                @pl.loop(0, nb)
                def _(t):
                    finish(0, t)

                weight_grads(0, 0)
                weight_grads(0, 1)

            for m in range(1, nz - 1):
                @pl.when(n == after(1, min(2 + m, nb - 1)))
                def _():
                    hop(0, m)

            @pl.when(n == after(1, nb - 2))
            def _():
                if nz > 2:
                    hop(1, 1)

        low_at = jnp.where(odd, after(last, 1), after(last, nb - 1))
        high_at = jnp.where(odd, after(last, nb - 1), after(last, 1))

        @pl.when((n == low_at) & has_low)
        def _():
            rim_out(last, 1, 0)
            rim_down(last).start()

        @pl.when((n == high_at) & has_high)
        def _():
            rim_out(last, 0, nb + RIM)
            rim_up(last).start()

        @pl.when(n == after(last, 2))
        def _():
            @pl.when(odd)
            def _():
                low_in(last)

            @pl.when(jnp.logical_not(odd) & has_high)
            def _():
                high_in(last)

        @pl.when(n >= after(last, 2))
        def _():
            m = n - after(last, 2)
            finish(last, tile(m))
            produce(m)
            forward(m)

    weight_grads(last, 0)
    if pairs > 1:
        for m in range(2, nz - 1):
            hop(1, m)
    if nz > 2:
        hop(2 * last, 1)

    @pl.when(odd & has_high)
    def _():
        high_in(last)

    @pl.when(jnp.logical_not(odd) & has_low)
    def _():
        low_in(last)

    for m in (nb - 2, nb - 1):
        finish(last, tile(m))
    weight_grads(last, 1)
    for m in range(2, nz - 1):
        hop(2 * last, m)
    for m in (nb - 2, nb - 1):
        produce(m)
    if nz > 2:
        hop(2 * last + 1, 1)
    for m in (nb - 2, nb - 1):
        forward(m)
    for m in range(2, nz - 1):
        hop(2 * last + 1, m)
    if pairs > 1:
        land(0, 0)
        land(0, 1)
    for m in range(nb - 2):
        deliver(m)
    land(last, 0)
    for m in (nb - 2, nb - 1):
        deliver(m)
    land(last, 1)
    qkv_out[...] = sums[:3 * width, :].T
    ow_out[...] = sums[3 * width:, :].T

    @pl.when(has_high)
    def _():
        seg_up().wait_send()
        for p in range(pairs):
            halo_up(kt, 0, p).wait_send()
            halo_up(vt, 1, p).wait_send()
            rim_up(p).wait_send()

    @pl.when(has_low)
    def _():
        seg_down().wait_send()
        for p in range(pairs):
            halo_down(kt, 0, p).wait_send()
            halo_down(vt, 1, p).wait_send()
            rim_down(p).wait_send()

    for c in range(2 * pairs):
        for d in range(nz):
            if d > 0:
                @pl.when(z < d)
                def _():
                    right(c, d).wait_send()
            if d < nz - 1:
                @pl.when(z > d)
                def _():
                    left(c, d).wait_send()
    for k in range(nx):
        for m in range(nb):
            swap(k, m).wait_send()
            if k > 0:
                cross(k, m).wait_send()


def hand_over_kernel(count, *refs):
    sources, targets, held = refs[:count], refs[count:2 * count], refs[2 * count:3 * count]
    sems = refs[3 * count]
    into, out = [], []
    for source, target, hold in zip(sources, targets, held):
        size = source.shape[0] // PIECES
        for n in range(PIECES):
            at = pl.ds(n * size, size)
            into.append(pltpu.make_async_copy(source.at[at], hold.at[at], sems.at[0, len(into)]))
            out.append(pltpu.make_async_copy(hold.at[at], target.at[at], sems.at[1, len(out)]))
    for copy in into:
        copy.start()
    for first, second in zip(into, out):
        first.wait()
        second.start()
    for copy in out:
        copy.wait()


def hand_over(arrays):
    anywhere = pl.BlockSpec(memory_space=pl.ANY)
    return pl.pallas_call(
        functools.partial(hand_over_kernel, len(arrays)),
        in_specs=[anywhere] * len(arrays),
        out_specs=[anywhere] * len(arrays),
        out_shape=[jax.ShapeDtypeStruct(a.shape, a.dtype) for a in arrays],
        scratch_shapes=[pltpu.VMEM(a.shape, a.dtype) for a in arrays]
        + [pltpu.SemaphoreType.DMA((2, len(arrays) * PIECES))],
        compiler_params=pltpu.CompilerParams(vmem_limit_bytes=60 * 1024 * 1024),
    )(*arrays)


def local(activations, out_grad, segment_ids, qkv_weight, out_weight):
    tokens, model = activations.shape
    columns = qkv_weight.shape[1]
    width = columns // 3
    pairs = width // (2 * HD)
    nb = tokens // T
    nt = nb + 2 * RIM
    nz = lax.axis_size("ctx")
    nx = lax.axis_size("head") // 2
    cols = model // (2 * nx)
    share = model // nz
    position = np.arange(nz * tokens, dtype=np.float32)
    exponent = np.arange(HALF, dtype=np.float32) * np.float32(2.0 / HD)
    inverse = np.power(np.float32(10000.0), -exponent).astype(np.float32)
    angles = (inverse[None, :, None] * position.reshape(nz * nb, 1, T)).astype(np.float64)
    cos, sin = jnp.asarray(np.cos(angles), F32), jnp.asarray(np.sin(angles), F32)
    vmem = pl.BlockSpec(memory_space=pltpu.VMEM)
    dma = pltpu.SemaphoreType.DMA
    v = pltpu.VMEM
    out = pl.pallas_call(
        functools.partial(layer_kernel, nx, nz),
        in_specs=[pl.BlockSpec(memory_space=pl.ANY)] * 7,
        out_specs=[vmem] * 3,
        out_shape=[
            jax.ShapeDtypeStruct((tokens, cols), BF16),
            jax.ShapeDtypeStruct((share, columns), F32),
            jax.ShapeDtypeStruct((share, width), F32),
        ],
        scratch_shapes=[
            v((tokens, model), BF16), v((tokens, model), BF16), v((tokens // 128, 128), jnp.int32),
            v((model, columns), BF16), v((model, width), BF16), v((nb, HALF, T), F32), v((nb, HALF, T), F32),
            dma((nb,)), dma((nb,)), dma((5,)),
            v((columns, model), BF16), v((width, model), BF16),
            v((nt, width, T), BF16), v((nt, width, T), BF16),
            v((pairs, nt, T, 2 * HD + 128), BF16), v((pairs, nt, T, 2 * HD), BF16),
            v((nb, width, T), BF16), v((nb, width, T), BF16),
            v((nb, 128, T), BF16), v((tokens // 128, 128), jnp.int32), v((tokens // 128, 128), jnp.int32), v((2, T, T), F32),
            v((2, SPAN, T, T), F32), v((2, SPAN, T, T), BF16), v((2, SPAN, T, T), BF16),
            v((nt, width, T), F32), v((nt, width, T), F32),
            v((columns, tokens), BF16), v((width, tokens), BF16),
            v((pairs, 2, 2, RIM, 2 * HD, T), BF16), v((pairs, 2, 2, RIM, 2 * HD, T), BF16),
            v((2 * pairs, nz, 4 * HD, share), BF16), v((2 * pairs, nz + 1, 4 * HD, share), BF16),
            v((4 * width, share), F32),
            v((nx, nb, cols, T), BF16), v((nx, nb, cols, T), BF16),
            v((nx, nb, cols, T), BF16), v((nx, nb, cols, T), BF16),
            dma((2, 2, pairs)), dma((2, 2, pairs)), dma((2,)), dma((2,)), dma((pairs, 2)), dma((pairs, 2)),
            dma((2 * pairs, nz)), dma((2 * pairs, nz)), dma((2 * pairs, nz)), dma((2 * pairs, nz)),
            dma((nx, nb)), dma((nx, nb)), dma((nx, nb)), dma((nx, nb)),
        ],
        compiler_params=pltpu.CompilerParams(
            collective_id=0, has_side_effects=True, vmem_limit_bytes=60 * 1024 * 1024
        ),
        cost_estimate=pl.CostEstimate(
            flops=12 * tokens * SPAN * T * width + 16 * tokens * model * width,
            bytes_accessed=8 * tokens * model, transcendentals=tokens * SPAN * T * width // HD
        ),
    )(activations, out_grad, segment_ids.reshape(tokens // 128, 128), qkv_weight, out_weight, cos, sin)
    return hand_over(out)


def solution(mesh):
    in_specs = (
        P(("groups", "ctx"), None),
        P(("groups", "ctx"), None),
        P(("groups", "ctx")),
        P(None, "head"),
        P(None, "head"),
    )
    out_specs = (
        P(("groups", "ctx"), "head"),
        P(("groups", "ctx"), "head"),
        P(("groups", "ctx"), "head"),
    )
    return jax.shard_map(local, mesh=mesh, in_specs=in_specs, out_specs=out_specs, check_vma=False)
```

```python
import functools
import itertools

import jax
import jax.numpy as jnp
import numpy as np
from jax import lax
from jax.experimental import pallas as pl
from jax.experimental.pallas import tpu as pltpu
from jax.sharding import PartitionSpec as P

HD = 64
HALF = HD // 2
WIN = 512
T = 256
RIM = WIN // T
SPAN = 2 * RIM + 1
LOW = -1e30
OUTSIDE = 127
PIECES = 2
EARLY = 3
NT = (((1,), (1,)), ((), ()))
F32 = jnp.float32
BF16 = jnp.bfloat16
MESH = pl.DeviceIdType.MESH


def dot(a, b):
    return jnp.dot(a, b, preferred_element_type=F32)


def layer_kernel(nx, nz, acts_in, og_in, seg_in, w_in, ow_in, cos_in, sin_in,
                 in_out, qkv_out, ow_out,
                 in_held, in_sem, acts, og, seg, w, ow, cos_ref, sin_ref, acts_ls, og_ls, load_ls, wt, owt, kt, vt, kx, vx, qt, gt, pen, seg_low, seg_high, tri,
                 s_ref, p_ref, ds_ref, dk, dv, grad, att,
                 rim_send, rim_recv, part, recv, sums, send1, own, recv1, recv2,
                 halo_ss, halo_rs, seg_ss, seg_rs, rim_ss, rim_rs,
                 right_ss, right_rs, left_ss, left_rs, swap_ss, swap_rs, cross_ss, cross_rs):
    tokens, model = acts.shape
    width = ow.shape[1]
    heads = width // HD
    pairs = heads // 2
    nb = tokens // T
    cols = model // (2 * nx)
    share = model // nz
    head = lax.axis_index("head")
    z = lax.axis_index("ctx")
    x, core = head // 2, head % 2
    sibling = x * 2 + (1 - core)
    has_low, has_high = z > 0, z < nz - 1
    above = {"ctx": jnp.minimum(z + 1, nz - 1)}
    below = {"ctx": jnp.maximum(z - 1, 0)}

    def loads():
        here = pl.ds(z * nb, nb)
        pairs_of = ((w_in, w), (ow_in, ow), (cos_in.at[here], cos_ref), (sin_in.at[here], sin_ref), (seg_in, seg))
        return [pltpu.make_async_copy(src, dst, load_ls.at[n]) for n, (src, dst) in enumerate(pairs_of)]

    def load_tile(i):
        at = pl.ds(pl.multiple_of(i * T, T), T)
        return (pltpu.make_async_copy(acts_in.at[at], acts.at[at], acts_ls.at[i]),
                pltpu.make_async_copy(og_in.at[at], og.at[at], og_ls.at[i]))

    def early(j):
        return jnp.where(j < RIM, j, jnp.where(j < 2 * RIM, nb - 2 * RIM + j, j - RIM))

    for copy in loads():
        copy.start()
    for j in range(nb):
        for copy in load_tile(early(j)):
            copy.start()

    barrier = pltpu.get_barrier_semaphore()
    pl.semaphore_signal(barrier, inc=1, device_id={"head": sibling}, device_id_type=MESH)
    for k in range(1, nx):
        peer = ((x + k) % nx) * 2 + core
        pl.semaphore_signal(barrier, inc=1, device_id={"head": peer}, device_id_type=MESH)
    for k in range(1, nz):
        pl.semaphore_signal(barrier, inc=1, device_id={"ctx": (z + k) % nz}, device_id_type=MESH)

    def remote(src, dst, ss, rs, device):
        return pltpu.make_async_remote_copy(src_ref=src, dst_ref=dst, send_sem=ss, recv_sem=rs,
                                            device_id=device, device_id_type=MESH)

    def halo_up(a, n, p):
        at = pl.ds(p * 2 * HD, 2 * HD)
        return remote(a.at[pl.ds(nb, RIM), at], a.at[pl.ds(0, RIM), at], halo_ss.at[0, n, p], halo_rs.at[0, n, p], above)

    def halo_down(a, n, p):
        at = pl.ds(p * 2 * HD, 2 * HD)
        return remote(a.at[pl.ds(RIM, RIM), at], a.at[pl.ds(nb + RIM, RIM), at],
                      halo_ss.at[1, n, p], halo_rs.at[1, n, p], below)

    def seg_up():
        return remote(seg, seg_low, seg_ss.at[0], seg_rs.at[0], above)

    def seg_down():
        return remote(seg, seg_high, seg_ss.at[1], seg_rs.at[1], below)

    def rim_up(p):
        return remote(rim_send.at[p, 0], rim_recv.at[p, 0], rim_ss.at[p, 0], rim_rs.at[p, 0], above)

    def rim_down(p):
        return remote(rim_send.at[p, 1], rim_recv.at[p, 1], rim_ss.at[p, 1], rim_rs.at[p, 1], below)

    def right(c, d):
        return remote(part.at[c, d], recv.at[c, d + 1], right_ss.at[c, d], right_rs.at[c, d], above)

    def left(c, d):
        return remote(part.at[c, d], recv.at[c, d], left_ss.at[c, d], left_rs.at[c, d], below)

    def swap(k, r):
        return remote(send1.at[k, r], recv1.at[k, r], swap_ss.at[k, r], swap_rs.at[k, r], {"head": sibling})

    def cross(k, r):
        return remote(recv1.at[k, r], recv2.at[k, r], cross_ss.at[k, r], cross_rs.at[k, r],
                      {"head": ((x + k) % nx) * 2 + core})

    def rows(start, size, unit):
        return pl.ds(pl.multiple_of(start, unit), size)

    for copy in loads():
        copy.wait()

    @pl.loop(0, model // T)
    def _(c):
        at = rows(c * T, T, T)
        wt[:, at] = w[at, :].T
        owt[:, at] = ow[at, :].T

    lane_doc = lax.broadcasted_iota(jnp.int32, (128, T), 0)

    def doc_row(ids, i):
        return jnp.concatenate([ids[pl.ds(i * (T // 128) + n, 1), :] for n in range(T // 128)], axis=1)

    def token_major(t, row, which):
        one = jnp.where(lane_doc == row, 1.0, 0.0).astype(BF16).T
        for p in which:
            kx[p, t, :, :2 * HD] = kt[t, p * 2 * HD:(p + 1) * 2 * HD, :].T
            kx[p, t, :, 2 * HD:] = one
            vx[p, t] = vt[t, p * 2 * HD:(p + 1) * 2 * HD, :].T

    def project(i):
        at = rows(i * T, T, T)
        projected = lax.dot_general(wt[...], acts[at, :], NT, preferred_element_type=F32).astype(BF16)
        gt[i] = lax.dot_general(owt[...], og[at, :], NT, preferred_element_type=F32).astype(BF16)
        cos, sin = cos_ref[i], sin_ref[i]

        def rope(u):
            u = u.astype(F32)
            low, high = u[:HALF], u[HALF:]
            return jnp.concatenate([low * cos - high * sin, high * cos + low * sin], axis=0).astype(BF16)

        for h in range(heads):
            to = slice(h * HD, (h + 1) * HD)
            base = h * 3 * HD
            qt[i, to, :] = rope(projected[base:base + HD]) * BF16(HD ** -0.5)
            kt[i + RIM, to, :] = rope(projected[base + HD:base + 2 * HD])
            vt[i + RIM, to, :] = projected[base + 2 * HD:base + 3 * HD]
        row = doc_row(seg, i)
        pen[i] = jnp.where(lane_doc == row, 0.0, LOW).astype(BF16)
        token_major(i + RIM, row, range(pairs))

    @pl.loop(0, nb)
    def _(j):
        for copy in load_tile(early(j)):
            copy.wait()
        project(early(j))

        @pl.when(j == 2 * RIM - 1)
        def _():
            pl.semaphore_wait(barrier, nx + nz - 1)

            @pl.when(has_high)
            def _():
                seg_up().start()
                for p in range(pairs):
                    halo_up(kt, 0, p).start()
                    halo_up(vt, 1, p).start()

            @pl.when(has_low)
            def _():
                seg_down().start()
                for p in range(pairs):
                    halo_down(kt, 0, p).start()
                    halo_down(vt, 1, p).start()

    r = lax.broadcasted_iota(jnp.int32, (T, T), 0)
    c = lax.broadcasted_iota(jnp.int32, (T, T), 1)
    tri[0] = jnp.where(r >= c, 0.0, LOW).astype(F32)
    tri[1] = jnp.where(r <= c, 0.0, LOW).astype(F32)

    @pl.loop(0, nb + 2 * RIM)
    def _(t):
        dk[t] = jnp.zeros_like(dk[t])
        dv[t] = jnp.zeros_like(dv[t])

    def fill(a, first):
        a[first:first + RIM] = jnp.zeros((RIM, width, T), BF16)

    @pl.when(z == 0)
    def _():
        fill(kt, 0)
        fill(vt, 0)
        seg_low[...] = jnp.full_like(seg_low, OUTSIDE)

    @pl.when(z == nz - 1)
    def _():
        fill(kt, nb + RIM)
        fill(vt, nb + RIM)
        seg_high[...] = jnp.full_like(seg_high, OUTSIDE)

    def halo_arrive(p):
        @pl.when(has_low)
        def _():
            if p == 0:
                seg_up().wait_recv()
            halo_up(kt, 0, p).wait_recv()
            halo_up(vt, 1, p).wait_recv()

        @pl.when(has_high)
        def _():
            if p == 0:
                seg_down().wait_recv()
            halo_down(kt, 0, p).wait_recv()
            halo_down(vt, 1, p).wait_recv()

        for t in range(RIM):
            token_major(t, doc_row(seg_low, nb - RIM + t), [p])
            token_major(nb + RIM + t, doc_row(seg_high, t), [p])

    zero = jnp.zeros((HD, T), BF16)

    def place(h, block, rest):
        return jnp.concatenate(([block, zero] if h == 0 else [zero, block]) + rest, axis=0)

    def feature(p, h):
        return rows(p * 2 * HD + h * HD, HD, HD)

    def block(p, i):
        top, scale, delta = [None] * 2, [None] * 2, [None] * 2
        ats = [feature(p, h) for h in range(2)]

        def score(h):
            rhs = place(h, qt[i, ats[h], :], [pen[i]])
            high = None
            for t in range(SPAN):
                s = dot(kx[p, i + t], rhs)
                if t == 0:
                    s = s + tri[0]
                if t == SPAN - 1:
                    s = s + tri[1]
                s_ref[h, t] = s
                best = jnp.max(s.reshape(T // 8, 8, T), axis=0)
                high = best if high is None else jnp.maximum(high, best)
                yield
            top[h] = jnp.max(high, axis=0, keepdims=True)

        def soft(h):
            total = jnp.zeros((8, T), F32)
            for t in range(SPAN):
                e = jnp.exp(s_ref[h, t] - top[h])
                total = total + jnp.sum(e.reshape(T // 8, 8, T), axis=0)
                p_ref[h, t] = e.astype(BF16)
                yield
            scale[h] = 1.0 / jnp.sum(total, axis=0, keepdims=True)

        def attend(h):
            out = jnp.zeros((HD, T), F32)
            for t in range(SPAN):
                out = out + dot(vt[i + t, ats[h], :], p_ref[h, t])
                yield
            out = (out * scale[h]).astype(BF16)
            att[ats[h], rows(i * T, T, T)] = out
            delta[h] = jnp.sum(out.astype(F32) * gt[i, ats[h], :].astype(F32), axis=0, keepdims=True)

        def score_grad(h):
            rhs = place(h, gt[i, ats[h], :], [])
            for t in range(SPAN):
                back = dot(vx[p, i + t], rhs)
                ds_ref[h, t] = (p_ref[h, t].astype(F32) * (back - delta[h])).astype(BF16)
                yield

        def query_grad(h):
            out = jnp.zeros((HD, T), F32)
            for t in range(SPAN):
                out = out + dot(kt[i + t, ats[h], :], ds_ref[h, t])
                yield
            out = out * (scale[h] * HD ** -0.5)
            grad[rows((2 * p + h) * 3 * HD, HD, HD), rows(i * T, T, T)] = unrope(out, i)

        def value_grad(h):
            g = (gt[i, ats[h], :].astype(F32) * scale[h]).astype(BF16)
            for t in range(SPAN):
                dv[i + t, ats[h], :] += lax.dot_general(g, p_ref[h, t], NT, preferred_element_type=F32)
                yield

        def key_grad(h):
            q = (qt[i, ats[h], :].astype(F32) * scale[h]).astype(BF16)
            for t in range(SPAN):
                dk[i + t, ats[h], :] += lax.dot_general(q, ds_ref[h, t], NT, preferred_element_type=F32)
                yield

        def run(*stages):
            for _ in itertools.zip_longest(*stages):
                pass

        run(score(0))
        run(score(1))
        run(soft(0))
        run(attend(0))
        run(soft(1), value_grad(0))
        run(attend(1))
        run(score_grad(0), value_grad(1))
        run(score_grad(1))
        run(query_grad(0))
        run(key_grad(0))
        run(query_grad(1))
        run(key_grad(1))

    def unrope(u, i):
        cos, sin = cos_ref[i], sin_ref[i]
        low, high = u[:HALF], u[HALF:]
        return jnp.concatenate([low * cos + high * sin, high * cos - low * sin], axis=0).astype(BF16)

    def rim_out(p, side, first):
        at = rows(p * 2 * HD, 2 * HD, 2 * HD)
        for t in range(RIM):
            rim_send[p, side, 0, t] = dk[first + t, at, :].astype(BF16)
            rim_send[p, side, 1, t] = dv[first + t, at, :].astype(BF16)

    def rim_in(p, side, first):
        at = rows(p * 2 * HD, 2 * HD, 2 * HD)
        for t in range(RIM):
            dk[first + t, at, :] += rim_recv[p, side, 0, t].astype(F32)
            dv[first + t, at, :] += rim_recv[p, side, 1, t].astype(F32)

    def low_in(p):
        rim_up(p).wait_recv()
        rim_in(p, 0, RIM)

    def high_in(p):
        rim_down(p).wait_recv()
        rim_in(p, 1, nb)

    def finish(p, i):
        to = rows(i * T, T, T)
        for h in range(2):
            base = (2 * p + h) * 3 * HD
            grad[rows(base + HD, HD, HD), to] = unrope(dk[i + RIM, feature(p, h), :], i)
            grad[rows(base + 2 * HD, HD, HD), to] = dv[i + RIM, feature(p, h), :].astype(BF16)

    def weight_grads(p, sub):
        c = 2 * p + sub
        order = []
        for n in range(nz):
            order.append(nz - 1 - n // 2 if n % 2 == 0 else n // 2)
        for d in order:
            to = slice(d * share, (d + 1) * share)
            for h in range(2):
                base = (2 * p + h) * 3 * HD
                if sub == 0:
                    part[c, d, h * HD:(h + 1) * HD, :] = dot(grad[rows(base, HD, HD), :], acts[:, to]).astype(BF16)
                else:
                    part[c, d, 2 * h * HD:2 * (h + 1) * HD, :] = dot(
                        grad[rows(base + HD, 2 * HD, HD), :], acts[:, to]).astype(BF16)
            if sub == 0:
                part[c, d, 2 * HD:, :] = dot(att[rows(p * 2 * HD, 2 * HD, 2 * HD), :], og[:, to]).astype(BF16)
            if d > 0:
                @pl.when(z == 0)
                def _():
                    right(c, d).start()
            if d < nz - 1:
                @pl.when(z == nz - 1)
                def _():
                    left(c, d).start()

    def hop(c, n):
        up = z + nz - 1 - n
        down = n - (nz - 1 - z)

        @pl.when(has_low & (up < nz))
        def _():
            right(c, up).wait_recv()
            part[c, up] = (part[c, up].astype(F32) + recv[c, up + 1].astype(F32)).astype(BF16)
            right(c, up).start()

        @pl.when(has_high & (down >= 0))
        def _():
            left(c, down).wait_recv()
            part[c, down] = (part[c, down].astype(F32) + recv[c, down].astype(F32)).astype(BF16)
            left(c, down).start()

    def land(p, sub):
        c = 2 * p + sub

        def put(value):
            for h in range(2):
                base = (2 * p + h) * 3 * HD
                if sub == 0:
                    sums[rows(base, HD, HD), :] = value[h * HD:(h + 1) * HD]
                else:
                    sums[rows(base + HD, 2 * HD, HD), :] = value[2 * h * HD:2 * (h + 1) * HD]
            if sub == 0:
                sums[rows(3 * width + p * 2 * HD, 2 * HD, 2 * HD), :] = value[2 * HD:]

        @pl.when(z == 0)
        def _():
            left(c, z).wait_recv()
            put(part[c, z].astype(F32) + recv[c, z].astype(F32))

        @pl.when(z == nz - 1)
        def _():
            right(c, z).wait_recv()
            put(part[c, z].astype(F32) + recv[c, z + 1].astype(F32))

        @pl.when(has_low & has_high)
        def _():
            right(c, z).wait_recv()
            left(c, z).wait_recv()
            put(part[c, z].astype(F32) + recv[c, z].astype(F32) + recv[c, z + 1].astype(F32))

    odd = z % 2 == 1
    last = pairs - 1

    def tile(m):
        return jnp.where(odd, m, nb - 1 - m)

    def produce(m):
        to = rows(tile(m) * T, T, T)
        for k in list(range(1, nx)) + [0]:
            there = ((x + k) % nx) * 2
            at = rows((there + 1 - core) * cols, cols, cols)
            send1[k, m] = dot(w[at, :], grad[:, to]).astype(BF16)
            swap(k, m).start()
        for k in list(range(1, nx)) + [0]:
            there = ((x + k) % nx) * 2
            at = rows((there + core) * cols, cols, cols)
            own[k, m] = dot(w[at, :], grad[:, to]).astype(BF16)

    def forward(m):
        for k in range(1, nx):
            swap(k, m).wait_recv()
            recv1[k, m] = (own[k, m].astype(F32) + recv1[k, m].astype(F32)).astype(BF16)
            cross(k, m).start()

    def deliver(m):
        swap(0, m).wait_recv()
        value = own[0, m].astype(F32) + recv1[0, m].astype(F32)
        for k in range(1, nx):
            cross(k, m).wait_recv()
            value = value + recv2[k, m].astype(F32)
        in_held[rows(tile(m) * T, T, T), :] = value.astype(BF16).T

    if pairs > 1:
        plan = [(0, 2), (0, 3), (0, 4), (0, 0), (0, 1), (0, nb - 2), (0, nb - 1), (1, 0), (1, 1)]
        plan = plan + [(0, i) for i in range(5, nb - 2)] + [(1, m) for m in range(2, nb)]
    else:
        plan = [(0, m) for m in range(nb)]

    def after(p, i):
        return plan.index((p, i))

    first_end = after(0, nb - 3) if pairs > 1 else None

    @pl.loop(0, len(plan))
    def _(n):
        p, i = jnp.int32(plan[0][0]), jnp.int32(plan[0][1])
        for k, (pair, at_block) in enumerate(plan[1:], 1):
            p = jnp.where(n == k, pair, p)
            i = jnp.where(n == k, at_block, i)
        i = jnp.where(p == last, tile(i), i)

        for q in range(pairs):
            @pl.when(n == (after(q, 0) if q == last else 3))
            def _():
                halo_arrive(q)

        block(p, i)

        if pairs > 1:
            @pl.when((n == after(0, 1)) & has_low)
            def _():
                rim_out(0, 1, 0)
                rim_down(0).start()

            @pl.when((n == after(0, nb - 1)) & has_high)
            def _():
                rim_out(0, 0, nb + RIM)
                rim_up(0).start()

            @pl.when(n == first_end)
            def _():
                @pl.when(has_low)
                def _():
                    low_in(0)

                @pl.when(has_high)
                def _():
                    high_in(0)

                @pl.loop(0, nb)
                def _(t):
                    finish(0, t)

                weight_grads(0, 0)
                weight_grads(0, 1)

            for m in range(1, nz - 1):
                @pl.when(n == after(1, min(2 * m, nb - 1)))
                def _():
                    hop(0, m)

            for m in range(1, nz - 1):
                @pl.when(n == after(1, min(3 + 2 * m, nb - 1)))
                def _():
                    hop(1, m)

        low_at = jnp.where(odd, after(last, 1), after(last, nb - 1))
        high_at = jnp.where(odd, after(last, nb - 1), after(last, 1))

        @pl.when((n == low_at) & has_low)
        def _():
            rim_out(last, 1, 0)
            rim_down(last).start()

        @pl.when((n == high_at) & has_high)
        def _():
            rim_out(last, 0, nb + RIM)
            rim_up(last).start()

        @pl.when(n == after(last, 2))
        def _():
            @pl.when(odd)
            def _():
                low_in(last)

            @pl.when(jnp.logical_not(odd) & has_high)
            def _():
                high_in(last)

        @pl.when((n >= after(last, 2)) & (n < after(last, 2) + EARLY))
        def _():
            m = n - after(last, 2)
            finish(last, tile(m))
            produce(m)
            forward(m)

    def put_out(p):
        to = slice(p * 6 * HD, (p + 1) * 6 * HD)
        qkv_out[:, to] = sums[to, :].T
        ow_out[:, p * 2 * HD:(p + 1) * 2 * HD] = sums[3 * width + p * 2 * HD:3 * width + (p + 1) * 2 * HD, :].T

    weight_grads(last, 0)

    @pl.loop(EARLY, nb - 2)
    def _(m):
        finish(last, tile(m))
        produce(m)
        forward(m)

    if nz > 2:
        hop(2 * last, 1)

    @pl.when(odd & has_high)
    def _():
        high_in(last)

    @pl.when(jnp.logical_not(odd) & has_low)
    def _():
        low_in(last)

    for m in (nb - 2, nb - 1):
        finish(last, tile(m))
    weight_grads(last, 1)
    for m in range(2, nz - 1):
        hop(2 * last, m)
    for m in (nb - 2, nb - 1):
        produce(m)
    for m in (nb - 2, nb - 1):
        forward(m)
    if nz > 2:
        hop(2 * last + 1, 1)
    if pairs > 1:
        land(0, 0)
        land(0, 1)
        put_out(0)
    for m in range(2, nz - 1):
        hop(2 * last + 1, m)
    land(last, 0)

    @pl.loop(0, nb)
    def _(m):
        deliver(m)

    result = pltpu.make_async_copy(in_held, in_out, in_sem)
    result.start()
    land(last, 1)
    put_out(last)
    result.wait()

    @pl.when(has_high)
    def _():
        seg_up().wait_send()
        for p in range(pairs):
            halo_up(kt, 0, p).wait_send()
            halo_up(vt, 1, p).wait_send()
            rim_up(p).wait_send()

    @pl.when(has_low)
    def _():
        seg_down().wait_send()
        for p in range(pairs):
            halo_down(kt, 0, p).wait_send()
            halo_down(vt, 1, p).wait_send()
            rim_down(p).wait_send()

    for c in range(2 * pairs):
        for d in range(nz):
            if d > 0:
                @pl.when(z < d)
                def _():
                    right(c, d).wait_send()
            if d < nz - 1:
                @pl.when(z > d)
                def _():
                    left(c, d).wait_send()
    for k in range(nx):
        for m in range(nb):
            swap(k, m).wait_send()
            if k > 0:
                cross(k, m).wait_send()


def hand_over_kernel(count, *refs):
    sources, targets, held = refs[:count], refs[count:2 * count], refs[2 * count:3 * count]
    sems = refs[3 * count]
    into, out = [], []
    for source, target, hold in zip(sources, targets, held):
        size = source.shape[0] // PIECES
        for n in range(PIECES):
            at = pl.ds(n * size, size)
            into.append(pltpu.make_async_copy(source.at[at], hold.at[at], sems.at[0, len(into)]))
            out.append(pltpu.make_async_copy(hold.at[at], target.at[at], sems.at[1, len(out)]))
    for copy in into:
        copy.start()
    for first, second in zip(into, out):
        first.wait()
        second.start()
    for copy in out:
        copy.wait()


def hand_over(arrays):
    anywhere = pl.BlockSpec(memory_space=pl.ANY)
    return pl.pallas_call(
        functools.partial(hand_over_kernel, len(arrays)),
        in_specs=[anywhere] * len(arrays),
        out_specs=[anywhere] * len(arrays),
        out_shape=[jax.ShapeDtypeStruct(a.shape, a.dtype) for a in arrays],
        scratch_shapes=[pltpu.VMEM(a.shape, a.dtype) for a in arrays]
        + [pltpu.SemaphoreType.DMA((2, len(arrays) * PIECES))],
        compiler_params=pltpu.CompilerParams(vmem_limit_bytes=60 * 1024 * 1024),
    )(*arrays)


def local(activations, out_grad, segment_ids, qkv_weight, out_weight):
    tokens, model = activations.shape
    columns = qkv_weight.shape[1]
    width = columns // 3
    pairs = width // (2 * HD)
    nb = tokens // T
    nt = nb + 2 * RIM
    nz = lax.axis_size("ctx")
    nx = lax.axis_size("head") // 2
    cols = model // (2 * nx)
    share = model // nz
    position = np.arange(nz * tokens, dtype=np.float32)
    exponent = np.arange(HALF, dtype=np.float32) * np.float32(2.0 / HD)
    inverse = np.power(np.float32(10000.0), -exponent).astype(np.float32)
    angles = (inverse[None, :, None] * position.reshape(nz * nb, 1, T)).astype(np.float64)
    cos, sin = jnp.asarray(np.cos(angles), F32), jnp.asarray(np.sin(angles), F32)
    vmem = pl.BlockSpec(memory_space=pltpu.VMEM)
    dma = pltpu.SemaphoreType.DMA
    v = pltpu.VMEM
    out = pl.pallas_call(
        functools.partial(layer_kernel, nx, nz),
        in_specs=[pl.BlockSpec(memory_space=pl.ANY)] * 7,
        out_specs=[pl.BlockSpec(memory_space=pl.ANY), vmem, vmem],
        out_shape=[
            jax.ShapeDtypeStruct((tokens, cols), BF16),
            jax.ShapeDtypeStruct((share, columns), F32),
            jax.ShapeDtypeStruct((share, width), F32),
        ],
        scratch_shapes=[
            v((tokens, cols), BF16), dma(()),
            v((tokens, model), BF16), v((tokens, model), BF16), v((tokens // 128, 128), jnp.int32),
            v((model, columns), BF16), v((model, width), BF16), v((nb, HALF, T), F32), v((nb, HALF, T), F32),
            dma((nb,)), dma((nb,)), dma((5,)),
            v((columns, model), BF16), v((width, model), BF16),
            v((nt, width, T), BF16), v((nt, width, T), BF16),
            v((pairs, nt, T, 2 * HD + 128), BF16), v((pairs, nt, T, 2 * HD), BF16),
            v((nb, width, T), BF16), v((nb, width, T), BF16),
            v((nb, 128, T), BF16), v((tokens // 128, 128), jnp.int32), v((tokens // 128, 128), jnp.int32), v((2, T, T), F32),
            v((2, SPAN, T, T), F32), v((2, SPAN, T, T), BF16), v((2, SPAN, T, T), BF16),
            v((nt, width, T), F32), v((nt, width, T), F32),
            v((columns, tokens), BF16), v((width, tokens), BF16),
            v((pairs, 2, 2, RIM, 2 * HD, T), BF16), v((pairs, 2, 2, RIM, 2 * HD, T), BF16),
            v((2 * pairs, nz, 4 * HD, share), BF16), v((2 * pairs, nz + 1, 4 * HD, share), BF16),
            v((4 * width, share), F32),
            v((nx, nb, cols, T), BF16), v((nx, nb, cols, T), BF16),
            v((nx, nb, cols, T), BF16), v((nx, nb, cols, T), BF16),
            dma((2, 2, pairs)), dma((2, 2, pairs)), dma((2,)), dma((2,)), dma((pairs, 2)), dma((pairs, 2)),
            dma((2 * pairs, nz)), dma((2 * pairs, nz)), dma((2 * pairs, nz)), dma((2 * pairs, nz)),
            dma((nx, nb)), dma((nx, nb)), dma((nx, nb)), dma((nx, nb)),
        ],
        compiler_params=pltpu.CompilerParams(
            collective_id=0, has_side_effects=True, vmem_limit_bytes=60 * 1024 * 1024
        ),
        cost_estimate=pl.CostEstimate(
            flops=12 * tokens * SPAN * T * width + 16 * tokens * model * width,
            bytes_accessed=8 * tokens * model, transcendentals=tokens * SPAN * T * width // HD
        ),
    )(activations, out_grad, segment_ids.reshape(tokens // 128, 128), qkv_weight, out_weight, cos, sin)
    return hand_over(out)


def solution(mesh):
    in_specs = (
        P(("groups", "ctx"), None),
        P(("groups", "ctx"), None),
        P(("groups", "ctx")),
        P(None, "head"),
        P(None, "head"),
    )
    out_specs = (
        P(("groups", "ctx"), "head"),
        P(("groups", "ctx"), "head"),
        P(("groups", "ctx"), "head"),
    )
    return jax.shard_map(local, mesh=mesh, in_specs=in_specs, out_specs=out_specs, check_vma=False)
```

```python
import functools
import itertools

import jax
import jax.numpy as jnp
import numpy as np
from jax import lax
from jax.experimental import pallas as pl
from jax.experimental.pallas import tpu as pltpu
from jax.sharding import PartitionSpec as P

HD = 64
HALF = HD // 2
WIN = 512
T = 256
RIM = WIN // T
SPAN = 2 * RIM + 1
LOW = -1e30
OUTSIDE = 127
PIECES = 2
EARLY = 3
NT = (((1,), (1,)), ((), ()))
F32 = jnp.float32
BF16 = jnp.bfloat16
MESH = pl.DeviceIdType.MESH


def dot(a, b):
    return jnp.dot(a, b, preferred_element_type=F32)


def layer_kernel(nx, nz, acts_in, og_in, seg_in, w_in, ow_in, cos_in, sin_in,
                 in_out, qkv_out, ow_out,
                 in_held, in_sem, acts, og, seg, w, ow, cos_ref, sin_ref, acts_ls, og_ls, load_ls, wt, owt, kt, vt, kx, vx, qt, gt, pen, seg_low, seg_high, tri,
                 s_ref, p_ref, ds_ref, dk, dv, grad, att,
                 rim_send, rim_recv, part, recv, sums, send1, own, recv1, recv2,
                 halo_ss, halo_rs, seg_ss, seg_rs, rim_ss, rim_rs,
                 right_ss, right_rs, left_ss, left_rs, swap_ss, swap_rs, cross_ss, cross_rs):
    tokens, model = acts.shape
    width = ow.shape[1]
    heads = width // HD
    pairs = heads // 2
    nb = tokens // T
    cols = model // (2 * nx)
    share = model // nz
    head = lax.axis_index("head")
    z = lax.axis_index("ctx")
    x, core = head // 2, head % 2
    sibling = x * 2 + (1 - core)
    has_low, has_high = z > 0, z < nz - 1
    above = {"ctx": jnp.minimum(z + 1, nz - 1)}
    below = {"ctx": jnp.maximum(z - 1, 0)}

    def loads():
        here = pl.ds(z * nb, nb)
        pairs_of = ((w_in, w), (ow_in, ow), (cos_in.at[here], cos_ref), (sin_in.at[here], sin_ref), (seg_in, seg))
        return [pltpu.make_async_copy(src, dst, load_ls.at[n]) for n, (src, dst) in enumerate(pairs_of)]

    def load_tile(i):
        at = pl.ds(pl.multiple_of(i * T, T), T)
        return (pltpu.make_async_copy(acts_in.at[at], acts.at[at], acts_ls.at[i]),
                pltpu.make_async_copy(og_in.at[at], og.at[at], og_ls.at[i]))

    def early(j):
        return jnp.where(j < RIM, j, jnp.where(j < 2 * RIM, nb - 2 * RIM + j, j - RIM))

    for copy in loads():
        copy.start()
    for j in range(nb):
        for copy in load_tile(early(j)):
            copy.start()

    barrier = pltpu.get_barrier_semaphore()
    pl.semaphore_signal(barrier, inc=1, device_id={"head": sibling}, device_id_type=MESH)
    for k in range(1, nx):
        peer = ((x + k) % nx) * 2 + core
        pl.semaphore_signal(barrier, inc=1, device_id={"head": peer}, device_id_type=MESH)
    for k in range(1, nz):
        pl.semaphore_signal(barrier, inc=1, device_id={"ctx": (z + k) % nz}, device_id_type=MESH)

    def remote(src, dst, ss, rs, device):
        return pltpu.make_async_remote_copy(src_ref=src, dst_ref=dst, send_sem=ss, recv_sem=rs,
                                            device_id=device, device_id_type=MESH)

    def halo_up(a, n, p):
        at = pl.ds(p * 2 * HD, 2 * HD)
        return remote(a.at[pl.ds(nb, RIM), at], a.at[pl.ds(0, RIM), at], halo_ss.at[0, n, p], halo_rs.at[0, n, p], above)

    def halo_down(a, n, p):
        at = pl.ds(p * 2 * HD, 2 * HD)
        return remote(a.at[pl.ds(RIM, RIM), at], a.at[pl.ds(nb + RIM, RIM), at],
                      halo_ss.at[1, n, p], halo_rs.at[1, n, p], below)

    def seg_up():
        return remote(seg, seg_low, seg_ss.at[0], seg_rs.at[0], above)

    def seg_down():
        return remote(seg, seg_high, seg_ss.at[1], seg_rs.at[1], below)

    def rim_up(p):
        return remote(rim_send.at[p, 0], rim_recv.at[p, 0], rim_ss.at[p, 0], rim_rs.at[p, 0], above)

    def rim_down(p):
        return remote(rim_send.at[p, 1], rim_recv.at[p, 1], rim_ss.at[p, 1], rim_rs.at[p, 1], below)

    def right(c, d):
        return remote(part.at[c, d], recv.at[c, d + 1], right_ss.at[c, d], right_rs.at[c, d], above)

    def left(c, d):
        return remote(part.at[c, d], recv.at[c, d], left_ss.at[c, d], left_rs.at[c, d], below)

    def swap(k, r):
        return remote(send1.at[k, r], recv1.at[k, r], swap_ss.at[k, r], swap_rs.at[k, r], {"head": sibling})

    def cross(k, r):
        return remote(recv1.at[k, r], recv2.at[k, r], cross_ss.at[k, r], cross_rs.at[k, r],
                      {"head": ((x + k) % nx) * 2 + core})

    def rows(start, size, unit):
        return pl.ds(pl.multiple_of(start, unit), size)

    for copy in loads():
        copy.wait()

    @pl.loop(0, model // T)
    def _(c):
        at = rows(c * T, T, T)
        wt[:, at] = w[at, :].T
        owt[:, at] = ow[at, :].T

    lane_doc = lax.broadcasted_iota(jnp.int32, (128, T), 0)

    def doc_row(ids, i):
        return jnp.concatenate([ids[pl.ds(i * (T // 128) + n, 1), :] for n in range(T // 128)], axis=1)

    def token_major(t, row, which):
        one = jnp.where(lane_doc == row, 1.0, 0.0).astype(BF16).T
        for p in which:
            kx[p, t, :, :2 * HD] = kt[t, p * 2 * HD:(p + 1) * 2 * HD, :].T
            kx[p, t, :, 2 * HD:] = one
            vx[p, t] = vt[t, p * 2 * HD:(p + 1) * 2 * HD, :].T

    def project(i):
        at = rows(i * T, T, T)
        projected = lax.dot_general(wt[...], acts[at, :], NT, preferred_element_type=F32).astype(BF16)
        gt[i] = lax.dot_general(owt[...], og[at, :], NT, preferred_element_type=F32).astype(BF16)
        cos, sin = cos_ref[i], sin_ref[i]

        def rope(u):
            u = u.astype(F32)
            low, high = u[:HALF], u[HALF:]
            return jnp.concatenate([low * cos - high * sin, high * cos + low * sin], axis=0).astype(BF16)

        for h in range(heads):
            to = slice(h * HD, (h + 1) * HD)
            base = h * 3 * HD
            qt[i, to, :] = rope(projected[base:base + HD]) * BF16(HD ** -0.5)
            kt[i + RIM, to, :] = rope(projected[base + HD:base + 2 * HD])
            vt[i + RIM, to, :] = projected[base + 2 * HD:base + 3 * HD]
        row = doc_row(seg, i)
        pen[i] = jnp.where(lane_doc == row, 0.0, LOW).astype(BF16)
        token_major(i + RIM, row, range(pairs))

    @pl.loop(0, nb)
    def _(j):
        for copy in load_tile(early(j)):
            copy.wait()
        project(early(j))

        @pl.when(j == 2 * RIM - 1)
        def _():
            pl.semaphore_wait(barrier, nx + nz - 1)

            @pl.when(has_high)
            def _():
                seg_up().start()
                for p in range(pairs):
                    halo_up(kt, 0, p).start()
                    halo_up(vt, 1, p).start()

            @pl.when(has_low)
            def _():
                seg_down().start()
                for p in range(pairs):
                    halo_down(kt, 0, p).start()
                    halo_down(vt, 1, p).start()

    r = lax.broadcasted_iota(jnp.int32, (T, T), 0)
    c = lax.broadcasted_iota(jnp.int32, (T, T), 1)
    tri[0] = jnp.where(r >= c, 0.0, LOW).astype(F32)
    tri[1] = jnp.where(r <= c, 0.0, LOW).astype(F32)

    @pl.loop(0, nb + 2 * RIM)
    def _(t):
        dk[t] = jnp.zeros_like(dk[t])
        dv[t] = jnp.zeros_like(dv[t])

    def fill(a, first):
        a[first:first + RIM] = jnp.zeros((RIM, width, T), BF16)

    @pl.when(z == 0)
    def _():
        fill(kt, 0)
        fill(vt, 0)
        seg_low[...] = jnp.full_like(seg_low, OUTSIDE)

    @pl.when(z == nz - 1)
    def _():
        fill(kt, nb + RIM)
        fill(vt, nb + RIM)
        seg_high[...] = jnp.full_like(seg_high, OUTSIDE)

    def halo_arrive(p):
        @pl.when(has_low)
        def _():
            if p == 0:
                seg_up().wait_recv()
            halo_up(kt, 0, p).wait_recv()
            halo_up(vt, 1, p).wait_recv()

        @pl.when(has_high)
        def _():
            if p == 0:
                seg_down().wait_recv()
            halo_down(kt, 0, p).wait_recv()
            halo_down(vt, 1, p).wait_recv()

        for t in range(RIM):
            token_major(t, doc_row(seg_low, nb - RIM + t), [p])
            token_major(nb + RIM + t, doc_row(seg_high, t), [p])

    zero = jnp.zeros((HD, T), BF16)

    def place(h, block, rest):
        return jnp.concatenate(([block, zero] if h == 0 else [zero, block]) + rest, axis=0)

    def feature(p, h):
        return rows(p * 2 * HD + h * HD, HD, HD)

    def block(p, i):
        top, scale, delta = [None] * 2, [None] * 2, [None] * 2
        ats = [feature(p, h) for h in range(2)]

        def score(h):
            rhs = place(h, qt[i, ats[h], :], [pen[i]])
            high = None
            for t in range(SPAN):
                s = dot(kx[p, i + t], rhs)
                if t == 0:
                    s = s + tri[0]
                if t == SPAN - 1:
                    s = s + tri[1]
                s_ref[h, t] = s
                best = jnp.max(s.reshape(T // 8, 8, T), axis=0)
                high = best if high is None else jnp.maximum(high, best)
                yield
            top[h] = jnp.max(high, axis=0, keepdims=True)

        def soft(h):
            total = jnp.zeros((8, T), F32)
            for t in range(SPAN):
                e = jnp.exp(s_ref[h, t] - top[h])
                total = total + jnp.sum(e.reshape(T // 8, 8, T), axis=0)
                p_ref[h, t] = e.astype(BF16)
                yield
            scale[h] = 1.0 / jnp.sum(total, axis=0, keepdims=True)

        def attend(h):
            out = jnp.zeros((HD, T), F32)
            for t in range(SPAN):
                out = out + dot(vt[i + t, ats[h], :], p_ref[h, t])
                yield
            out = (out * scale[h]).astype(BF16)
            att[ats[h], rows(i * T, T, T)] = out
            delta[h] = jnp.sum(out.astype(F32) * gt[i, ats[h], :].astype(F32), axis=0, keepdims=True)

        def score_grad(h):
            rhs = place(h, gt[i, ats[h], :], [])
            for t in range(SPAN):
                back = dot(vx[p, i + t], rhs)
                ds_ref[h, t] = (p_ref[h, t].astype(F32) * (back - delta[h])).astype(BF16)
                yield

        def query_grad(h):
            out = jnp.zeros((HD, T), F32)
            for t in range(SPAN):
                out = out + dot(kt[i + t, ats[h], :], ds_ref[h, t])
                yield
            out = out * (scale[h] * HD ** -0.5)
            grad[rows((2 * p + h) * 3 * HD, HD, HD), rows(i * T, T, T)] = unrope(out, i)

        def value_grad(h):
            g = (gt[i, ats[h], :].astype(F32) * scale[h]).astype(BF16)
            for t in range(SPAN):
                dv[i + t, ats[h], :] += lax.dot_general(g, p_ref[h, t], NT, preferred_element_type=F32)
                yield

        def key_grad(h):
            q = (qt[i, ats[h], :].astype(F32) * scale[h]).astype(BF16)
            for t in range(SPAN):
                dk[i + t, ats[h], :] += lax.dot_general(q, ds_ref[h, t], NT, preferred_element_type=F32)
                yield

        def run(*stages):
            for _ in itertools.zip_longest(*stages):
                pass

        run(score(0))
        run(score(1))
        run(soft(0))
        run(attend(0))
        run(soft(1), value_grad(0))
        run(attend(1))
        run(score_grad(0), value_grad(1))
        run(score_grad(1))
        run(query_grad(0))
        run(key_grad(0))
        run(query_grad(1))
        run(key_grad(1))

    def unrope(u, i):
        cos, sin = cos_ref[i], sin_ref[i]
        low, high = u[:HALF], u[HALF:]
        return jnp.concatenate([low * cos + high * sin, high * cos - low * sin], axis=0).astype(BF16)

    def rim_out(p, side, first):
        at = rows(p * 2 * HD, 2 * HD, 2 * HD)
        for t in range(RIM):
            rim_send[p, side, 0, t] = dk[first + t, at, :].astype(BF16)
            rim_send[p, side, 1, t] = dv[first + t, at, :].astype(BF16)

    def rim_in(p, side, first):
        at = rows(p * 2 * HD, 2 * HD, 2 * HD)
        for t in range(RIM):
            dk[first + t, at, :] += rim_recv[p, side, 0, t].astype(F32)
            dv[first + t, at, :] += rim_recv[p, side, 1, t].astype(F32)

    def low_in(p):
        rim_up(p).wait_recv()
        rim_in(p, 0, RIM)

    def high_in(p):
        rim_down(p).wait_recv()
        rim_in(p, 1, nb)

    def finish(p, i):
        to = rows(i * T, T, T)
        for h in range(2):
            base = (2 * p + h) * 3 * HD
            grad[rows(base + HD, HD, HD), to] = unrope(dk[i + RIM, feature(p, h), :], i)
            grad[rows(base + 2 * HD, HD, HD), to] = dv[i + RIM, feature(p, h), :].astype(BF16)

    def weight_grads(p, sub):
        c = 2 * p + sub
        order = []
        for n in range(nz):
            order.append(nz - 1 - n // 2 if n % 2 == 0 else n // 2)
        for d in order:
            to = slice(d * share, (d + 1) * share)
            for h in range(2):
                base = (2 * p + h) * 3 * HD
                if sub == 0:
                    part[c, d, h * HD:(h + 1) * HD, :] = dot(grad[rows(base, HD, HD), :], acts[:, to]).astype(BF16)
                else:
                    part[c, d, 2 * h * HD:2 * (h + 1) * HD, :] = dot(
                        grad[rows(base + HD, 2 * HD, HD), :], acts[:, to]).astype(BF16)
            if sub == 0:
                part[c, d, 2 * HD:, :] = dot(att[rows(p * 2 * HD, 2 * HD, 2 * HD), :], og[:, to]).astype(BF16)
            if d > 0:
                @pl.when(z == 0)
                def _():
                    right(c, d).start()
            if d < nz - 1:
                @pl.when(z == nz - 1)
                def _():
                    left(c, d).start()

    def hop(c, n):
        up = z + nz - 1 - n
        down = n - (nz - 1 - z)

        @pl.when(has_low & (up < nz))
        def _():
            right(c, up).wait_recv()
            part[c, up] = (part[c, up].astype(F32) + recv[c, up + 1].astype(F32)).astype(BF16)
            right(c, up).start()

        @pl.when(has_high & (down >= 0))
        def _():
            left(c, down).wait_recv()
            part[c, down] = (part[c, down].astype(F32) + recv[c, down].astype(F32)).astype(BF16)
            left(c, down).start()

    def land(p, sub):
        c = 2 * p + sub

        def put(value):
            for h in range(2):
                base = (2 * p + h) * 3 * HD
                if sub == 0:
                    sums[rows(base, HD, HD), :] = value[h * HD:(h + 1) * HD]
                else:
                    sums[rows(base + HD, 2 * HD, HD), :] = value[2 * h * HD:2 * (h + 1) * HD]
            if sub == 0:
                sums[rows(3 * width + p * 2 * HD, 2 * HD, 2 * HD), :] = value[2 * HD:]

        @pl.when(z == 0)
        def _():
            left(c, z).wait_recv()
            put(part[c, z].astype(F32) + recv[c, z].astype(F32))

        @pl.when(z == nz - 1)
        def _():
            right(c, z).wait_recv()
            put(part[c, z].astype(F32) + recv[c, z + 1].astype(F32))

        @pl.when(has_low & has_high)
        def _():
            right(c, z).wait_recv()
            left(c, z).wait_recv()
            put(part[c, z].astype(F32) + recv[c, z].astype(F32) + recv[c, z + 1].astype(F32))

    odd = z % 2 == 1
    last = pairs - 1

    def tile(m):
        return jnp.where(odd, m, nb - 1 - m)

    def produce(m):
        to = rows(tile(m) * T, T, T)
        for k in list(range(1, nx)) + [0]:
            there = ((x + k) % nx) * 2
            at = rows((there + 1 - core) * cols, cols, cols)
            send1[k, m] = dot(w[at, :], grad[:, to]).astype(BF16)
            swap(k, m).start()
        for k in list(range(1, nx)) + [0]:
            there = ((x + k) % nx) * 2
            at = rows((there + core) * cols, cols, cols)
            own[k, m] = dot(w[at, :], grad[:, to]).astype(BF16)

    def forward(m):
        for k in range(1, nx):
            swap(k, m).wait_recv()
            recv1[k, m] = (own[k, m].astype(F32) + recv1[k, m].astype(F32)).astype(BF16)
            cross(k, m).start()

    def deliver(m):
        swap(0, m).wait_recv()
        value = own[0, m].astype(F32) + recv1[0, m].astype(F32)
        for k in range(1, nx):
            cross(k, m).wait_recv()
            value = value + recv2[k, m].astype(F32)
        in_held[rows(tile(m) * T, T, T), :] = value.astype(BF16).T

    if pairs > 1:
        plan = [(0, 2), (0, 3), (0, 4), (0, 0), (0, 1), (0, nb - 2), (0, nb - 1), (1, 0), (1, 1)]
        plan = plan + [(0, i) for i in range(5, nb - 2)] + [(1, m) for m in range(2, nb)]
    else:
        plan = [(0, m) for m in range(nb)]

    def after(p, i):
        return plan.index((p, i))

    first_end = after(0, nb - 3) if pairs > 1 else None

    @pl.loop(0, len(plan))
    def _(n):
        p, i = jnp.int32(plan[0][0]), jnp.int32(plan[0][1])
        for k, (pair, at_block) in enumerate(plan[1:], 1):
            p = jnp.where(n == k, pair, p)
            i = jnp.where(n == k, at_block, i)
        i = jnp.where(p == last, tile(i), i)

        for q in range(pairs):
            @pl.when(n == (after(q, 0) if q == last else 3))
            def _():
                halo_arrive(q)

        block(p, i)

        if pairs > 1:
            @pl.when((n == after(0, 1)) & has_low)
            def _():
                rim_out(0, 1, 0)
                rim_down(0).start()

            @pl.when((n == after(0, nb - 1)) & has_high)
            def _():
                rim_out(0, 0, nb + RIM)
                rim_up(0).start()

            @pl.when(n == first_end)
            def _():
                @pl.when(has_low)
                def _():
                    low_in(0)

                @pl.when(has_high)
                def _():
                    high_in(0)

                @pl.loop(0, nb)
                def _(t):
                    finish(0, t)

                weight_grads(0, 0)
                weight_grads(0, 1)

            for m in range(1, nz - 1):
                @pl.when(n == after(1, min(2 * m, nb - 1)))
                def _():
                    hop(0, m)

            for m in range(1, nz - 1):
                @pl.when(n == after(1, min(3 + 2 * m, nb - 1)))
                def _():
                    hop(1, m)

        low_at = jnp.where(odd, after(last, 1), after(last, nb - 1))
        high_at = jnp.where(odd, after(last, nb - 1), after(last, 1))

        @pl.when((n == low_at) & has_low)
        def _():
            rim_out(last, 1, 0)
            rim_down(last).start()

        @pl.when((n == high_at) & has_high)
        def _():
            rim_out(last, 0, nb + RIM)
            rim_up(last).start()

        @pl.when(n == after(last, 2))
        def _():
            @pl.when(odd)
            def _():
                low_in(last)

            @pl.when(jnp.logical_not(odd) & has_high)
            def _():
                high_in(last)

        @pl.when((n >= after(last, 2)) & (n < after(last, 2) + EARLY))
        def _():
            m = n - after(last, 2)

            @pl.when(m > 0)
            def _():
                forward(m - 1)

            finish(last, tile(m))
            produce(m)

    def put_out(p):
        to = slice(p * 6 * HD, (p + 1) * 6 * HD)
        qkv_out[:, to] = sums[to, :].T
        ow_out[:, p * 2 * HD:(p + 1) * 2 * HD] = sums[3 * width + p * 2 * HD:3 * width + (p + 1) * 2 * HD, :].T

    weight_grads(last, 0)

    @pl.loop(EARLY, nb - 2)
    def _(m):
        forward(m - 1)
        finish(last, tile(m))
        produce(m)

    forward(nb - 3)
    if nz > 2:
        hop(2 * last, 1)

    @pl.when(odd & has_high)
    def _():
        high_in(last)

    @pl.when(jnp.logical_not(odd) & has_low)
    def _():
        low_in(last)

    for m in (nb - 2, nb - 1):
        finish(last, tile(m))
    weight_grads(last, 1)
    for m in range(2, nz - 1):
        hop(2 * last, m)
    for m in (nb - 2, nb - 1):
        produce(m)
    for m in (nb - 2, nb - 1):
        forward(m)
    if nz > 2:
        hop(2 * last + 1, 1)
    if pairs > 1:
        land(0, 0)
        land(0, 1)
        put_out(0)
    for m in range(2, nz - 1):
        hop(2 * last + 1, m)
    land(last, 0)

    @pl.loop(0, nb)
    def _(m):
        deliver(m)

    result = pltpu.make_async_copy(in_held, in_out, in_sem)
    result.start()
    land(last, 1)
    put_out(last)
    result.wait()

    @pl.when(has_high)
    def _():
        seg_up().wait_send()
        for p in range(pairs):
            halo_up(kt, 0, p).wait_send()
            halo_up(vt, 1, p).wait_send()
            rim_up(p).wait_send()

    @pl.when(has_low)
    def _():
        seg_down().wait_send()
        for p in range(pairs):
            halo_down(kt, 0, p).wait_send()
            halo_down(vt, 1, p).wait_send()
            rim_down(p).wait_send()

    for c in range(2 * pairs):
        for d in range(nz):
            if d > 0:
                @pl.when(z < d)
                def _():
                    right(c, d).wait_send()
            if d < nz - 1:
                @pl.when(z > d)
                def _():
                    left(c, d).wait_send()
    for k in range(nx):
        for m in range(nb):
            swap(k, m).wait_send()
            if k > 0:
                cross(k, m).wait_send()


def hand_over_kernel(count, *refs):
    sources, targets, held = refs[:count], refs[count:2 * count], refs[2 * count:3 * count]
    sems = refs[3 * count]
    into, out = [], []
    for source, target, hold in zip(sources, targets, held):
        size = source.shape[0] // PIECES
        for n in range(PIECES):
            at = pl.ds(n * size, size)
            into.append(pltpu.make_async_copy(source.at[at], hold.at[at], sems.at[0, len(into)]))
            out.append(pltpu.make_async_copy(hold.at[at], target.at[at], sems.at[1, len(out)]))
    for copy in into:
        copy.start()
    for first, second in zip(into, out):
        first.wait()
        second.start()
    for copy in out:
        copy.wait()


def hand_over(arrays):
    anywhere = pl.BlockSpec(memory_space=pl.ANY)
    return pl.pallas_call(
        functools.partial(hand_over_kernel, len(arrays)),
        in_specs=[anywhere] * len(arrays),
        out_specs=[anywhere] * len(arrays),
        out_shape=[jax.ShapeDtypeStruct(a.shape, a.dtype) for a in arrays],
        scratch_shapes=[pltpu.VMEM(a.shape, a.dtype) for a in arrays]
        + [pltpu.SemaphoreType.DMA((2, len(arrays) * PIECES))],
        compiler_params=pltpu.CompilerParams(vmem_limit_bytes=60 * 1024 * 1024),
    )(*arrays)


def local(activations, out_grad, segment_ids, qkv_weight, out_weight):
    tokens, model = activations.shape
    columns = qkv_weight.shape[1]
    width = columns // 3
    pairs = width // (2 * HD)
    nb = tokens // T
    nt = nb + 2 * RIM
    nz = lax.axis_size("ctx")
    nx = lax.axis_size("head") // 2
    cols = model // (2 * nx)
    share = model // nz
    position = np.arange(nz * tokens, dtype=np.float32)
    exponent = np.arange(HALF, dtype=np.float32) * np.float32(2.0 / HD)
    inverse = np.power(np.float32(10000.0), -exponent).astype(np.float32)
    angles = (inverse[None, :, None] * position.reshape(nz * nb, 1, T)).astype(np.float64)
    cos, sin = jnp.asarray(np.cos(angles), F32), jnp.asarray(np.sin(angles), F32)
    vmem = pl.BlockSpec(memory_space=pltpu.VMEM)
    dma = pltpu.SemaphoreType.DMA
    v = pltpu.VMEM
    out = pl.pallas_call(
        functools.partial(layer_kernel, nx, nz),
        in_specs=[pl.BlockSpec(memory_space=pl.ANY)] * 7,
        out_specs=[pl.BlockSpec(memory_space=pl.ANY), vmem, vmem],
        out_shape=[
            jax.ShapeDtypeStruct((tokens, cols), BF16),
            jax.ShapeDtypeStruct((share, columns), F32),
            jax.ShapeDtypeStruct((share, width), F32),
        ],
        scratch_shapes=[
            v((tokens, cols), BF16), dma(()),
            v((tokens, model), BF16), v((tokens, model), BF16), v((tokens // 128, 128), jnp.int32),
            v((model, columns), BF16), v((model, width), BF16), v((nb, HALF, T), F32), v((nb, HALF, T), F32),
            dma((nb,)), dma((nb,)), dma((5,)),
            v((columns, model), BF16), v((width, model), BF16),
            v((nt, width, T), BF16), v((nt, width, T), BF16),
            v((pairs, nt, T, 2 * HD + 128), BF16), v((pairs, nt, T, 2 * HD), BF16),
            v((nb, width, T), BF16), v((nb, width, T), BF16),
            v((nb, 128, T), BF16), v((tokens // 128, 128), jnp.int32), v((tokens // 128, 128), jnp.int32), v((2, T, T), F32),
            v((2, SPAN, T, T), F32), v((2, SPAN, T, T), BF16), v((2, SPAN, T, T), BF16),
            v((nt, width, T), F32), v((nt, width, T), F32),
            v((columns, tokens), BF16), v((width, tokens), BF16),
            v((pairs, 2, 2, RIM, 2 * HD, T), BF16), v((pairs, 2, 2, RIM, 2 * HD, T), BF16),
            v((2 * pairs, nz, 4 * HD, share), BF16), v((2 * pairs, nz + 1, 4 * HD, share), BF16),
            v((4 * width, share), F32),
            v((nx, nb, cols, T), BF16), v((nx, nb, cols, T), BF16),
            v((nx, nb, cols, T), BF16), v((nx, nb, cols, T), BF16),
            dma((2, 2, pairs)), dma((2, 2, pairs)), dma((2,)), dma((2,)), dma((pairs, 2)), dma((pairs, 2)),
            dma((2 * pairs, nz)), dma((2 * pairs, nz)), dma((2 * pairs, nz)), dma((2 * pairs, nz)),
            dma((nx, nb)), dma((nx, nb)), dma((nx, nb)), dma((nx, nb)),
        ],
        compiler_params=pltpu.CompilerParams(
            collective_id=0, has_side_effects=True, vmem_limit_bytes=60 * 1024 * 1024
        ),
        cost_estimate=pl.CostEstimate(
            flops=12 * tokens * SPAN * T * width + 16 * tokens * model * width,
            bytes_accessed=8 * tokens * model, transcendentals=tokens * SPAN * T * width // HD
        ),
    )(activations, out_grad, segment_ids.reshape(tokens // 128, 128), qkv_weight, out_weight, cos, sin)
    return hand_over(out)


def solution(mesh):
    in_specs = (
        P(("groups", "ctx"), None),
        P(("groups", "ctx"), None),
        P(("groups", "ctx")),
        P(None, "head"),
        P(None, "head"),
    )
    out_specs = (
        P(("groups", "ctx"), "head"),
        P(("groups", "ctx"), "head"),
        P(("groups", "ctx"), "head"),
    )
    return jax.shard_map(local, mesh=mesh, in_specs=in_specs, out_specs=out_specs, check_vma=False)
```

```python
import functools
import itertools

import jax
import jax.numpy as jnp
import numpy as np
from jax import lax
from jax.experimental import pallas as pl
from jax.experimental.pallas import tpu as pltpu
from jax.sharding import PartitionSpec as P

HD = 64
HALF = HD // 2
WIN = 512
T = 256
RIM = WIN // T
SPAN = 2 * RIM + 1
LOW = -1e30
OUTSIDE = 127
PIECES = 2
EARLY = 4
NT = (((1,), (1,)), ((), ()))
F32 = jnp.float32
BF16 = jnp.bfloat16
MESH = pl.DeviceIdType.MESH


def dot(a, b):
    return jnp.dot(a, b, preferred_element_type=F32)


def layer_kernel(nx, nz, acts_in, og_in, seg_in, w_in, ow_in, cos_in, sin_in,
                 in_out, qkv_out, ow_out,
                 in_held, in_sem, acts, og, seg, w, ow, cos_ref, sin_ref, acts_ls, og_ls, load_ls, wt, owt, kt, vt, kx, vx, qt, gt, pen, seg_low, seg_high, tri,
                 s_ref, p_ref, ds_ref, dk, dv, grad, att,
                 rim_send, rim_recv, part, recv, sums, send1, own, recv1, recv2,
                 halo_ss, halo_rs, seg_ss, seg_rs, rim_ss, rim_rs,
                 right_ss, right_rs, left_ss, left_rs, swap_ss, swap_rs, cross_ss, cross_rs):
    tokens, model = acts.shape
    width = ow.shape[1]
    heads = width // HD
    pairs = heads // 2
    nb = tokens // T
    cols = model // (2 * nx)
    share = model // nz
    head = lax.axis_index("head")
    z = lax.axis_index("ctx")
    x, core = head // 2, head % 2
    sibling = x * 2 + (1 - core)
    has_low, has_high = z > 0, z < nz - 1
    above = {"ctx": jnp.minimum(z + 1, nz - 1)}
    below = {"ctx": jnp.maximum(z - 1, 0)}

    def loads():
        here = pl.ds(z * nb, nb)
        pairs_of = ((w_in, w), (ow_in, ow), (cos_in.at[here], cos_ref), (sin_in.at[here], sin_ref), (seg_in, seg))
        return [pltpu.make_async_copy(src, dst, load_ls.at[n]) for n, (src, dst) in enumerate(pairs_of)]

    def load_tile(i):
        at = pl.ds(pl.multiple_of(i * T, T), T)
        return (pltpu.make_async_copy(acts_in.at[at], acts.at[at], acts_ls.at[i]),
                pltpu.make_async_copy(og_in.at[at], og.at[at], og_ls.at[i]))

    def early(j):
        return jnp.where(j < RIM, j, jnp.where(j < 2 * RIM, nb - 2 * RIM + j, j - RIM))

    for copy in loads():
        copy.start()
    for j in range(nb):
        for copy in load_tile(early(j)):
            copy.start()

    barrier = pltpu.get_barrier_semaphore()
    pl.semaphore_signal(barrier, inc=1, device_id={"head": sibling}, device_id_type=MESH)
    for k in range(1, nx):
        peer = ((x + k) % nx) * 2 + core
        pl.semaphore_signal(barrier, inc=1, device_id={"head": peer}, device_id_type=MESH)
    for k in range(1, nz):
        pl.semaphore_signal(barrier, inc=1, device_id={"ctx": (z + k) % nz}, device_id_type=MESH)

    def remote(src, dst, ss, rs, device):
        return pltpu.make_async_remote_copy(src_ref=src, dst_ref=dst, send_sem=ss, recv_sem=rs,
                                            device_id=device, device_id_type=MESH)

    def halo_up(a, n, p):
        at = pl.ds(p * 2 * HD, 2 * HD)
        return remote(a.at[pl.ds(nb, RIM), at], a.at[pl.ds(0, RIM), at], halo_ss.at[0, n, p], halo_rs.at[0, n, p], above)

    def halo_down(a, n, p):
        at = pl.ds(p * 2 * HD, 2 * HD)
        return remote(a.at[pl.ds(RIM, RIM), at], a.at[pl.ds(nb + RIM, RIM), at],
                      halo_ss.at[1, n, p], halo_rs.at[1, n, p], below)

    def seg_up():
        return remote(seg, seg_low, seg_ss.at[0], seg_rs.at[0], above)

    def seg_down():
        return remote(seg, seg_high, seg_ss.at[1], seg_rs.at[1], below)

    def rim_up(p):
        return remote(rim_send.at[p, 0], rim_recv.at[p, 0], rim_ss.at[p, 0], rim_rs.at[p, 0], above)

    def rim_down(p):
        return remote(rim_send.at[p, 1], rim_recv.at[p, 1], rim_ss.at[p, 1], rim_rs.at[p, 1], below)

    def right(c, d):
        return remote(part.at[c, d], recv.at[c, d + 1], right_ss.at[c, d], right_rs.at[c, d], above)

    def left(c, d):
        return remote(part.at[c, d], recv.at[c, d], left_ss.at[c, d], left_rs.at[c, d], below)

    def swap(k, r):
        return remote(send1.at[k, r], recv1.at[k, r], swap_ss.at[k, r], swap_rs.at[k, r], {"head": sibling})

    def cross(k, r):
        return remote(recv1.at[k, r], recv2.at[k, r], cross_ss.at[k, r], cross_rs.at[k, r],
                      {"head": ((x + k) % nx) * 2 + core})

    def rows(start, size, unit):
        return pl.ds(pl.multiple_of(start, unit), size)

    for copy in loads():
        copy.wait()

    @pl.loop(0, model // T)
    def _(c):
        at = rows(c * T, T, T)
        wt[:, at] = w[at, :].T
        owt[:, at] = ow[at, :].T

    lane_doc = lax.broadcasted_iota(jnp.int32, (128, T), 0)

    def doc_row(ids, i):
        return jnp.concatenate([ids[pl.ds(i * (T // 128) + n, 1), :] for n in range(T // 128)], axis=1)

    def token_major(t, row, which):
        one = jnp.where(lane_doc == row, 1.0, 0.0).astype(BF16).T
        for p in which:
            kx[p, t, :, :2 * HD] = kt[t, p * 2 * HD:(p + 1) * 2 * HD, :].T
            kx[p, t, :, 2 * HD:] = one
            vx[p, t] = vt[t, p * 2 * HD:(p + 1) * 2 * HD, :].T

    def project(i):
        at = rows(i * T, T, T)
        projected = lax.dot_general(wt[...], acts[at, :], NT, preferred_element_type=F32).astype(BF16)
        gt[i] = lax.dot_general(owt[...], og[at, :], NT, preferred_element_type=F32).astype(BF16)
        cos, sin = cos_ref[i], sin_ref[i]

        def rope(u):
            u = u.astype(F32)
            low, high = u[:HALF], u[HALF:]
            return jnp.concatenate([low * cos - high * sin, high * cos + low * sin], axis=0).astype(BF16)

        for h in range(heads):
            to = slice(h * HD, (h + 1) * HD)
            base = h * 3 * HD
            qt[i, to, :] = rope(projected[base:base + HD]) * BF16(HD ** -0.5)
            kt[i + RIM, to, :] = rope(projected[base + HD:base + 2 * HD])
            vt[i + RIM, to, :] = projected[base + 2 * HD:base + 3 * HD]
        row = doc_row(seg, i)
        pen[i] = jnp.where(lane_doc == row, 0.0, LOW).astype(BF16)
        token_major(i + RIM, row, range(pairs))

    @pl.loop(0, nb)
    def _(j):
        for copy in load_tile(early(j)):
            copy.wait()
        project(early(j))

        @pl.when(j == 2 * RIM - 1)
        def _():
            pl.semaphore_wait(barrier, nx + nz - 1)

            @pl.when(has_high)
            def _():
                seg_up().start()
                for p in range(pairs):
                    halo_up(kt, 0, p).start()
                    halo_up(vt, 1, p).start()

            @pl.when(has_low)
            def _():
                seg_down().start()
                for p in range(pairs):
                    halo_down(kt, 0, p).start()
                    halo_down(vt, 1, p).start()

    r = lax.broadcasted_iota(jnp.int32, (T, T), 0)
    c = lax.broadcasted_iota(jnp.int32, (T, T), 1)
    tri[0] = jnp.where(r >= c, 0.0, LOW).astype(F32)
    tri[1] = jnp.where(r <= c, 0.0, LOW).astype(F32)

    @pl.loop(0, nb + 2 * RIM)
    def _(t):
        dk[t] = jnp.zeros_like(dk[t])
        dv[t] = jnp.zeros_like(dv[t])

    def fill(a, first):
        a[first:first + RIM] = jnp.zeros((RIM, width, T), BF16)

    @pl.when(z == 0)
    def _():
        fill(kt, 0)
        fill(vt, 0)
        seg_low[...] = jnp.full_like(seg_low, OUTSIDE)

    @pl.when(z == nz - 1)
    def _():
        fill(kt, nb + RIM)
        fill(vt, nb + RIM)
        seg_high[...] = jnp.full_like(seg_high, OUTSIDE)

    def halo_arrive(p):
        @pl.when(has_low)
        def _():
            if p == 0:
                seg_up().wait_recv()
            halo_up(kt, 0, p).wait_recv()
            halo_up(vt, 1, p).wait_recv()

        @pl.when(has_high)
        def _():
            if p == 0:
                seg_down().wait_recv()
            halo_down(kt, 0, p).wait_recv()
            halo_down(vt, 1, p).wait_recv()

        for t in range(RIM):
            token_major(t, doc_row(seg_low, nb - RIM + t), [p])
            token_major(nb + RIM + t, doc_row(seg_high, t), [p])

    zero = jnp.zeros((HD, T), BF16)

    def place(h, block, rest):
        return jnp.concatenate(([block, zero] if h == 0 else [zero, block]) + rest, axis=0)

    def feature(p, h):
        return rows(p * 2 * HD + h * HD, HD, HD)

    def block(p, i):
        top, scale, delta = [None] * 2, [None] * 2, [None] * 2
        ats = [feature(p, h) for h in range(2)]

        def score(h):
            rhs = place(h, qt[i, ats[h], :], [pen[i]])
            high = None
            for t in range(SPAN):
                s = dot(kx[p, i + t], rhs)
                if t == 0:
                    s = s + tri[0]
                if t == SPAN - 1:
                    s = s + tri[1]
                s_ref[h, t] = s
                best = jnp.max(s.reshape(T // 8, 8, T), axis=0)
                high = best if high is None else jnp.maximum(high, best)
                yield
            top[h] = jnp.max(high, axis=0, keepdims=True)

        def soft(h):
            total = jnp.zeros((8, T), F32)
            for t in range(SPAN):
                e = jnp.exp(s_ref[h, t] - top[h])
                total = total + jnp.sum(e.reshape(T // 8, 8, T), axis=0)
                p_ref[h, t] = e.astype(BF16)
                yield
            scale[h] = 1.0 / jnp.sum(total, axis=0, keepdims=True)

        def attend(h):
            out = jnp.zeros((HD, T), F32)
            for t in range(SPAN):
                out = out + dot(vt[i + t, ats[h], :], p_ref[h, t])
                yield
            out = (out * scale[h]).astype(BF16)
            att[ats[h], rows(i * T, T, T)] = out
            delta[h] = jnp.sum(out.astype(F32) * gt[i, ats[h], :].astype(F32), axis=0, keepdims=True)

        def score_grad(h):
            rhs = place(h, gt[i, ats[h], :], [])
            for t in range(SPAN):
                back = dot(vx[p, i + t], rhs)
                ds_ref[h, t] = (p_ref[h, t].astype(F32) * (back - delta[h])).astype(BF16)
                yield

        def query_grad(h):
            out = jnp.zeros((HD, T), F32)
            for t in range(SPAN):
                out = out + dot(kt[i + t, ats[h], :], ds_ref[h, t])
                yield
            out = out * (scale[h] * HD ** -0.5)
            grad[rows((2 * p + h) * 3 * HD, HD, HD), rows(i * T, T, T)] = unrope(out, i)

        def value_grad(h):
            g = (gt[i, ats[h], :].astype(F32) * scale[h]).astype(BF16)
            for t in range(SPAN):
                dv[i + t, ats[h], :] += lax.dot_general(g, p_ref[h, t], NT, preferred_element_type=F32)
                yield

        def key_grad(h):
            q = (qt[i, ats[h], :].astype(F32) * scale[h]).astype(BF16)
            for t in range(SPAN):
                dk[i + t, ats[h], :] += lax.dot_general(q, ds_ref[h, t], NT, preferred_element_type=F32)
                yield

        def run(*stages):
            for _ in itertools.zip_longest(*stages):
                pass

        run(score(0))
        run(score(1))
        run(soft(0))
        run(attend(0))
        run(soft(1), value_grad(0))
        run(attend(1))
        run(score_grad(0), value_grad(1))
        run(score_grad(1))
        run(query_grad(0))
        run(key_grad(0))
        run(query_grad(1))
        run(key_grad(1))

    def unrope(u, i):
        cos, sin = cos_ref[i], sin_ref[i]
        low, high = u[:HALF], u[HALF:]
        return jnp.concatenate([low * cos + high * sin, high * cos - low * sin], axis=0).astype(BF16)

    def rim_out(p, side, first):
        at = rows(p * 2 * HD, 2 * HD, 2 * HD)
        for t in range(RIM):
            rim_send[p, side, 0, t] = dk[first + t, at, :].astype(BF16)
            rim_send[p, side, 1, t] = dv[first + t, at, :].astype(BF16)

    def rim_in(p, side, first):
        at = rows(p * 2 * HD, 2 * HD, 2 * HD)
        for t in range(RIM):
            dk[first + t, at, :] += rim_recv[p, side, 0, t].astype(F32)
            dv[first + t, at, :] += rim_recv[p, side, 1, t].astype(F32)

    def low_in(p):
        rim_up(p).wait_recv()
        rim_in(p, 0, RIM)

    def high_in(p):
        rim_down(p).wait_recv()
        rim_in(p, 1, nb)

    def finish(p, i):
        to = rows(i * T, T, T)
        for h in range(2):
            base = (2 * p + h) * 3 * HD
            grad[rows(base + HD, HD, HD), to] = unrope(dk[i + RIM, feature(p, h), :], i)
            grad[rows(base + 2 * HD, HD, HD), to] = dv[i + RIM, feature(p, h), :].astype(BF16)

    def weight_grads(p, sub):
        c = 2 * p + sub
        order = []
        for n in range(nz):
            order.append(nz - 1 - n // 2 if n % 2 == 0 else n // 2)
        for d in order:
            to = slice(d * share, (d + 1) * share)
            for h in range(2):
                base = (2 * p + h) * 3 * HD
                if sub == 0:
                    part[c, d, h * HD:(h + 1) * HD, :] = dot(grad[rows(base, HD, HD), :], acts[:, to]).astype(BF16)
                else:
                    part[c, d, 2 * h * HD:2 * (h + 1) * HD, :] = dot(
                        grad[rows(base + HD, 2 * HD, HD), :], acts[:, to]).astype(BF16)
            if sub == 0:
                part[c, d, 2 * HD:, :] = dot(att[rows(p * 2 * HD, 2 * HD, 2 * HD), :], og[:, to]).astype(BF16)
            if d > 0:
                @pl.when(z == 0)
                def _():
                    right(c, d).start()
            if d < nz - 1:
                @pl.when(z == nz - 1)
                def _():
                    left(c, d).start()

    def hop(c, n):
        up = z + nz - 1 - n
        down = n - (nz - 1 - z)

        @pl.when(has_low & (up < nz))
        def _():
            right(c, up).wait_recv()
            part[c, up] = (part[c, up].astype(F32) + recv[c, up + 1].astype(F32)).astype(BF16)
            right(c, up).start()

        @pl.when(has_high & (down >= 0))
        def _():
            left(c, down).wait_recv()
            part[c, down] = (part[c, down].astype(F32) + recv[c, down].astype(F32)).astype(BF16)
            left(c, down).start()

    def land(p, sub):
        c = 2 * p + sub

        def put(value):
            for h in range(2):
                base = (2 * p + h) * 3 * HD
                if sub == 0:
                    sums[rows(base, HD, HD), :] = value[h * HD:(h + 1) * HD]
                else:
                    sums[rows(base + HD, 2 * HD, HD), :] = value[2 * h * HD:2 * (h + 1) * HD]
            if sub == 0:
                sums[rows(3 * width + p * 2 * HD, 2 * HD, 2 * HD), :] = value[2 * HD:]

        @pl.when(z == 0)
        def _():
            left(c, z).wait_recv()
            put(part[c, z].astype(F32) + recv[c, z].astype(F32))

        @pl.when(z == nz - 1)
        def _():
            right(c, z).wait_recv()
            put(part[c, z].astype(F32) + recv[c, z + 1].astype(F32))

        @pl.when(has_low & has_high)
        def _():
            right(c, z).wait_recv()
            left(c, z).wait_recv()
            put(part[c, z].astype(F32) + recv[c, z].astype(F32) + recv[c, z + 1].astype(F32))

    odd = z % 2 == 1
    last = pairs - 1

    def tile(m):
        return jnp.where(odd, m, nb - 1 - m)

    def produce(m):
        to = rows(tile(m) * T, T, T)
        for k in list(range(1, nx)) + [0]:
            there = ((x + k) % nx) * 2
            at = rows((there + 1 - core) * cols, cols, cols)
            send1[k, m] = dot(w[at, :], grad[:, to]).astype(BF16)
            swap(k, m).start()
        for k in list(range(1, nx)) + [0]:
            there = ((x + k) % nx) * 2
            at = rows((there + core) * cols, cols, cols)
            own[k, m] = dot(w[at, :], grad[:, to]).astype(BF16)

    def forward(m):
        for k in range(1, nx):
            swap(k, m).wait_recv()
            recv1[k, m] = (own[k, m].astype(F32) + recv1[k, m].astype(F32)).astype(BF16)
            cross(k, m).start()

    def deliver(m):
        swap(0, m).wait_recv()
        value = own[0, m].astype(F32) + recv1[0, m].astype(F32)
        for k in range(1, nx):
            cross(k, m).wait_recv()
            value = value + recv2[k, m].astype(F32)
        in_held[rows(tile(m) * T, T, T), :] = value.astype(BF16).T

    if pairs > 1:
        plan = [(0, 2), (0, 3), (0, 4), (0, 0), (0, 1), (0, nb - 2), (0, nb - 1), (1, 0), (1, 1)]
        plan = plan + [(0, i) for i in range(5, nb - 2)] + [(1, m) for m in range(2, nb)]
    else:
        plan = [(0, m) for m in range(nb)]

    def after(p, i):
        return plan.index((p, i))

    first_end = after(0, nb - 3) if pairs > 1 else None

    @pl.loop(0, len(plan))
    def _(n):
        p, i = jnp.int32(plan[0][0]), jnp.int32(plan[0][1])
        for k, (pair, at_block) in enumerate(plan[1:], 1):
            p = jnp.where(n == k, pair, p)
            i = jnp.where(n == k, at_block, i)
        i = jnp.where(p == last, tile(i), i)

        for q in range(pairs):
            @pl.when(n == (after(q, 0) if q == last else 3))
            def _():
                halo_arrive(q)

        block(p, i)

        if pairs > 1:
            @pl.when((n == after(0, 1)) & has_low)
            def _():
                rim_out(0, 1, 0)
                rim_down(0).start()

            @pl.when((n == after(0, nb - 1)) & has_high)
            def _():
                rim_out(0, 0, nb + RIM)
                rim_up(0).start()

            @pl.when(n == first_end)
            def _():
                @pl.when(has_low)
                def _():
                    low_in(0)

                @pl.when(has_high)
                def _():
                    high_in(0)

                @pl.loop(0, nb)
                def _(t):
                    finish(0, t)

                weight_grads(0, 0)
                weight_grads(0, 1)

            for m in range(1, nz - 1):
                @pl.when(n == after(1, min(2 * m, nb - 1)))
                def _():
                    hop(0, m)

            for m in range(1, nz - 1):
                @pl.when(n == after(1, min(3 + 2 * m, nb - 1)))
                def _():
                    hop(1, m)

        low_at = jnp.where(odd, after(last, 1), after(last, nb - 1))
        high_at = jnp.where(odd, after(last, nb - 1), after(last, 1))

        @pl.when((n == low_at) & has_low)
        def _():
            rim_out(last, 1, 0)
            rim_down(last).start()

        @pl.when((n == high_at) & has_high)
        def _():
            rim_out(last, 0, nb + RIM)
            rim_up(last).start()

        @pl.when(n == after(last, 2))
        def _():
            @pl.when(odd)
            def _():
                low_in(last)

            @pl.when(jnp.logical_not(odd) & has_high)
            def _():
                high_in(last)

        @pl.when((n >= after(last, 2)) & (n < after(last, 2) + EARLY))
        def _():
            m = n - after(last, 2)

            @pl.when(m > 0)
            def _():
                forward(m - 1)

            finish(last, tile(m))
            produce(m)

    def put_out(p):
        to = slice(p * 6 * HD, (p + 1) * 6 * HD)
        qkv_out[:, to] = sums[to, :].T
        ow_out[:, p * 2 * HD:(p + 1) * 2 * HD] = sums[3 * width + p * 2 * HD:3 * width + (p + 1) * 2 * HD, :].T

    weight_grads(last, 0)

    @pl.loop(EARLY, nb - 2)
    def _(m):
        forward(m - 1)
        finish(last, tile(m))
        produce(m)

    forward(nb - 3)
    if nz > 2:
        hop(2 * last, 1)

    @pl.when(odd & has_high)
    def _():
        high_in(last)

    @pl.when(jnp.logical_not(odd) & has_low)
    def _():
        low_in(last)

    for m in (nb - 2, nb - 1):
        finish(last, tile(m))
    weight_grads(last, 1)
    for m in range(2, nz - 1):
        hop(2 * last, m)
    for m in (nb - 2, nb - 1):
        produce(m)
    for m in (nb - 2, nb - 1):
        forward(m)
    if nz > 2:
        hop(2 * last + 1, 1)
    if pairs > 1:
        land(0, 0)
        land(0, 1)
        put_out(0)
    for m in range(2, nz - 1):
        hop(2 * last + 1, m)
    land(last, 0)

    @pl.loop(0, nb)
    def _(m):
        deliver(m)

    result = pltpu.make_async_copy(in_held, in_out, in_sem)
    result.start()
    land(last, 1)
    put_out(last)
    result.wait()

    @pl.when(has_high)
    def _():
        seg_up().wait_send()
        for p in range(pairs):
            halo_up(kt, 0, p).wait_send()
            halo_up(vt, 1, p).wait_send()
            rim_up(p).wait_send()

    @pl.when(has_low)
    def _():
        seg_down().wait_send()
        for p in range(pairs):
            halo_down(kt, 0, p).wait_send()
            halo_down(vt, 1, p).wait_send()
            rim_down(p).wait_send()

    for c in range(2 * pairs):
        for d in range(nz):
            if d > 0:
                @pl.when(z < d)
                def _():
                    right(c, d).wait_send()
            if d < nz - 1:
                @pl.when(z > d)
                def _():
                    left(c, d).wait_send()
    for k in range(nx):
        for m in range(nb):
            swap(k, m).wait_send()
            if k > 0:
                cross(k, m).wait_send()


def hand_over_kernel(count, *refs):
    sources, targets, held = refs[:count], refs[count:2 * count], refs[2 * count:3 * count]
    sems = refs[3 * count]
    into, out = [], []
    for source, target, hold in zip(sources, targets, held):
        size = source.shape[0] // PIECES
        for n in range(PIECES):
            at = pl.ds(n * size, size)
            into.append(pltpu.make_async_copy(source.at[at], hold.at[at], sems.at[0, len(into)]))
            out.append(pltpu.make_async_copy(hold.at[at], target.at[at], sems.at[1, len(out)]))
    for copy in into:
        copy.start()
    for first, second in zip(into, out):
        first.wait()
        second.start()
    for copy in out:
        copy.wait()


def hand_over(arrays):
    anywhere = pl.BlockSpec(memory_space=pl.ANY)
    return pl.pallas_call(
        functools.partial(hand_over_kernel, len(arrays)),
        in_specs=[anywhere] * len(arrays),
        out_specs=[anywhere] * len(arrays),
        out_shape=[jax.ShapeDtypeStruct(a.shape, a.dtype) for a in arrays],
        scratch_shapes=[pltpu.VMEM(a.shape, a.dtype) for a in arrays]
        + [pltpu.SemaphoreType.DMA((2, len(arrays) * PIECES))],
        compiler_params=pltpu.CompilerParams(vmem_limit_bytes=60 * 1024 * 1024),
    )(*arrays)


def local(activations, out_grad, segment_ids, qkv_weight, out_weight):
    tokens, model = activations.shape
    columns = qkv_weight.shape[1]
    width = columns // 3
    pairs = width // (2 * HD)
    nb = tokens // T
    nt = nb + 2 * RIM
    nz = lax.axis_size("ctx")
    nx = lax.axis_size("head") // 2
    cols = model // (2 * nx)
    share = model // nz
    position = np.arange(nz * tokens, dtype=np.float32)
    exponent = np.arange(HALF, dtype=np.float32) * np.float32(2.0 / HD)
    inverse = np.power(np.float32(10000.0), -exponent).astype(np.float32)
    angles = (inverse[None, :, None] * position.reshape(nz * nb, 1, T)).astype(np.float64)
    cos, sin = jnp.asarray(np.cos(angles), F32), jnp.asarray(np.sin(angles), F32)
    vmem = pl.BlockSpec(memory_space=pltpu.VMEM)
    dma = pltpu.SemaphoreType.DMA
    v = pltpu.VMEM
    out = pl.pallas_call(
        functools.partial(layer_kernel, nx, nz),
        in_specs=[pl.BlockSpec(memory_space=pl.ANY)] * 7,
        out_specs=[pl.BlockSpec(memory_space=pl.ANY), vmem, vmem],
        out_shape=[
            jax.ShapeDtypeStruct((tokens, cols), BF16),
            jax.ShapeDtypeStruct((share, columns), F32),
            jax.ShapeDtypeStruct((share, width), F32),
        ],
        scratch_shapes=[
            v((tokens, cols), BF16), dma(()),
            v((tokens, model), BF16), v((tokens, model), BF16), v((tokens // 128, 128), jnp.int32),
            v((model, columns), BF16), v((model, width), BF16), v((nb, HALF, T), F32), v((nb, HALF, T), F32),
            dma((nb,)), dma((nb,)), dma((5,)),
            v((columns, model), BF16), v((width, model), BF16),
            v((nt, width, T), BF16), v((nt, width, T), BF16),
            v((pairs, nt, T, 2 * HD + 128), BF16), v((pairs, nt, T, 2 * HD), BF16),
            v((nb, width, T), BF16), v((nb, width, T), BF16),
            v((nb, 128, T), BF16), v((tokens // 128, 128), jnp.int32), v((tokens // 128, 128), jnp.int32), v((2, T, T), F32),
            v((2, SPAN, T, T), F32), v((2, SPAN, T, T), BF16), v((2, SPAN, T, T), BF16),
            v((nt, width, T), F32), v((nt, width, T), F32),
            v((columns, tokens), BF16), v((width, tokens), BF16),
            v((pairs, 2, 2, RIM, 2 * HD, T), BF16), v((pairs, 2, 2, RIM, 2 * HD, T), BF16),
            v((2 * pairs, nz, 4 * HD, share), BF16), v((2 * pairs, nz + 1, 4 * HD, share), BF16),
            v((4 * width, share), F32),
            v((nx, nb, cols, T), BF16), v((nx, nb, cols, T), BF16),
            v((nx, nb, cols, T), BF16), v((nx, nb, cols, T), BF16),
            dma((2, 2, pairs)), dma((2, 2, pairs)), dma((2,)), dma((2,)), dma((pairs, 2)), dma((pairs, 2)),
            dma((2 * pairs, nz)), dma((2 * pairs, nz)), dma((2 * pairs, nz)), dma((2 * pairs, nz)),
            dma((nx, nb)), dma((nx, nb)), dma((nx, nb)), dma((nx, nb)),
        ],
        compiler_params=pltpu.CompilerParams(
            collective_id=0, has_side_effects=True, vmem_limit_bytes=60 * 1024 * 1024
        ),
        cost_estimate=pl.CostEstimate(
            flops=12 * tokens * SPAN * T * width + 16 * tokens * model * width,
            bytes_accessed=8 * tokens * model, transcendentals=tokens * SPAN * T * width // HD
        ),
    )(activations, out_grad, segment_ids.reshape(tokens // 128, 128), qkv_weight, out_weight, cos, sin)
    return hand_over(out)


def solution(mesh):
    in_specs = (
        P(("groups", "ctx"), None),
        P(("groups", "ctx"), None),
        P(("groups", "ctx")),
        P(None, "head"),
        P(None, "head"),
    )
    out_specs = (
        P(("groups", "ctx"), "head"),
        P(("groups", "ctx"), "head"),
        P(("groups", "ctx"), "head"),
    )
    return jax.shard_map(local, mesh=mesh, in_specs=in_specs, out_specs=out_specs, check_vma=False)
```
